32 devices in a mesh: dp: 8 (over y, x, core), tensor: 4 (over z).
Axes of the slice: x: 2, y: 2, z: 4, core: 2. Of those that a mesh axis runs over, the one named last changes fastest.
Arguments:
- tokens_in: bfloat16 [8192, 768], P('dp'), may hold values from -6 to 6
- w_qkv: bfloat16 [3, 768, 768], P(None, None, 'tensor'), may hold values from -0.21875 to 0.21875
- b_qv: bfloat16 [2, 768], P(None, 'tensor'), may hold values from -3 to 3
- w_out: bfloat16 [768, 768], P('tensor'), may hold values from -1.75 to 1.75
- b_out: bfloat16 [768], replicated, may hold values from -3 to 3
- gain_one: float32 [768], replicated, may hold values from 0.25 to 1.75
- shift_one: float32 [768], replicated, may hold values from -3 to 3
- w_up: bfloat16 [768, 3072], P(None, 'tensor'), may hold values from -0.21875 to 0.21875
- b_up: bfloat16 [3072], P('tensor'), may hold values from -3 to 3
- w_down: bfloat16 [3072, 768], P('tensor'), may hold values from -0.15625 to 0.15625
- b_down: bfloat16 [768], replicated, may hold values from -3 to 3
- gain_two: float32 [768], replicated, may hold values from 0.25 to 1.75
- shift_two: float32 [768], replicated, may hold values from -3 to 3
- bucket_len: int32 [8], P('dp'), may hold values from 64 to 1024, as said below
- key_mask: int32 [8192], P('dp'), may hold values from 0 to 1, as said below
- block_perm: int32 [12, 2], P('tensor'), may hold values from 0 to 1, each once within a row
- grad_output: bfloat16 [8192, 768], P('dp'), may hold values from -6 to 6
Outputs:
- layer_out: float32 [8192, 768], P(('dp', 'tensor'))
- grad_tokens: float32 [8192, 768], P(('dp', 'tensor'))
- grad_w_qkv: float32 [3, 768, 768], P(None, 'dp', 'tensor')
- grad_b_qv: float32 [2, 768], P(None, 'tensor')
- grad_w_out: float32 [768, 768], P('tensor', 'dp')
- grad_b_out: float32 [768], replicated
- grad_gain_one: float32 [768], replicated
- grad_shift_one: float32 [768], replicated
- grad_w_up: float32 [768, 3072], P('dp', 'tensor')
- grad_b_up: float32 [3072], P('tensor')
- grad_w_down: float32 [3072, 768], P('tensor', 'dp')
- grad_b_down: float32 [768], replicated
- grad_gain_two: float32 [768], replicated
- grad_shift_two: float32 [768], replicated
The draws below stay inside these ranges and needn't reach their ends.
Inputs may be any that keep to these rules, and one draw needn't show every extreme that they name: `bucket_len`: a power of two times 64 that divides 1024; the 1024 rows of an index of dp are 1024 / bucket_len padded sequences of bucket_len rows each, in order. `key_mask`: in each padded sequence the first L rows are 1 and the rest 0, where L is more than three quarters of that index's bucket_len.
All inputs are finite; a program needn't handle non-finite values.
Results may differ from the reference program's by a relative error of at most 0.013.
The reference program's roundings to bfloat16 on the way count: a program that leaves them out, or rounds other values in their place, can miss the bound.
Values sent between devices are 32-bit elements; how exact they have to be, the bound alone decides.
No kernel may reach another device: no remote copies, remote signals or barrier semaphores. Data moves between devices by JAX's collectives and lax.ppermute only.
A program may use at most 128 MiB of HBM per device.

```python
import jax
import jax.numpy as jnp
from jax import lax

D = 768
HEADS = 12
HDIM = 64
FF = 3072
TOK_DEV = 1024
MAXLEN = 1024
TOKENS = 8192


def bucket_levels(key):
    devices = TOKENS // TOK_DEV
    levels = (MAXLEN // 64).bit_length()
    first_draw = jax.random.randint(jax.random.fold_in(key, 11), (devices,), 0, levels)
    second_draw = jax.random.randint(jax.random.fold_in(key, 12), (devices,), 0, levels)
    chosen = jnp.minimum(first_draw, second_draw).astype(jnp.int32)
    positions = jnp.arange(devices, dtype=jnp.int32)
    chosen = jnp.where(positions == 0, levels - 1, jnp.where(positions == 1, 0, chosen)).astype(jnp.int32)
    return jnp.left_shift(jnp.full((devices,), 64, jnp.int32), chosen)


def draw_bucket_len(key, part):
    return bucket_levels(key)


def draw_key_mask(key, part):
    devices = TOKENS // TOK_DEV
    lengths = bucket_levels(key)
    slots = TOK_DEV // 64
    raw_bits = jax.random.randint(jax.random.fold_in(key, 13), (devices, slots), 0, 1 << 30)
    cut_rows = raw_bits % jnp.maximum(lengths // 4, 1)[:, None]
    row_index = jnp.arange(TOK_DEV, dtype=jnp.int32)
    member = row_index[None, :] // lengths[:, None]
    offset = row_index[None, :] % lengths[:, None]
    row_cut = jnp.take_along_axis(cut_rows, member, axis=1)
    return (offset < lengths[:, None] - row_cut).astype(jnp.int32).reshape(TOKENS)


def spiked(values, stream_key, source, target, blocks, factor):
    def block_of(axis_at):
        return (jnp.arange(values.shape[axis_at]) // (values.shape[axis_at] // blocks)).reshape((-1,) + (1,) * (values.ndim - 1 - axis_at))

    first = jax.random.permutation(stream_key, blocks)[block_of(target)]
    far = (block_of(target) + blocks // 2) % blocks
    return jnp.where((block_of(source) == first) | (block_of(source) == far), factor * values, values)


def shard_levels(key, shape, split, smallest, high):
    gain, own = 1.0, jax.random.fold_in(key, 6)
    for dim, blocks in split:
        heights = jnp.exp(jax.random.uniform(jax.random.fold_in(own, dim), (blocks,), jnp.float32, smallest / len(split), high / len(split)))
        gain = gain * jnp.repeat(heights, shape[dim] // blocks).reshape([-1 if axis == dim else 1 for axis in range(len(shape))])
    return gain


def centred(key, dims, spread, reach, pieces=(), kind=jnp.bfloat16):
    array = spread * jax.random.normal(key, dims, jnp.float32)
    if pieces:
        array = array * shard_levels(key, dims, pieces, -0.22, 0.18)
    return jnp.clip(array, -reach, reach).astype(kind)


def noise_with(stream_key, dims, scale, reach, pieces, heavy, held_as=jnp.bfloat16):
    entries = scale * jax.random.normal(stream_key, dims, jnp.float32)
    if pieces:
        entries = entries * shard_levels(stream_key, dims, pieces, -0.22, 0.18)
    return jnp.clip(spiked(entries, jax.random.fold_in(stream_key, 3), *heavy), -reach, reach).astype(held_as)


def setup_inputs(seed: int = 0) -> dict:
    seeds = jax.random.split(jax.random.key(seed), 18)
    return {
        "tokens_in": centred(seeds[0], (TOKENS, D), 1.0, 6.0, ((0, 8),)),
        "w_qkv": centred(seeds[1], (3, D, D), D ** -0.5, 0.21875, ((2, 4),)),
        "b_qv": centred(seeds[2], (2, D), 0.5, 3.0, ((1, 4),)),
        "w_out": centred(seeds[3], (D, D), (D // 64) ** -0.5, 1.75, ((0, 4),)),
        "b_out": centred(seeds[4], (D,), 0.5, 3.0),
        "gain_one": jnp.clip(1.0 + 0.15 * jax.random.normal(seeds[5], (D,), jnp.float32), 0.25, 1.75),
        "shift_one": centred(seeds[6], (D,), 0.5, 3.0, (), jnp.float32),
        "w_up": centred(seeds[7], (D, FF), D ** -0.5, 0.21875, ((1, 4),)),
        "b_up": centred(seeds[8], (FF,), 0.5, 3.0, ((0, 4),)),
        "w_down": centred(seeds[9], (FF, D), (FF // 2) ** -0.5, 0.15625, ((0, 4),)),
        "b_down": centred(seeds[10], (D,), 0.5, 3.0),
        "gain_two": jnp.clip(1.0 + 0.15 * jax.random.normal(seeds[11], (D,), jnp.float32), 0.25, 1.75),
        "shift_two": centred(seeds[12], (D,), 0.5, 3.0, (), jnp.float32),
        "bucket_len": draw_bucket_len(jax.random.fold_in(seeds[17], 71), 0),
        "key_mask": draw_key_mask(jax.random.fold_in(seeds[17], 71), 0),
        "block_perm": jax.vmap(lambda own: jax.random.permutation(own, 2))(jax.random.split(seeds[15], HEADS)).reshape((HEADS, 2)).astype(jnp.int32),
        "grad_output": noise_with(seeds[16], (TOKENS, D), 1.0, 6.0, ((0, 8),), (0, 1, 8, 2.0)),
    }


@jax.custom_vjp
def low(v):
    return lax.optimization_barrier(v.astype(jnp.bfloat16)).astype(jnp.float32)

@jax.custom_vjp
def low_back(v):
    return v

def low_keep(v):
    return (low(v), None)

def low_pass(kept, grad):
    return (grad,)

def back_keep(v):
    return (v, None)

def back_low(kept, grad):
    return (low(grad),)
low.defvjp(low_keep, low_pass)
low_back.defvjp(back_keep, back_low)
NEG_FILL = -1e+30
LN_EPS = 1e-06
HIGH = lax.Precision.HIGHEST

def normalize(row_values, gain_vec, shift_vec):
    center = row_values - lax.optimization_barrier(jnp.mean(row_values, axis=-1, keepdims=True))
    inverse = lax.rsqrt(lax.optimization_barrier(jnp.mean(center * center, axis=-1, keepdims=True)) + LN_EPS)
    return center * inverse * gain_vec + shift_vec

def block_pattern(bucket, block_order):
    positions = jnp.arange(MAXLEN, dtype=jnp.int32)
    member = positions // bucket
    half_index = (positions % bucket * 2 >= bucket).astype(jnp.int32)
    target = jnp.where(half_index[None, :] == 0, block_order[:, 0:1], block_order[:, 1:2])
    same_seq = member[:, None] == member[None, :]
    return same_seq[None, :, :] & (half_index[None, None, :] == target[:, :, None])

def attend_window(queries, key_rows, values, live_keys, bucket, block_order):
    pattern = block_pattern(bucket, block_order) & (live_keys[None, None, :] == 1)
    raw_scores = jnp.einsum('qhd,khd->hqk', queries, key_rows, precision=HIGH)
    scores = jnp.where(pattern, low_back(raw_scores * HDIM ** (-0.5)), NEG_FILL)
    prob_rows = jnp.exp(scores - jax.nn.logsumexp(scores, axis=-1, keepdims=True))
    return jnp.einsum('hqk,khd->qhd', low(prob_rows), values, precision=HIGH)

def layer(tokens_f, w_qkv, b_qv, w_out, b_out, gain_one, shift_one, w_up, b_up, w_down, b_down, gain_two, shift_two, bucket_len, key_mask, block_perm):
    projected = jnp.einsum('td,cde->cte', tokens_f, w_qkv, precision=HIGH)
    bias_rows = jnp.stack([b_qv[0], jnp.zeros_like(b_qv[0]), b_qv[1]])
    qkv_all = low(low_back(projected + bias_rows[:, None, :]))
    windows = TOKENS // MAXLEN
    per_dev = TOK_DEV // MAXLEN
    split_heads = qkv_all.reshape(3, windows, MAXLEN, HEADS, HDIM)
    buckets = jnp.repeat(bucket_len, per_dev)
    live_rows = key_mask.reshape(windows, MAXLEN)

    def window_step(window_items):
        return attend_window(window_items[0], window_items[1], window_items[2], window_items[3], window_items[4], block_perm)
    mixed = lax.map(jax.checkpoint(window_step), (split_heads[0], split_heads[1], split_heads[2], live_rows, buckets))
    attended = low(low_back(mixed.reshape(TOKENS, D)))
    attn_branch = low_back(jnp.dot(attended, w_out, precision=HIGH))
    s_one = tokens_f + attn_branch + b_out
    h_one = normalize(s_one, gain_one, shift_one)
    up_proj = low_back(jnp.dot(low(h_one), w_up, precision=HIGH) + b_up)
    activated = low(jax.nn.gelu(up_proj, approximate=False))
    ffn_branch = low_back(jnp.dot(activated, w_down, precision=HIGH))
    s_two = h_one + ffn_branch + b_down
    return normalize(s_two, gain_two, shift_two)

def reference(tokens_in, w_qkv, b_qv, w_out, b_out, gain_one, shift_one, w_up, b_up, w_down, b_down, gain_two, shift_two, bucket_len, key_mask, block_perm, grad_output):

    def forward(tokens_f, wqkv_f, bqv_f, wout_f, bout_f, gone_f, sone_f, wup_f, bup_f, wdown_f, bdown_f, gtwo_f, stwo_f):
        return layer(tokens_f, wqkv_f, bqv_f, wout_f, bout_f, gone_f, sone_f, wup_f, bup_f, wdown_f, bdown_f, gtwo_f, stwo_f, bucket_len, key_mask, block_perm)
    layer_out, pull_back = jax.vjp(forward, tokens_in.astype(jnp.float32), w_qkv.astype(jnp.float32), b_qv.astype(jnp.float32), w_out.astype(jnp.float32), b_out.astype(jnp.float32), gain_one.astype(jnp.float32), shift_one.astype(jnp.float32), w_up.astype(jnp.float32), b_up.astype(jnp.float32), w_down.astype(jnp.float32), b_down.astype(jnp.float32), gain_two.astype(jnp.float32), shift_two.astype(jnp.float32))
    grads = pull_back(grad_output.astype(jnp.float32))
    return (layer_out, grads[0], grads[1], grads[2], grads[3], grads[4], grads[5], grads[6], grads[7], grads[8], grads[9], grads[10], grads[11], grads[12])
```

```python
import functools
import jax, jax.numpy as jnp
from jax import lax
from jax.experimental import pallas as pl
from jax.experimental.pallas import tpu as pltpu
F32=jnp.float32; BF=jnp.bfloat16
NT=(((1,),(1,)),((),())); NN=(((1,),(0,)),((),())); TN=(((0,),(0,)),((),()))
def dg(a,b,dn): return lax.dot_general(a,b,dn,preferred_element_type=F32)
NEG=-1e30

def fwd_kernel(nh, own, *refs):
    if own:
        perm, buck, tok, wlow, bias, qc, kc, acc, qkv, att = refs
        acc_in = None
    else:
        perm, buck, tok, wa, wb, bias, qc, kc, acc_in, acc, qkv, wlow, att = refs
        for b in range(4*nh):
            for half,ref in ((0,wa),(1,wb)):
                lo=jnp.concatenate([ref[j,b] for j in range(4)],axis=0).astype(BF)
                wlow[pl.ds(b*64+half*32,32),:]=lo
    hw=64*nh
    x=tok[...]
    for c in range(3):
        y=dg(x,wlow[pl.ds(c*hw,hw),:],NT)
        if c!=1: y=y+bias[c//2:c//2+1,:]
        qkv[:,c*hw:(c+1)*hw]=y.astype(BF)
    full=buck[0]==1024
    for h in range(nh):
        s_flag=perm[h,0]
        for i in range(2):
            j=jnp.where(full,perm[h,i],i)
            q=qkv[i*512:(i+1)*512,h*64:(h+1)*64]*jnp.asarray(0.125,BF)
            kj=qkv[pl.ds(pl.multiple_of(j*512,512),512),hw+h*64:hw+(h+1)*64]
            vj=qkv[pl.ds(pl.multiple_of(j*512,512),512),2*hw+h*64:2*hw+(h+1)*64]
            s=dg(q,kj,NT)
            ok=(qc[i*512:(i+1)*512,:]^s_flag)==kc[j]
            s=jnp.where(ok,s,NEG)
            m=jnp.max(s,axis=1,keepdims=True)
            p=jnp.exp(s-m)
            l=jnp.sum(p,axis=1,keepdims=True)
            p=(p*(1.0/l)).astype(BF)
            o=dg(p,vj,NN)
            att[i*512:(i+1)*512,h*64:(h+1)*64]=o.astype(BF)
    y=dg(att[...],wlow[pl.ds(3*hw,hw),:],NN)
    acc[...]=y if own else acc_in[...]+y

def attn_fwd(nh,own,perm,buck,tok,ws,bias,qc,kc,acc_in=None,vmem=40):
    T,D=tok.shape; hw=64*nh
    V=pl.BlockSpec(memory_space=pltpu.VMEM); S=pl.BlockSpec(memory_space=pltpu.SMEM)
    ins=[perm,buck,tok,*ws,bias,qc,kc]+([] if own else [acc_in])
    out=[jax.ShapeDtypeStruct((T,D),F32),jax.ShapeDtypeStruct((T,3*hw),BF)]
    if not own: out.append(jax.ShapeDtypeStruct((4*hw,D),BF))
    scratch=[]
    if own: out.append(jax.ShapeDtypeStruct((T,hw),BF))
    else: scratch.append(pltpu.VMEM((T,hw),BF))
    return pcall(functools.partial(fwd_kernel,nh,own),"attn_fwd",out,ins,[S,S]+[V]*(len(ins)-2),scratch=scratch,
        alias=None if own else {len(ins)-1:0},vmem=vmem,flops=2*T*D*hw*4+nh*2*512*512*256)

ERFC_P=0.3
ERFC=(0.16919777,0.17054635,0.14956615,0.21002719,-0.08287393,0.53022837,-0.49656831,0.47774502,-0.1278686)
def phi_pair(v):
    e=jnp.exp(v*v*-0.5)
    t=1.0/(1.0+jnp.abs(v)*(ERFC_P*0.7071067811865476))
    a=jnp.full_like(t,ERFC[-1])
    for k in ERFC[-2::-1]: a=a*t+k
    tail=0.5*(a*t*e)
    return jnp.where(v>=0,1.0-tail,tail), e*0.3989422804014327

def pcall(fn,name,out,ins,specs,scratch=(),alias=None,vmem=40,flops=0,grid=None,outspecs=None,nbytes=16<<20):
    V=pl.BlockSpec(memory_space=pltpu.VMEM)
    return pl.pallas_call(fn,out_shape=tuple(out),in_specs=specs,out_specs=tuple(outspecs) if outspecs else (V,)*len(out),
        input_output_aliases=alias or {},scratch_shapes=list(scratch),
        cost_estimate=pl.CostEstimate(flops=int(flops),bytes_accessed=nbytes,transcendentals=0),
        compiler_params=pltpu.CompilerParams(vmem_limit_bytes=vmem<<20),name=name)(*ins)

def ffn_fwd_kernel(own,first,*refs):
    refs=list(refs)
    h=refs.pop(0)
    if own: wu,wd=refs.pop(0),refs.pop(0)
    else: wa,wb=refs.pop(0),refs.pop(0)
    b=refs.pop(0)
    acc_in=None if first else refs.pop(0)
    acc,gp,act_out=refs[0],refs[1],refs[2]
    if not own:
        wu,wd=refs[2],refs[3]
        act_out=None
        for half,ref in ((0,wa),(1,wb)):
            for j in range(4):
                o=(half*4+j)*96
                wu[o:o+96,:]=ref[j,0:96,:].astype(BF)
                wd[o:o+96,:]=ref[j,96:192,:].astype(BF)
    n=256
    for r in range(h.shape[0]//n):
        rows=slice(r*n,(r+1)*n)
        up=dg(h[rows,:],wu[...],NT)+b[...]
        P,d=phi_pair(up)
        gp[rows,:]=P+up*d
        a=(up*P).astype(BF)
        if own: act_out[rows,:]=a
        y=dg(a,wd[...],NN)
        acc[rows,:]=y if first else acc_in[rows,:]+y

def ffn_fwd(own,h,ws,b,acc_in=None,vmem=40):
    T,D=h.shape; H=b.shape[1]
    V=pl.BlockSpec(memory_space=pltpu.VMEM)
    first=acc_in is None
    ins=[h,*ws,b]+([] if first else [acc_in])
    out=[jax.ShapeDtypeStruct((T,D),F32),jax.ShapeDtypeStruct((T,H),F32)]
    if own: out.append(jax.ShapeDtypeStruct((T,H),BF))
    else: out+=[jax.ShapeDtypeStruct((H,D),BF)]*2
    return pcall(functools.partial(ffn_fwd_kernel,own,first),"ffn_fwd",out,ins,[V]*len(ins),alias=None if first else {len(ins)-1:0},vmem=vmem,flops=4*T*D*H)

def ffn_bwd_kernel(own,first,*refs):
    refs=list(refs)
    g,wu,wd,gp=refs[:4]; refs=refs[4:]
    acc_in=None if first else refs.pop(0)
    acc=refs[0]
    n=256
    bs=None
    for r in range(g.shape[0]//n):
        rows=slice(r*n,(r+1)*n)
        da=dg(g[rows,:],wd[...],NT)
        du=(da*gp[rows,:]).astype(BF)
        if own:
            refs[1][rows,:]=du
            s=jnp.sum(du.astype(F32),axis=0,keepdims=True)
            bs=s if bs is None else bs+s
        y=dg(du,wu[...],NN)
        acc[rows,:]=y if first else acc_in[rows,:]+y
    if own: refs[2][...]=bs

def ffn_bwd(own,g,wu,wd,gp,acc_in=None,vmem=40):
    T,D=g.shape; H=gp.shape[1]
    V=pl.BlockSpec(memory_space=pltpu.VMEM)
    first=acc_in is None
    ins=[g,wu,wd,gp]+([] if first else [acc_in])
    out=[jax.ShapeDtypeStruct((T,D),F32)]
    if own: out+=[jax.ShapeDtypeStruct((T,H),BF),jax.ShapeDtypeStruct((1,H),F32)]
    return pcall(functools.partial(ffn_bwd_kernel,own,first),"ffn_bwd",out,ins,[V]*len(ins),alias=None if first else {len(ins)-1:0},vmem=vmem,flops=4*T*D*H)

def bwd_kernel(nh,own,*refs):
    perm,buck,meta,g,wlow,qkv,qcr,kcc,*outs=refs
    hw=64*nh
    T=g.shape[0]
    datt=outs[-1]
    datt[...]=dg(g[...],wlow[pl.ds(3*hw,hw),:],NT).astype(BF)
    full=buck[0]==1024
    dst=outs[0] if own else outs[1]
    for h in range(nh):
        s_flag=perm[h,0]
        for i in range(2):
            j=jnp.where(full,perm[h,i],i)
            rj=pl.ds(pl.multiple_of(j*512,512),512)
            q=qkv[i*512:(i+1)*512,h*64:(h+1)*64]*jnp.asarray(0.125,BF)
            kj=qkv[rj,hw+h*64:hw+(h+1)*64]
            vj=qkv[rj,2*hw+h*64:2*hw+(h+1)*64]
            do=datt[i*512:(i+1)*512,h*64:(h+1)*64]
            s=dg(kj,q,NT)
            s=jnp.where((qcr[i]^s_flag)==kcc[rj,:],s,NEG)
            m=jnp.max(s,axis=0,keepdims=True)
            p=jnp.exp(s-m)
            l=jnp.sum(p,axis=0,keepdims=True)
            p=p*(1.0/l)
            dp=dg(vj,do,NT)
            delta=jnp.sum(p*dp,axis=0,keepdims=True)
            ds=(p*(dp-delta)).astype(BF)
            dst[rj,2*hw+h*64:2*hw+(h+1)*64]=dg(p.astype(BF),do,NN).astype(BF)
            dst[rj,hw+h*64:hw+(h+1)*64]=dg(ds,q,NN).astype(BF)
            dst[i*512:(i+1)*512,h*64:(h+1)*64]=(dg(ds,kj,TN)*0.125).astype(BF)
    R=outs[1].shape[0] if own else outs[0].shape[0]
    rows=pl.ds(pl.multiple_of(meta[0]*R,R),R)
    y=dg(dst[rows,:],wlow[0:3*hw,:],NN)
    if own:
        outs[1][...]=y
        cs=jnp.sum(dst[...].astype(F32),axis=0,keepdims=True)
        outs[2][...]=cs
    else:
        outs[0][...]=y

def attn_bwd(nh,own,perm,buck,meta,g,wlow,qkv,qcr,kcc,R,vmem=40):
    T,D=g.shape; hw=64*nh
    V=pl.BlockSpec(memory_space=pltpu.VMEM); S=pl.BlockSpec(memory_space=pltpu.SMEM)
    if own: out=[jax.ShapeDtypeStruct((T,3*hw),BF),jax.ShapeDtypeStruct((R,D),F32),jax.ShapeDtypeStruct((1,3*hw),F32)]; scratch=[pltpu.VMEM((T,hw),BF)]
    else: out=[jax.ShapeDtypeStruct((R,D),F32)]; scratch=[pltpu.VMEM((T,3*hw),BF),pltpu.VMEM((T,hw),BF)]
    return pcall(functools.partial(bwd_kernel,nh,own),"attn_bwd",out,[perm,buck,meta,g,wlow,qkv,qcr,kcc],[S,S,S]+[V]*5,scratch=scratch,vmem=vmem,flops=2*T*D*hw*4+nh*2*512*512*640)


from jax.sharding import PartitionSpec as P

MAXLEN = 1024
LN_EPS = 1e-06
AXES = ("dp", "tensor")


def normalize(row_values, gain_vec, shift_vec):
    center = row_values - jnp.mean(row_values, axis=-1, keepdims=True)
    inverse = lax.rsqrt(jnp.mean(center * center, axis=-1, keepdims=True) + LN_EPS)
    scaled = center * inverse
    return (scaled * gain_vec + shift_vec, scaled, inverse)


def norm_back(grad_rows, gain_vec, scaled, inverse):
    weighted = grad_rows * gain_vec
    inner_sum = jnp.mean(weighted, axis=-1, keepdims=True)
    along_sum = jnp.mean(weighted * scaled, axis=-1, keepdims=True)
    return inverse * (weighted - inner_sum - scaled * along_sum)


def body(n_dp, n_tp, tokens_in, w_qkv, b_qv, w_out, b_out, gain_one, shift_one, w_up, b_up,
         w_down, b_down, gain_two, shift_two, bucket_len, key_mask, block_perm, grad_output):
    T, D = tokens_in.shape
    nh = block_perm.shape[0]
    hw = w_qkv.shape[2]
    H = w_up.shape[1]
    R = T // n_tp
    d = lax.axis_index("dp")
    t = lax.axis_index("tensor")
    core, bx, by = d & 1, (d >> 1) & 1, (d >> 2) & 1
    J = bx + 2 * by + 4 * core

    def bit(b):
        return [(i * n_tp + k, (i ^ b) * n_tp + k) for i in range(n_dp) for k in range(n_tp)]

    CORE, X, Y = bit(1), bit(2), bit(4)
    RING = [(i * n_tp + k, i * n_tp + (k + 1) % n_tp) for i in range(n_dp) for k in range(n_tp)]

    def pp(v, perm):
        return lax.ppermute(v, AXES, perm)

    def spread(cur):
        half = cur.shape[0] // 2
        rx = pp(cur, X)
        ry = pp(cur, Y)
        r1 = pp(rx[:half], Y)
        r2 = pp(ry[half:], X)
        mine = jnp.stack([cur, rx, ry, jnp.concatenate([r1, r2])])
        return mine, pp(mine, CORE)

    a_own = jnp.concatenate([jnp.swapaxes(w_qkv, 1, 2).reshape(3 * hw, D), w_out])
    u_own = w_up.T
    a_piece = lax.dynamic_index_in_dim(a_own.reshape(4 * nh, 8, 8, D), J, 1, False).astype(F32)
    up_piece = lax.dynamic_index_in_dim(u_own.reshape(8, H // 8, D), J, 0, False)
    dn_piece = lax.dynamic_index_in_dim(w_down.reshape(8, H // 8, D), J, 0, False)
    f_piece = jnp.concatenate([up_piece, dn_piece]).astype(F32)
    small = jnp.concatenate([b_qv.astype(F32).reshape(-1), b_up.astype(F32), block_perm.astype(F32).reshape(-1)])
    pad = -small.shape[0] % 1024
    small = jnp.pad(small, (0, pad)).reshape(-1, 128)

    def relative(v):
        lead, n = v.shape[:-2], v.shape[-1]
        v = v.reshape(lead + (2, 2, 2, n))
        at = len(lead)
        for axis, on in ((at, core), (at + 1, by), (at + 2, bx)):
            v = jnp.where(on == 1, jnp.flip(v, axis), v)
        return v.reshape(lead + (8, n))

    a_parts, f_parts, biases, perms, up_biases = [], [], [], [], []
    cur = small
    for k in range(1, n_tp):
        cur = pp(cur, RING)
        flat = cur.reshape(-1)
        biases.append(relative(flat[: 2 * hw].reshape(2 * nh, 8, 8)).reshape(2, hw))
        up_biases.append(relative(flat[2 * hw : 2 * hw + H].reshape(8, H // 8)).reshape(1, H))
        perms.append(flat[2 * hw + H : 2 * hw + H + 2 * nh].astype(jnp.int32).reshape(nh, 2))
    cur = a_piece
    for k in range(1, n_tp):
        cur = pp(cur, RING)
        a_parts.append(spread(cur))
    cur = f_piece
    for k in range(1, n_tp):
        cur = pp(cur, RING)
        f_parts.append(spread(cur))

    bucket = bucket_len[0]
    pos = jnp.arange(T, dtype=jnp.int32)
    code = pos // bucket * 2 + (pos % bucket * 2 >= bucket).astype(jnp.int32)
    kcode = jnp.where(key_mask == 1, code, -1)
    q_col, q_row = code[:, None], code.reshape(2, 1, T // 2)
    k_col, k_row = kcode[:, None], kcode.reshape(2, 1, T // 2)

    acc, qkv0, attended = attn_fwd(nh, True, block_perm, bucket_len, tokens_in, (a_own,), b_qv.astype(F32), q_col, k_row)
    qkvs, a_low = [qkv0], [a_own]
    for k in range(n_tp - 1):
        acc, qkv_k, low_k = attn_fwd(nh, False, perms[k], bucket_len, tokens_in, a_parts[k], biases[k], q_col, k_row, acc)
        qkvs.append(qkv_k)
        a_low.append(low_k)
    s_one = tokens_in.astype(F32) + acc + b_out.astype(F32)
    h_one, scaled_one, inverse_one = normalize(s_one, gain_one, shift_one)
    h_low = h_one.astype(BF)
    acc, gp0, act_low = ffn_fwd(True, h_low, (u_own, w_down), b_up.astype(F32)[None])
    gps, f_low = [gp0], [(u_own, w_down)]
    for k in range(n_tp - 1):
        acc, gp_k, wu_k, wd_k = ffn_fwd(False, h_low, f_parts[k], up_biases[k], acc)
        gps.append(gp_k)
        f_low.append((wu_k, wd_k))
    s_two = h_one + acc + b_down.astype(F32)
    y_full, scaled_two, inverse_two = normalize(s_two, gain_two, shift_two)

    def mine(v):
        return lax.dynamic_slice_in_dim(v, t * R, R, 0)

    layer_out = mine(y_full)
    grad_y = grad_output.astype(F32)
    gy_own = mine(grad_y)
    grad_two = norm_back(grad_y, gain_two, scaled_two, inverse_two)
    two_low = grad_two.astype(BF)
    vec_two = [jnp.sum(mine(grad_two), 0), jnp.sum(gy_own * mine(scaled_two), 0), jnp.sum(gy_own, 0)]
    acc, up_low, grad_b_up = ffn_bwd(True, two_low, *f_low[0], gps[0])
    down_local = dg(two_low, act_low, TN)
    up_local = dg(h_low, up_low, TN)
    for k in range(1, n_tp):
        (acc,) = ffn_bwd(False, two_low, *f_low[k], gps[k], acc)
    grad_h = grad_two + acc
    grad_one = norm_back(grad_h, gain_one, scaled_one, inverse_one)
    one_low = grad_one.astype(BF)
    gh_own = mine(grad_h)
    grad_one_own = mine(grad_one)
    vec_one = [jnp.sum(grad_one_own, 0), jnp.sum(gh_own * mine(scaled_one), 0), jnp.sum(gh_own, 0)]
    out_local = dg(one_low, attended, TN)
    meta = t[None].astype(jnp.int32)
    all_perms = [block_perm] + perms
    g_low, total, cols = attn_bwd(nh, True, block_perm, bucket_len, meta, one_low, a_low[0], qkvs[0], q_row, k_col, R)
    qkv_local = dg(tokens_in, g_low, TN)
    grad_tokens = grad_one_own + total
    for k in range(1, n_tp):
        (part,) = attn_bwd(nh, False, all_perms[k], bucket_len, meta, one_low, a_low[k], qkvs[k], q_row, k_col, R)
        grad_tokens = grad_tokens + part

    tens = [[(i * n_tp + k, i * n_tp + (k ^ b)) for i in range(n_dp) for k in range(n_tp)] for b in (1, 2)]

    def sum_dp(v):
        if n_dp != 8:
            return lax.psum(v, "dp")
        for perm in (CORE, X, Y):
            v = v + pp(v, perm)
        return v

    def sum_tp(v):
        if n_tp != 4:
            return lax.psum(v, "tensor")
        for perm in tens:
            v = v + pp(v, perm)
        return v

    def scatter(g):
        if n_dp != 8:
            return lax.psum_scatter(g, "dp", scatter_dimension=0, tiled=True)
        n = g.shape[0] // 8
        h = n // 2
        g = g.reshape(4, 2, n, g.shape[1])
        keep = lax.dynamic_index_in_dim(g, core, 1, False)
        give = lax.dynamic_index_in_dim(g, 1 - core, 1, False)
        p = keep + pp(give, CORE)
        own = bx + 2 * by

        def block(r):
            return lax.dynamic_index_in_dim(p, own ^ r, 0, False)

        o_b, x_b, y_b, d_b = block(0), block(1), block(2), block(3)
        got_x = pp(jnp.concatenate([d_b[:h], x_b[:h]]), X)
        got_y = pp(jnp.concatenate([d_b[h:], y_b[h:]]), Y)
        x2 = pp(x_b[h:] + got_y[:h], X)
        y2 = pp(y_b[:h] + got_x[:h], Y)
        return jnp.concatenate([o_b[:h] + got_x[h:] + y2, o_b[h:] + got_y[h:] + x2])

    vec = jnp.stack(vec_one + vec_two + [jnp.pad(grad_b_up[0], (0, D - H)) if H < D else grad_b_up[0]])
    vec = sum_dp(vec)
    g_b_up = vec[6]
    vec = sum_tp(vec[:6])
    own_down = scatter(down_local).T
    own_up = scatter(up_local)
    own_out = scatter(out_local).T
    own_qkv = jnp.swapaxes(scatter(qkv_local).reshape(-1, 3, hw), 0, 1)
    bqv = sum_dp(cols).reshape(3, hw)
    grad_b_qv = jnp.stack([bqv[0], bqv[2]])
    return (layer_out, grad_tokens, own_qkv, grad_b_qv, own_out, vec[0], vec[1], vec[2], own_up,
            g_b_up, own_down, vec[3], vec[4], vec[5])


def solution(mesh):
    n_dp, n_tp = mesh.shape["dp"], mesh.shape["tensor"]
    in_specs = (
        P("dp", None), P(None, None, "tensor"), P(None, "tensor"), P("tensor", None), P(), P(), P(),
        P(None, "tensor"), P("tensor"), P("tensor", None), P(), P(), P(), P("dp"), P("dp"),
        P("tensor", None), P("dp", None),
    )
    out_specs = (
        P(("dp", "tensor"), None), P(("dp", "tensor"), None), P(None, "dp", "tensor"), P(None, "tensor"),
        P("tensor", "dp"), P(), P(), P(), P("dp", "tensor"), P("tensor"), P("tensor", "dp"), P(), P(), P(),
    )
    return jax.shard_map(functools.partial(body, n_dp, n_tp), mesh=mesh, in_specs=in_specs, out_specs=out_specs, check_vma=False)
```

```python
import functools
import jax
import jax.numpy as jnp
from jax import lax
from jax.experimental import pallas as pl
from jax.experimental.pallas import tpu as pltpu
from jax.sharding import PartitionSpec as P

F32 = jnp.float32
BF = jnp.bfloat16
NT = (((1,), (1,)), ((), ()))
NN = (((1,), (0,)), ((), ()))
TN = (((0,), (0,)), ((), ()))
NEG = -1e30
LN_EPS = 1e-06
AXES = ("dp", "tensor")
VM = pl.BlockSpec(memory_space=pltpu.VMEM)
SM = pl.BlockSpec(memory_space=pltpu.SMEM)
ANY = pl.BlockSpec(memory_space=pl.ANY)


def dg(a, b, dn):
    return lax.dot_general(a, b, dn, preferred_element_type=F32)


def sds(shape, dtype):
    return jax.ShapeDtypeStruct(shape, dtype)


def pcall(fn, name, out, smem, ins, scratch=(), alias=None, vmem=40, us=8, after=()):
    n, k = len(smem) + len(ins), len(after)

    def run(*refs):
        fn(*refs[:n], *refs[n + k:])

    return pl.pallas_call(
        run, out_shape=tuple(out), in_specs=[SM] * len(smem) + [VM] * len(ins) + [ANY] * k,
        out_specs=(VM,) * len(out),
        input_output_aliases={len(smem) + i: o for i, o in (alias or {}).items()}, scratch_shapes=list(scratch),
        cost_estimate=pl.CostEstimate(flops=int(us * 8e8), bytes_accessed=int(us * 2e6), transcendentals=0),
        compiler_params=pltpu.CompilerParams(vmem_limit_bytes=vmem << 20), name=name)(*smem, *ins, *after)


def prep_a_kernel(J, perm, w, wo, b_qv, b_up, a):
    hw = w.shape[2]
    for c in range(3):
        v = w[c].astype(F32)
        for g in range(4):
            a[c * 24:(c + 1) * 24, g * hw:(g + 1) * hw] = v[g * 24:(g + 1) * 24, :]
    a[72:96, :] = wo[...].astype(F32)
    b = b_qv[...].astype(F32)
    a[96:97, 0:hw] = b[0:1]
    a[96:97, hw:2 * hw] = b[1:2]
    a[96:97, 2 * hw:] = jnp.zeros((1, a.shape[1] - 2 * hw), F32)
    a[97:98, :] = b_up[...].astype(F32)
    bits = perm[0, 0]
    for h in range(1, perm.shape[0]):
        bits = bits + (perm[h, 0] << h)
    a[98:104, :] = jnp.full((6, a.shape[1]), bits.astype(F32))


def prep_a(J, perm, w_qkv, w_out, b_qv, b_up):
    D, hw = w_qkv.shape[1:]
    nh = perm.shape[0]
    return pl.pallas_call(
        prep_a_kernel, out_shape=sds((104, D), F32),
        grid_spec=pltpu.PrefetchScalarGridSpec(
            num_scalar_prefetch=2, grid=(1,),
            in_specs=[pl.BlockSpec((3, D // 8, hw), lambda i, J, p: (0, J[0], 0)),
                      pl.BlockSpec((hw // 8, D), lambda i, J, p: (J[0], 0)),
                      pl.BlockSpec((2, hw), lambda i, J, p: (0, 0)),
                      pl.BlockSpec((1, D), lambda i, J, p: (0, 0))],
            out_specs=pl.BlockSpec((104, D), lambda i, J, p: (0, 0))),
        cost_estimate=pl.CostEstimate(flops=int(1e9), bytes_accessed=1 << 20, transcendentals=0),
        compiler_params=pltpu.CompilerParams(vmem_limit_bytes=16 << 20), name="prep_a")(J, perm, w_qkv, w_out, b_qv, b_up)


def prep_f_kernel(J, wu, wd, after, f):
    f[0:96, :] = wu[...].astype(F32)
    f[96:192, :] = wd[...].astype(F32)


def prep_f(J, w_up, w_down, after):
    D, H = w_up.shape
    return pl.pallas_call(
        prep_f_kernel, out_shape=sds((192, D), F32),
        grid_spec=pltpu.PrefetchScalarGridSpec(
            num_scalar_prefetch=1, grid=(1,),
            in_specs=[pl.BlockSpec((D // 8, H), lambda i, J: (J[0], 0)),
                      pl.BlockSpec((H // 8, D), lambda i, J: (J[0], 0)), ANY],
            out_specs=pl.BlockSpec((192, D), lambda i, J: (0, 0))),
        cost_estimate=pl.CostEstimate(flops=int(1e9), bytes_accessed=1 << 20, transcendentals=0),
        compiler_params=pltpu.CompilerParams(vmem_limit_bytes=16 << 20), name="prep_f")(J, w_up, w_down, after)


def cat_kernel(a, b, c, d, o):
    o[0], o[1], o[2], o[3] = a[...], b[...], c[...], d[...]


def cat(parts, after=()):
    return pcall(cat_kernel, "cat", [sds((4,) + parts[0].shape, F32)], (), parts, vmem=16, us=1, after=after)[0]


def attend_fwd(nh, full, first, qc, kc, qkv, att):
    hw = 64 * nh
    for h in range(nh):
        flag = first(h)
        for i in range(2):
            j = jnp.where(full, flag if i == 0 else 1 - flag, i)
            rj = pl.ds(pl.multiple_of(j * 512, 512), 512)
            q = qkv[i * 512:(i + 1) * 512, h * 64:(h + 1) * 64] * jnp.asarray(0.125, BF)
            s = dg(q, qkv[rj, hw + h * 64:hw + (h + 1) * 64], NT)
            s = jnp.where((qc[i * 512:(i + 1) * 512, :] ^ flag) == kc[j], s, NEG)
            p = jnp.exp(s - jnp.max(s, axis=1, keepdims=True))
            p = (p * (1.0 / jnp.sum(p, axis=1, keepdims=True))).astype(BF)
            att[i * 512:(i + 1) * 512, h * 64:(h + 1) * 64] = dg(p, qkv[rj, 2 * hw + h * 64:2 * hw + (h + 1) * 64], NN).astype(BF)


def project(x, w3, bq, bv, qkv, hw):
    qkv[:, 0:hw] = (dg(x[...], w3[0], NN) + bq).astype(BF)
    qkv[:, hw:2 * hw] = dg(x[...], w3[1], NN).astype(BF)
    qkv[:, 2 * hw:3 * hw] = (dg(x[...], w3[2], NN) + bv).astype(BF)


def attn_own_kernel(nh, perm, buck, tok, w3, wo, b_qv, qc, kc, acc, qkv, att):
    hw = 64 * nh
    b = b_qv[...].astype(F32)
    project(tok, w3, b[0:1], b[1:2], qkv, hw)
    attend_fwd(nh, buck[0] == 1024, lambda h: perm[h, 0], qc, kc, qkv, att)
    acc[...] = dg(att[...], wo[...], NN)


def piece_bits(c0):
    return jnp.max(c0[98:99, 0:128]).astype(jnp.int32)


def attn_other_kernel(nh, J, buck, tok, c0, c1, c2, c3, o, qc, kc, acc_in, acc, qkv, w3, wo, att, w32, wo32):
    hw = 64 * nh
    D = tok.shape[1]
    for r in range(8):
        piece = (c0, c1, c2, c3)[r] if r < 4 else o.at[r - 4]
        at = J[0] ^ r
        for c in range(3):
            v = piece[c * 24:(c + 1) * 24, :]
            for g in range(4):
                w32[pl.ds(pl.multiple_of(c * D + at * 96 + g * 24, 8), 24), :] = v[:, g * hw:(g + 1) * hw]
        wo32[pl.ds(pl.multiple_of(at * 24, 8), 24), :] = piece[72:96, :]
    for c in range(3):
        w3[c] = w32[c * D:(c + 1) * D, :].astype(BF)
    wo[...] = wo32[...].astype(BF)
    project(tok, w3, c0[96:97, 0:hw], c0[96:97, hw:2 * hw], qkv, hw)
    bits = piece_bits(c0)
    attend_fwd(nh, buck[0] == 1024, lambda h: (bits >> h) & 1, qc, kc, qkv, att)
    acc[...] = acc_in[...] + dg(att[...], wo[...], NN)


def attn_own(nh, perm, buck, tok, w3, wo, b_qv, qc, kc):
    T, D = tok.shape
    hw = 64 * nh
    return pcall(functools.partial(attn_own_kernel, nh), "attn_own",
                 [sds((T, D), F32), sds((T, 3 * hw), BF), sds((T, hw), BF)], [perm, buck], [tok, w3, wo, b_qv, qc, kc])


def attn_other(nh, J, buck, tok, pieces, qc, kc, acc, after=()):
    T, D = tok.shape
    hw = 64 * nh
    return pcall(functools.partial(attn_other_kernel, nh), "attn_other",
                 [sds((T, D), F32), sds((T, 3 * hw), BF), sds((3, D, hw), BF), sds((hw, D), BF)],
                 [J, buck], [tok, *pieces, qc, kc, acc],
                 scratch=[pltpu.VMEM((T, hw), BF), pltpu.VMEM((3 * D, hw), F32), pltpu.VMEM((hw, D), F32)],
                 alias={8: 0}, after=after)


def attn_bwd_kernel(nh, own, *refs):
    if own:
        t, perm, buck, g, w3, wo, qkv, qcr, kcc, dst, acc, cols, datt = refs
    else:
        t, buck, g, w3, wo, qkv, qcr, kcc, c0, acc_in, acc, dst, datt = refs
        bits = piece_bits(c0)
    hw = 64 * nh
    datt[...] = dg(g[...], wo[...], NT).astype(BF)
    full = buck[0] == 1024
    for h in range(nh):
        flag = perm[h, 0] if own else (bits >> h) & 1
        for i in range(2):
            j = jnp.where(full, flag if i == 0 else 1 - flag, i)
            rj = pl.ds(pl.multiple_of(j * 512, 512), 512)
            q = qkv[i * 512:(i + 1) * 512, h * 64:(h + 1) * 64] * jnp.asarray(0.125, BF)
            kj = qkv[rj, hw + h * 64:hw + (h + 1) * 64]
            vj = qkv[rj, 2 * hw + h * 64:2 * hw + (h + 1) * 64]
            do = datt[i * 512:(i + 1) * 512, h * 64:(h + 1) * 64]
            s = dg(kj, q, NT)
            s = jnp.where((qcr[i] ^ flag) == kcc[rj, :], s, NEG)
            p = jnp.exp(s - jnp.max(s, axis=0, keepdims=True))
            p = p * (1.0 / jnp.sum(p, axis=0, keepdims=True))
            dp = dg(vj, do, NT)
            ds = (p * (dp - jnp.sum(p * dp, axis=0, keepdims=True))).astype(BF)
            dst[rj, 2 * hw + h * 64:2 * hw + (h + 1) * 64] = dg(p.astype(BF), do, NN).astype(BF)
            dst[rj, hw + h * 64:hw + (h + 1) * 64] = dg(ds, q, NN).astype(BF)
            dst[i * 512:(i + 1) * 512, h * 64:(h + 1) * 64] = (dg(ds, kj, TN) * 0.125).astype(BF)
    R = acc.shape[0]
    rows = pl.ds(pl.multiple_of(t[0] * R, R), R)
    y = dg(dst[rows, 0:hw], w3[0], NT) + dg(dst[rows, hw:2 * hw], w3[1], NT) + dg(dst[rows, 2 * hw:3 * hw], w3[2], NT)
    if own:
        acc[...] = y
        cols[...] = jnp.sum(dst[...].astype(F32), axis=0, keepdims=True)
    else:
        acc[...] = acc_in[...] + y


def attn_bwd_own(nh, t, perm, buck, g, w3, wo, qkv, qcr, kcc, R, after=()):
    T, D = g.shape
    hw = 64 * nh
    return pcall(functools.partial(attn_bwd_kernel, nh, True), "attn_bwd_own",
                 [sds((T, 3 * hw), BF), sds((R, D), F32), sds((1, 3 * hw), F32)], [t, perm, buck],
                 [g, w3, wo, qkv, qcr, kcc], scratch=[pltpu.VMEM((T, hw), BF)], after=after)


def attn_bwd_other(nh, t, buck, g, w3, wo, qkv, qcr, kcc, c0, acc, after=()):
    T, D = g.shape
    hw = 64 * nh
    return pcall(functools.partial(attn_bwd_kernel, nh, False), "attn_bwd_other", [sds(acc.shape, F32)], [t, buck],
                 [g, w3, wo, qkv, qcr, kcc, c0, acc],
                 scratch=[pltpu.VMEM((T, 3 * hw), BF), pltpu.VMEM((T, hw), BF)], alias={7: 0}, after=after)[0]


ERFC_P = 0.3
ERFC = (0.16919777, 0.17054635, 0.14956615, 0.21002719, -0.08287393, 0.53022837, -0.49656831, 0.47774502, -0.1278686)


def phi_pair(v):
    e = jnp.exp(v * v * -0.5)
    t = 1.0 / (1.0 + jnp.abs(v) * (ERFC_P * 0.7071067811865476))
    a = jnp.full_like(t, ERFC[-1])
    for k in ERFC[-2::-1]:
        a = a * t + k
    tail = 0.5 * (a * t * e)
    return jnp.where(v >= 0, 1.0 - tail, tail), e * 0.3989422804014327


def ffn_rows(h, wu, wd, b, acc_in, acc, gp, act):
    n = 256
    for r in range(h.shape[0] // n):
        rows = slice(r * n, (r + 1) * n)
        up = dg(h[rows, :], wu[...], NN) + b
        big, density = phi_pair(up)
        gp[rows, :] = big + up * density
        a = (up * big).astype(BF)
        if act is not None:
            act[rows, :] = a
        y = dg(a, wd[...], NN)
        acc[rows, :] = y if acc_in is None else acc_in[rows, :] + y


def ffn_own_kernel(h, wu, wd, b, acc, gp, act):
    ffn_rows(h, wu, wd, b[...].astype(F32), None, acc, gp, act)


def ffn_other_kernel(J, h, a0, c0, c1, c2, c3, o, acc_in, acc, gp, wu, wd):
    for r in range(8):
        piece = (c0, c1, c2, c3)[r] if r < 4 else o.at[r - 4]
        rows = pl.ds(pl.multiple_of((J[0] ^ r) * 96, 32), 96)
        wu[rows, :] = piece[0:96, :].astype(BF)
        wd[rows, :] = piece[96:192, :].astype(BF)
    ffn_rows(h, wu, wd, a0[97:98, :], acc_in, acc, gp, None)


def ffn_own(h, wu, wd, b, after=()):
    T, D = h.shape
    H = wu.shape[1]
    return pcall(ffn_own_kernel, "ffn_own", [sds((T, D), F32), sds((T, H), F32), sds((T, H), BF)], (), [h, wu, wd, b], after=after)


def ffn_other(J, h, a0, pieces, acc, after=()):
    T, D = h.shape
    H = 768
    return pcall(ffn_other_kernel, "ffn_other", [sds((T, D), F32), sds((T, H), F32), sds((D, H), BF), sds((H, D), BF)],
                 [J], [h, a0, *pieces, acc], alias={7: 0}, after=after)


def ffn_bwd_kernel(own, *refs):
    if own:
        g, wu, wd, gp, acc, up_low, bsum = refs
    else:
        g, wu, wd, gp, acc_in, acc = refs
    n = 256
    bs = None
    for r in range(g.shape[0] // n):
        rows = slice(r * n, (r + 1) * n)
        du = (dg(g[rows, :], wd[...], NT) * gp[rows, :]).astype(BF)
        if own:
            up_low[rows, :] = du
            s = jnp.sum(du.astype(F32), axis=0, keepdims=True)
            bs = s if bs is None else bs + s
        y = dg(du, wu[...], NT)
        acc[rows, :] = y if own else acc_in[rows, :] + y
    if own:
        bsum[...] = bs


def ffn_bwd(own, g, wu, wd, gp, acc=None, after=()):
    T, D = g.shape
    H = gp.shape[1]
    out = [sds((T, D), F32)]
    if own:
        out += [sds((T, H), BF), sds((1, H), F32)]
    return pcall(functools.partial(ffn_bwd_kernel, own), "ffn_bwd", out, (), [g, wu, wd, gp] + ([] if own else [acc]),
                 alias=None if own else {4: 0}, us=4, after=after)


def norm(s):
    center = s - jnp.mean(s, axis=-1, keepdims=True)
    inverse = lax.rsqrt(jnp.mean(center * center, axis=-1, keepdims=True) + LN_EPS)
    return center * inverse, inverse


def norm_back(w, scaled, inverse):
    return inverse * (w - jnp.mean(w, axis=-1, keepdims=True) - scaled * jnp.mean(w * scaled, axis=-1, keepdims=True))


def ln1_kernel(tok, acc, b_out, gain, shift, h_low, scaled, inverse):
    n = 128
    for r in range(tok.shape[0] // n):
        rows = slice(r * n, (r + 1) * n)
        x, inv = norm(tok[rows, :].astype(F32) + acc[rows, :] + b_out[...].astype(F32))
        scaled[rows, :] = x
        inverse[rows, :] = inv
        h_low[rows, :] = (x * gain[...] + shift[...]).astype(BF)


def ln2_kernel(t, scaled, gain1, shift1, acc, b_down, gain2, shift2, gy, out, two, two_low, vec):
    R = out.shape[0]

    def rows_of(rows):
        s = scaled[rows, :] * gain1[...] + shift1[...] + acc[rows, :] + b_down[...].astype(F32)
        x, inv = norm(s)
        g = gy[rows, :].astype(F32)
        return x, g, norm_back(g * gain2[...], x, inv)

    n = 128
    for r in range(gy.shape[0] // n):
        rows = slice(r * n, (r + 1) * n)
        _, _, d = rows_of(rows)
        two[rows, :] = d
        two_low[rows, :] = d.astype(BF)
    tot = [jnp.zeros((1, gy.shape[1]), F32)] * 3
    for r in range(R // n):
        rows = pl.ds(pl.multiple_of(t[0] * R + r * n, n), n)
        x, g, d = rows_of(rows)
        out[r * n:(r + 1) * n, :] = x * gain2[...] + shift2[...]
        for i, v in enumerate((d, g * x, g)):
            tot[i] = tot[i] + jnp.sum(v, axis=0, keepdims=True)
    for i in range(3):
        vec[i:i + 1, :] = tot[i]


def ln1_back_kernel(t, two, acc, scaled, inverse, gain1, vec2, bup, one_low, one_own, vec):
    R = one_own.shape[0]
    n = 128

    def rows_of(rows):
        e = two[rows, :] + acc[rows, :]
        return e, norm_back(e * gain1[...], scaled[rows, :], inverse[rows, :])

    for r in range(two.shape[0] // n):
        rows = slice(r * n, (r + 1) * n)
        one_low[rows, :] = rows_of(rows)[1].astype(BF)
    tot = [jnp.zeros((1, two.shape[1]), F32)] * 3
    for r in range(R // n):
        rows = pl.ds(pl.multiple_of(t[0] * R + r * n, n), n)
        e, d = rows_of(rows)
        one_own[r * n:(r + 1) * n, :] = d
        for i, v in enumerate((d, e * scaled[rows, :], e)):
            tot[i] = tot[i] + jnp.sum(v, axis=0, keepdims=True)
    for i in range(3):
        vec[i:i + 1, :] = tot[i]
    vec[3:6, :] = vec2[0:3, :]
    vec[6:7, :] = bup[...]
    vec[7:8, :] = jnp.zeros_like(bup)


def split_blocks(place, full, keep, give):
    n = full.shape[0] // 8
    for q in range(4):
        for mine, ref in ((0, keep), (1, give)):
            b = ((place[1] ^ q) * 2 + (place[0] ^ mine)) * n
            ref[q * n:(q + 1) * n, :] = full[pl.ds(pl.multiple_of(b, 32), n), :]


def grads_ffn_kernel(place, two_low, act, h_low, up_low, keep, give, full):
    H = act.shape[1]
    full[:, 0:H] = dg(two_low[...], act[...], TN)
    full[:, H:] = dg(h_low[...], up_low[...], TN)
    split_blocks(place, full, keep, give)


def grads_attn_kernel(place, tok, dst, one_low, att, cols, vec, keep, give, full):
    W = dst.shape[1]
    full[:, 0:W] = dg(tok[...], dst[...], TN)
    full[:, W:] = dg(one_low[...], att[...], TN)
    n = full.shape[0] // 2
    split_blocks(place, full, keep, give)
    give[n:n + 8, :] = vec[...]
    give[n + 7:n + 8, 0:W // 3] = cols[:, 0:W // 3]
    give[n + 7:n + 8, W // 3:2 * W // 3] = cols[:, 2 * W // 3:]
    keep[n:n + 8, :] = give[n:n + 8, :]


def stage1_kernel(n, extra, keep, got, sx, sy, rest):
    h = n // 2

    def s(a, b):
        return keep[a:b, :] + got[a:b, :]

    sx[0:h, :] = s(3 * n, 3 * n + h)
    sx[h:n, :] = s(n, n + h)
    sy[0:h, :] = s(3 * n + h, 4 * n)
    sy[h:n, :] = s(2 * n + h, 3 * n)
    rest[0:h, :] = s(n + h, 2 * n)
    rest[h:n, :] = s(2 * n, 2 * n + h)
    rest[n:2 * n, :] = s(0, n)
    if extra:
        v = s(4 * n, 4 * n + 8)
        sx[n:n + 8, :] = v
        rest[2 * n:2 * n + 8, :] = v


def stage2_kernel(n, extra, rest, gx, gy, sx, sy, own):
    h = n // 2
    sx[0:h, :] = rest[0:h, :] + gy[0:h, :]
    sy[0:h, :] = rest[h:n, :] + gx[0:h, :]
    own[0:h, :] = rest[n:n + h, :] + gx[h:n, :]
    own[h:n, :] = rest[n + h:2 * n, :] + gy[h:n, :]
    if extra:
        v = rest[2 * n:2 * n + 8, :] + gx[n:n + 8, :]
        sy[h:h + 8, :] = v
        own[n:n + 8, :] = v


def body(n_dp, n_tp, tokens_in, w_qkv, b_qv, w_out, b_out, gain_one, shift_one, w_up, b_up,
         w_down, b_down, gain_two, shift_two, bucket_len, key_mask, block_perm, grad_output):
    T, D = tokens_in.shape
    nh = block_perm.shape[0]
    hw = w_qkv.shape[2]
    H = w_up.shape[1]
    R = T // n_tp
    d = lax.axis_index("dp").astype(jnp.int32)
    t = lax.axis_index("tensor").astype(jnp.int32)[None]
    core, yx = d & 1, (d >> 1) & 3
    J = (core * 4 + yx)[None]
    place = jnp.stack([core, yx])

    def swap(b, z):
        return [(i * n_tp + k, (i ^ b) * n_tp + (k ^ z)) for i in range(n_dp) for k in range(n_tp)]

    CORE, X, Y = swap(1, 0), swap(2, 0), swap(4, 0)

    def pp(v, perm):
        return lax.ppermute(v, AXES, perm)

    row = lambda v: v.reshape(1, -1)

    a_piece = prep_a(J, block_perm, w_qkv, w_out, b_qv, row(b_up))
    za = [pp(a_piece, swap(0, k)) for k in range(1, n_tp)]
    f_piece = prep_f(J, w_up, w_down, za[0])
    zf = [pp(f_piece, swap(0, k)) for k in range(1, n_tp)]

    def spread(cur, flip):
        rx, ry = pp(cur, X), pp(cur, Y)
        rd = pp(ry, X) if flip else pp(rx, Y)
        return cur, rx, ry, rd

    def finish(parts):
        return (*parts, pp(cat(parts), CORE))

    a_parts = [finish(spread(v, k % 2)) for k, v in enumerate(za)]
    f_parts = [finish(spread(v, (k + 1) % 2)) for k, v in enumerate(zf)]

    pos = jnp.arange(T, dtype=jnp.int32)
    code = pos >> (lax.population_count(bucket_len[0] - 1) - 1)
    kcode = jnp.where(key_mask == 1, code, -1)
    q_col, q_row = code[:, None], code.reshape(2, 1, T // 2)
    k_col, k_row = kcode[:, None], kcode.reshape(2, 1, T // 2)

    acc, qkv, attended = attn_own(nh, block_perm, bucket_len, tokens_in, w_qkv, w_out, b_qv, q_col, k_row)
    att_saved = [(w_qkv, w_out, qkv)]
    for k in range(n_tp - 1):
        acc, qkv, w3, wo = attn_other(nh, J, bucket_len, tokens_in, a_parts[k], q_col, k_row, acc)
        att_saved.append((w3, wo, qkv))
    h_low, scaled_one, inverse_one = pcall(
        ln1_kernel, "ln1", [sds((T, D), BF), sds((T, D), F32), sds((T, 1), F32)], (),
        [tokens_in, acc, row(b_out), row(gain_one), row(shift_one)], us=2)

    acc, gp, act_low = ffn_own(h_low, w_up, w_down, row(b_up))
    ffn_saved = [(w_up, w_down, gp)]
    for k in range(n_tp - 1):
        acc, gp, wu, wd = ffn_other(J, h_low, za[k], f_parts[k], acc)
        ffn_saved.append((wu, wd, gp))
    layer_out, two, two_low, vec_two = pcall(
        ln2_kernel, "ln2", [sds((R, D), F32), sds((T, D), F32), sds((T, D), BF), sds((3, D), F32)], [t],
        [scaled_one, row(gain_one), row(shift_one), acc, row(b_down), row(gain_two), row(shift_two), grad_output], us=4)

    fast = n_dp == 8
    n = D // 8
    acc, up_low, grad_b_up = ffn_bwd(True, two_low, *ffn_saved[0])
    if fast:
        keep, give = pcall(grads_ffn_kernel, "grads_ffn", [sds((D // 2, 2 * H), F32)] * 2, [place],
                           [two_low, act_low, h_low, up_low], scratch=[pltpu.VMEM((D, 2 * H), F32)], us=4)
        got = pp(give, CORE)
    (acc,) = ffn_bwd(False, two_low, *ffn_saved[1], acc)
    (acc,) = ffn_bwd(False, two_low, *ffn_saved[2], acc)
    if fast:
        sx, sy, rest = pcall(functools.partial(stage1_kernel, n, False), "stage1",
                             [sds((n, 2 * H), F32)] * 2 + [sds((2 * n, 2 * H), F32)], (), [keep, got], us=1)
        gx, gy = pp(sx, X), pp(sy, Y)
    for k in range(3, n_tp):
        (acc,) = ffn_bwd(False, two_low, *ffn_saved[k], acc)
    one_low, total, vec = pcall(
        ln1_back_kernel, "ln1_back", [sds((T, D), BF), sds((R, D), F32), sds((8, D), F32)], [t],
        [two, acc, scaled_one, inverse_one, row(gain_one), vec_two, grad_b_up], us=2)

    def sum_tp(v):
        for k in (1, 2):
            v = jnp.where(jnp.arange(8)[:, None] < 6, v + pp(v, swap(0, k)), v)
        return v

    g_low, part, cols = attn_bwd_own(nh, t, block_perm, bucket_len, one_low, *att_saved[0], q_row, k_col, R)
    if n_tp == 4:
        vec = sum_tp(vec)
    else:
        vec = jnp.concatenate([lax.psum(vec[:6], "tensor"), vec[6:]])
    if fast:
        sx2, sy2, own_f = pcall(functools.partial(stage2_kernel, n, False), "stage2",
                                [sds((n // 2, 2 * H), F32)] * 2 + [sds((n, 2 * H), F32)], (), [rest, gx, gy], us=1)
        fx, fy = pp(sx2, X), pp(sy2, Y)
        keep, give = pcall(grads_attn_kernel, "grads_attn", [sds((D // 2 + 8, 4 * hw), F32)] * 2, [place],
                           [tokens_in, g_low, one_low, attended, cols, vec], scratch=[pltpu.VMEM((D, 4 * hw), F32)], us=3)
        got = pp(give, CORE)
    total = total + part
    acc = attn_bwd_other(nh, t, bucket_len, one_low, *att_saved[1], q_row, k_col, za[0], total)
    if fast:
        sx, sy, rest = pcall(functools.partial(stage1_kernel, n, True), "stage1",
                             [sds((n + 8, 4 * hw), F32), sds((n, 4 * hw), F32), sds((2 * n + 8, 4 * hw), F32)], (), [keep, got], us=1)
        gx, gy = pp(sx, X), pp(sy, Y)
    acc = attn_bwd_other(nh, t, bucket_len, one_low, *att_saved[2], q_row, k_col, za[1], acc)
    if fast:
        sx2, sy2, own_a = pcall(functools.partial(stage2_kernel, n, True), "stage2",
                                [sds((n // 2, 4 * hw), F32), sds((n // 2 + 8, 4 * hw), F32), sds((n + 8, 4 * hw), F32)], (),
                                [rest, gx, gy], us=1)
        ax, ay = pp(sx2, X), pp(sy2, Y)
    for k in range(3, n_tp):
        acc = attn_bwd_other(nh, t, bucket_len, one_low, *att_saved[k], q_row, k_col, za[k - 1], acc)
    grad_tokens = acc

    if fast:
        h = n // 2
        f = own_f + jnp.concatenate([fy, fx])
        a = own_a[:n] + jnp.concatenate([ay[:h], ax])
        vec = own_a[n:] + ay[h:]
    else:
        def scatter(x, y):
            return lax.psum_scatter(dg(x, y, TN), "dp", scatter_dimension=0, tiled=True)

        f = jnp.concatenate([scatter(two_low, act_low), scatter(h_low, up_low)], axis=1)
        a = jnp.concatenate([scatter(tokens_in, g_low), scatter(one_low, attended)], axis=1)
        vec = lax.psum(jnp.concatenate([vec[:7], jnp.pad(jnp.concatenate([cols[:, :hw], cols[:, 2 * hw:]], 1), ((0, 0), (0, D - 2 * hw)))]), "dp")
    own_qkv = jnp.swapaxes(a[:, :3 * hw].reshape(-1, 3, hw), 0, 1)
    return (layer_out, grad_tokens, own_qkv, vec[7, :2 * hw].reshape(2, hw), a[:, 3 * hw:].T, vec[0], vec[1], vec[2], f[:, H:],
            vec[6, :H], f[:, :H].T, vec[3], vec[4], vec[5])


def solution(mesh):
    n_dp, n_tp = mesh.shape["dp"], mesh.shape["tensor"]
    in_specs = (
        P("dp", None), P(None, None, "tensor"), P(None, "tensor"), P("tensor", None), P(), P(), P(),
        P(None, "tensor"), P("tensor"), P("tensor", None), P(), P(), P(), P("dp"), P("dp"),
        P("tensor", None), P("dp", None),
    )
    out_specs = (
        P(("dp", "tensor"), None), P(("dp", "tensor"), None), P(None, "dp", "tensor"), P(None, "tensor"),
        P("tensor", "dp"), P(), P(), P(), P("dp", "tensor"), P("tensor"), P("tensor", "dp"), P(), P(), P(),
    )
    return jax.shard_map(functools.partial(body, n_dp, n_tp), mesh=mesh, in_specs=in_specs, out_specs=out_specs, check_vma=False)
```

```python
import functools
import jax
import jax.numpy as jnp
from jax import lax
from jax.experimental import pallas as pl
from jax.experimental.pallas import tpu as pltpu
from jax.sharding import PartitionSpec as P

F32 = jnp.float32
BF = jnp.bfloat16
NT = (((1,), (1,)), ((), ()))
NN = (((1,), (0,)), ((), ()))
TN = (((0,), (0,)), ((), ()))
NEG = -1e30
LN_EPS = 1e-06
AXES = ("dp", "tensor")
VM = pl.BlockSpec(memory_space=pltpu.VMEM)
SM = pl.BlockSpec(memory_space=pltpu.SMEM)
ANY = pl.BlockSpec(memory_space=pl.ANY)


def dg(a, b, dn):
    return lax.dot_general(a, b, dn, preferred_element_type=F32)


def sds(shape, dtype):
    return jax.ShapeDtypeStruct(shape, dtype)


def pcall(fn, name, out, smem, ins, scratch=(), alias=None, vmem=20, us=8, after=()):
    n, k = len(smem) + len(ins), len(after)

    def run(*refs):
        fn(*refs[:n], *refs[n + k:])

    return pl.pallas_call(
        run, out_shape=tuple(out), in_specs=[SM] * len(smem) + [VM] * len(ins) + [ANY] * k,
        out_specs=(VM,) * len(out),
        input_output_aliases={len(smem) + i: o for i, o in (alias or {}).items()}, scratch_shapes=list(scratch),
        cost_estimate=pl.CostEstimate(flops=int(us * 8e8), bytes_accessed=int(us * 2e6), transcendentals=0),
        compiler_params=pltpu.CompilerParams(vmem_limit_bytes=vmem << 20), name=name)(*smem, *ins, *after)


def prep_a_kernel(J, perm, w, wo, b_qv, b_up, a):
    hw = w.shape[2]
    for c in range(3):
        v = w[c].astype(F32)
        for g in range(4):
            a[c * 24:(c + 1) * 24, g * hw:(g + 1) * hw] = v[g * 24:(g + 1) * 24, :]
    a[72:96, :] = wo[...].astype(F32)
    b = b_qv[...].astype(F32)
    a[96:97, 0:hw] = b[0:1]
    a[96:97, hw:2 * hw] = b[1:2]
    a[96:97, 2 * hw:] = jnp.zeros((1, a.shape[1] - 2 * hw), F32)
    a[97:98, :] = b_up[...].astype(F32)
    bits = perm[0, 0]
    for h in range(1, perm.shape[0]):
        bits = bits + (perm[h, 0] << h)
    a[98:104, :] = jnp.full((6, a.shape[1]), bits.astype(F32))


def prep_a(J, perm, w_qkv, w_out, b_qv, b_up):
    D, hw = w_qkv.shape[1:]
    nh = perm.shape[0]
    return pl.pallas_call(
        prep_a_kernel, out_shape=sds((104, D), F32),
        grid_spec=pltpu.PrefetchScalarGridSpec(
            num_scalar_prefetch=2, grid=(1,),
            in_specs=[pl.BlockSpec((3, D // 8, hw), lambda i, J, p: (0, J[0], 0)),
                      pl.BlockSpec((hw // 8, D), lambda i, J, p: (J[0], 0)),
                      pl.BlockSpec((2, hw), lambda i, J, p: (0, 0)),
                      pl.BlockSpec((1, D), lambda i, J, p: (0, 0))],
            out_specs=pl.BlockSpec((104, D), lambda i, J, p: (0, 0))),
        cost_estimate=pl.CostEstimate(flops=1000, bytes_accessed=1000, transcendentals=0),
        compiler_params=pltpu.CompilerParams(vmem_limit_bytes=16 << 20), name="prep_a")(J, perm, w_qkv, w_out, b_qv, b_up)


def prep_f_kernel(J, wu, wd, wuq, wdq, after, f, uq, dq):
    f[0:96, :] = wu[...].astype(F32)
    f[96:192, :] = wd[...].astype(F32)
    uq[...] = wuq[...].astype(F32)
    dq[...] = wdq[...].astype(F32)


def prep_f(J, w_up, w_down, after):
    D, H = w_up.shape
    return pl.pallas_call(
        prep_f_kernel, out_shape=(sds((192, D), F32), sds((192, H), F32), sds((192, D), F32)),
        grid_spec=pltpu.PrefetchScalarGridSpec(
            num_scalar_prefetch=1, grid=(1,),
            in_specs=[pl.BlockSpec((D // 8, H), lambda i, J: (J[0], 0)), pl.BlockSpec((H // 8, D), lambda i, J: (J[0], 0)),
                      pl.BlockSpec((D // 4, H), lambda i, J: (J[1], 0)), pl.BlockSpec((H // 4, D), lambda i, J: (J[2], 0)), ANY],
            out_specs=(pl.BlockSpec((192, D), lambda i, J: (0, 0)),) * 3),
        cost_estimate=pl.CostEstimate(flops=1000, bytes_accessed=1000, transcendentals=0),
        compiler_params=pltpu.CompilerParams(vmem_limit_bytes=16 << 20), name="prep_f")(J, w_up, w_down, w_up, w_down, after)


def cat_kernel(a, b, c, d, o):
    o[0], o[1], o[2], o[3] = a[...], b[...], c[...], d[...]


def cat(parts, after=()):
    return pcall(cat_kernel, "cat", [sds((4,) + parts[0].shape, F32)], (), parts, vmem=16, us=1e-5, after=after)[0]


def attend_fwd(nh, full, first, qc, kc, qkv, att):
    hw = 64 * nh
    for h in range(nh):
        flag = first(h)
        for i in range(2):
            j = jnp.where(full, flag if i == 0 else 1 - flag, i)
            rj = pl.ds(pl.multiple_of(j * 512, 512), 512)
            q = qkv[i * 512:(i + 1) * 512, h * 64:(h + 1) * 64] * jnp.asarray(0.125, BF)
            s = dg(q, qkv[rj, hw + h * 64:hw + (h + 1) * 64], NT)
            s = jnp.where((qc[i * 512:(i + 1) * 512, :] ^ flag) == kc[j], s, NEG)
            p = jnp.exp(s - jnp.max(s, axis=1, keepdims=True))
            p = (p * (1.0 / jnp.sum(p, axis=1, keepdims=True))).astype(BF)
            att[i * 512:(i + 1) * 512, h * 64:(h + 1) * 64] = dg(p, qkv[rj, 2 * hw + h * 64:2 * hw + (h + 1) * 64], NN).astype(BF)


def project(x, w3, bq, bv, qkv, hw):
    qkv[:, 0:hw] = (dg(x[...], w3[0], NN) + bq).astype(BF)
    qkv[:, hw:2 * hw] = dg(x[...], w3[1], NN).astype(BF)
    qkv[:, 2 * hw:3 * hw] = (dg(x[...], w3[2], NN) + bv).astype(BF)


def attn_own_kernel(nh, perm, buck, tok, w3, wo, b_qv, qc, kc, acc, qkv, att):
    hw = 64 * nh
    b = b_qv[...].astype(F32)
    project(tok, w3, b[0:1], b[1:2], qkv, hw)
    attend_fwd(nh, buck[0] == 1024, lambda h: perm[h, 0], qc, kc, qkv, att)
    acc[...] = dg(att[...], wo[...], NN)


def piece_bits(c0):
    return jnp.max(c0[98:99, 0:128]).astype(jnp.int32)


def attn_other_kernel(nh, J, buck, tok, c0, c1, c2, c3, o, qc, kc, acc_in, acc, qkv, w3, wo, att, w32, wo32):
    hw = 64 * nh
    D = tok.shape[1]
    for r in range(8):
        piece = (c0, c1, c2, c3)[r] if r < 4 else o.at[r - 4]
        at = J[0] ^ r
        for c in range(3):
            v = piece[c * 24:(c + 1) * 24, :]
            for g in range(4):
                w32[pl.ds(pl.multiple_of(c * D + at * 96 + g * 24, 8), 24), :] = v[:, g * hw:(g + 1) * hw]
        wo32[pl.ds(pl.multiple_of(at * 24, 8), 24), :] = piece[72:96, :]
    for c in range(3):
        w3[c] = w32[c * D:(c + 1) * D, :].astype(BF)
    wo[...] = wo32[...].astype(BF)
    project(tok, w3, c0[96:97, 0:hw], c0[96:97, hw:2 * hw], qkv, hw)
    bits = piece_bits(c0)
    attend_fwd(nh, buck[0] == 1024, lambda h: (bits >> h) & 1, qc, kc, qkv, att)
    acc[...] = acc_in[...] + dg(att[...], wo[...], NN)


def attn_own(nh, perm, buck, tok, w3, wo, b_qv, qc, kc):
    T, D = tok.shape
    hw = 64 * nh
    return pcall(functools.partial(attn_own_kernel, nh), "attn_own",
                 [sds((T, D), F32), sds((T, 3 * hw), BF), sds((T, hw), BF)], [perm, buck], [tok, w3, wo, b_qv, qc, kc], us=1e-5)


def attn_other(nh, J, buck, tok, pieces, qc, kc, acc, after=()):
    T, D = tok.shape
    hw = 64 * nh
    return pcall(functools.partial(attn_other_kernel, nh), "attn_other",
                 [sds((T, D), F32), sds((T, 3 * hw), BF), sds((3, D, hw), BF), sds((hw, D), BF)],
                 [J, buck], [tok, *pieces, qc, kc, acc],
                 scratch=[pltpu.VMEM((T, hw), BF), pltpu.VMEM((3 * D, hw), F32), pltpu.VMEM((hw, D), F32)],
                 alias={8: 0}, us=1e-5, after=after)


def attn_bwd_kernel(nh, own, *refs):
    if own:
        t, perm, buck, g, w3, wo, qkv, qcr, kcc, dst, acc, cols, datt = refs
    else:
        t, buck, g, w3, wo, qkv, qcr, kcc, c0, acc_in, acc, dst, datt = refs
        bits = piece_bits(c0)
    hw = 64 * nh
    datt[...] = dg(g[...], wo[...], NT).astype(BF)
    full = buck[0] == 1024
    for h in range(nh):
        flag = perm[h, 0] if own else (bits >> h) & 1
        for i in range(2):
            j = jnp.where(full, flag if i == 0 else 1 - flag, i)
            rj = pl.ds(pl.multiple_of(j * 512, 512), 512)
            q = qkv[i * 512:(i + 1) * 512, h * 64:(h + 1) * 64] * jnp.asarray(0.125, BF)
            kj = qkv[rj, hw + h * 64:hw + (h + 1) * 64]
            vj = qkv[rj, 2 * hw + h * 64:2 * hw + (h + 1) * 64]
            do = datt[i * 512:(i + 1) * 512, h * 64:(h + 1) * 64]
            s = dg(kj, q, NT)
            s = jnp.where((qcr[i] ^ flag) == kcc[rj, :], s, NEG)
            p = jnp.exp(s - jnp.max(s, axis=0, keepdims=True))
            p = p * (1.0 / jnp.sum(p, axis=0, keepdims=True))
            dp = dg(vj, do, NT)
            ds = (p * (dp - jnp.sum(p * dp, axis=0, keepdims=True))).astype(BF)
            dst[rj, 2 * hw + h * 64:2 * hw + (h + 1) * 64] = dg(p.astype(BF), do, NN).astype(BF)
            dst[rj, hw + h * 64:hw + (h + 1) * 64] = dg(ds, q, NN).astype(BF)
            dst[i * 512:(i + 1) * 512, h * 64:(h + 1) * 64] = (dg(ds, kj, TN) * 0.125).astype(BF)
    R = acc.shape[0]
    rows = pl.ds(pl.multiple_of(t[0] * R, R), R)
    y = dg(dst[rows, 0:hw], w3[0], NT) + dg(dst[rows, hw:2 * hw], w3[1], NT) + dg(dst[rows, 2 * hw:3 * hw], w3[2], NT)
    if own:
        acc[...] = y
        cols[...] = jnp.sum(dst[...].astype(F32), axis=0, keepdims=True)
    else:
        acc[...] = acc_in[...] + y


def attn_bwd_own(nh, t, perm, buck, g, w3, wo, qkv, qcr, kcc, R, after=()):
    T, D = g.shape
    hw = 64 * nh
    return pcall(functools.partial(attn_bwd_kernel, nh, True), "attn_bwd_own",
                 [sds((T, 3 * hw), BF), sds((R, D), F32), sds((1, 3 * hw), F32)], [t, perm, buck],
                 [g, w3, wo, qkv, qcr, kcc], scratch=[pltpu.VMEM((T, hw), BF)], after=after)


def attn_bwd_other(nh, t, buck, g, w3, wo, qkv, qcr, kcc, c0, acc, after=()):
    T, D = g.shape
    hw = 64 * nh
    return pcall(functools.partial(attn_bwd_kernel, nh, False), "attn_bwd_other", [sds(acc.shape, F32)], [t, buck],
                 [g, w3, wo, qkv, qcr, kcc, c0, acc],
                 scratch=[pltpu.VMEM((T, 3 * hw), BF), pltpu.VMEM((T, hw), BF)], alias={7: 0}, after=after)[0]


ERFC_P = 0.3
ERFC = (0.16919777, 0.17054635, 0.14956615, 0.21002719, -0.08287393, 0.53022837, -0.49656831, 0.47774502, -0.1278686)


def phi_pair(v):
    e = jnp.exp(v * v * -0.5)
    t = 1.0 / (1.0 + jnp.abs(v) * (ERFC_P * 0.7071067811865476))
    a = jnp.full_like(t, ERFC[-1])
    for k in ERFC[-2::-1]:
        a = a * t + k
    tail = 0.5 * (a * t * e)
    return jnp.where(v >= 0, 1.0 - tail, tail), e * 0.3989422804014327


def ffn_rows(h, wu, wd, b, acc_in, acc, gp, act):
    n = 256
    for r in range(h.shape[0] // n):
        rows = slice(r * n, (r + 1) * n)
        up = dg(h[rows, :], wu[...], NN) + b
        big, density = phi_pair(up)
        gp[rows, :] = big + up * density
        a = (up * big).astype(BF)
        if act is not None:
            act[rows, :] = a
        y = dg(a, wd[...], NN)
        acc[rows, :] = y if acc_in is None else acc_in[rows, :] + y


def ffn_own_kernel(h, wu, wd, b, acc, gp, act):
    ffn_rows(h, wu, wd, b[...].astype(F32), None, acc, gp, act)


def ffn_other_kernel(pair, J, h, a0, c0, c1, c2, c3, o, acc_in, acc, gp, wu, wd):
    if pair:
        for r, (u, d) in enumerate(((c0, c2), (c1, c3), (o.at[0], o.at[2]), (o.at[1], o.at[3]))):
            wu[pl.ds(pl.multiple_of((J[1] ^ r) * 192, 32), 192), :] = u[...].astype(BF)
            wd[pl.ds(pl.multiple_of((J[2] ^ r) * 192, 32), 192), :] = d[...].astype(BF)
    for r in range(0 if pair else 8):
        piece = (c0, c1, c2, c3)[r] if r < 4 else o.at[r - 4]
        rows = pl.ds(pl.multiple_of((J[0] ^ r) * 96, 32), 96)
        wu[rows, :] = piece[0:96, :].astype(BF)
        wd[rows, :] = piece[96:192, :].astype(BF)
    ffn_rows(h, wu, wd, a0[97:98, :], acc_in, acc, gp, None)


def ffn_own(h, wu, wd, b, after=()):
    T, D = h.shape
    H = wu.shape[1]
    return pcall(ffn_own_kernel, "ffn_own", [sds((T, D), F32), sds((T, H), F32), sds((T, H), BF)], (), [h, wu, wd, b], us=1e-5, after=after)


def ffn_other(pair, J, h, a0, pieces, acc, after=()):
    T, D = h.shape
    H = 768
    return pcall(functools.partial(ffn_other_kernel, pair), "ffn_other", [sds((T, D), F32), sds((T, H), F32), sds((D, H), BF), sds((H, D), BF)],
                 [J], [h, a0, *pieces, acc], alias={7: 0}, us=1e-5, after=after)


def ffn_bwd_kernel(own, *refs):
    if own:
        g, wu, wd, gp, acc, up_low, bsum = refs
    else:
        g, wu, wd, gp, acc_in, acc = refs
    n = 256
    bs = None
    for r in range(g.shape[0] // n):
        rows = slice(r * n, (r + 1) * n)
        du = (dg(g[rows, :], wd[...], NT) * gp[rows, :]).astype(BF)
        if own:
            up_low[rows, :] = du
            s = jnp.sum(du.astype(F32), axis=0, keepdims=True)
            bs = s if bs is None else bs + s
        y = dg(du, wu[...], NT)
        acc[rows, :] = y if own else acc_in[rows, :] + y
    if own:
        bsum[...] = bs


def ffn_bwd(own, g, wu, wd, gp, acc=None, after=()):
    T, D = g.shape
    H = gp.shape[1]
    out = [sds((T, D), F32)]
    if own:
        out += [sds((T, H), BF), sds((1, H), F32)]
    return pcall(functools.partial(ffn_bwd_kernel, own), "ffn_bwd", out, (), [g, wu, wd, gp] + ([] if own else [acc]),
                 alias=None if own else {4: 0}, us=4, after=after)


def norm(s):
    center = s - jnp.mean(s, axis=-1, keepdims=True)
    inverse = lax.rsqrt(jnp.mean(center * center, axis=-1, keepdims=True) + LN_EPS)
    return center * inverse, inverse


def norm_back(w, scaled, inverse):
    return inverse * (w - jnp.mean(w, axis=-1, keepdims=True) - scaled * jnp.mean(w * scaled, axis=-1, keepdims=True))


def ln1_kernel(tok, acc, b_out, gain, shift, h_low, scaled, inverse):
    n = 128
    for r in range(tok.shape[0] // n):
        rows = slice(r * n, (r + 1) * n)
        x, inv = norm(tok[rows, :].astype(F32) + acc[rows, :] + b_out[...].astype(F32))
        scaled[rows, :] = x
        inverse[rows, :] = inv
        h_low[rows, :] = (x * gain[...] + shift[...]).astype(BF)


def ln2_kernel(t, scaled, gain1, shift1, acc, b_down, gain2, shift2, gy, out, two, two_low, vec):
    R = out.shape[0]

    def rows_of(rows):
        s = scaled[rows, :] * gain1[...] + shift1[...] + acc[rows, :] + b_down[...].astype(F32)
        x, inv = norm(s)
        g = gy[rows, :].astype(F32)
        return x, g, norm_back(g * gain2[...], x, inv)

    n = 128
    for r in range(gy.shape[0] // n):
        rows = slice(r * n, (r + 1) * n)
        _, _, d = rows_of(rows)
        two[rows, :] = d
        two_low[rows, :] = d.astype(BF)
    tot = [jnp.zeros((1, gy.shape[1]), F32)] * 3
    for r in range(R // n):
        rows = pl.ds(pl.multiple_of(t[0] * R + r * n, n), n)
        x, g, d = rows_of(rows)
        out[r * n:(r + 1) * n, :] = x * gain2[...] + shift2[...]
        for i, v in enumerate((d, g * x, g)):
            tot[i] = tot[i] + jnp.sum(v, axis=0, keepdims=True)
    for i in range(3):
        vec[i:i + 1, :] = tot[i]


def ln1_back_kernel(t, two, acc, scaled, inverse, gain1, vec2, bup, one_low, one_own, vec):
    R = one_own.shape[0]
    n = 128

    def rows_of(rows):
        e = two[rows, :] + acc[rows, :]
        return e, norm_back(e * gain1[...], scaled[rows, :], inverse[rows, :])

    for r in range(two.shape[0] // n):
        rows = slice(r * n, (r + 1) * n)
        one_low[rows, :] = rows_of(rows)[1].astype(BF)
    tot = [jnp.zeros((1, two.shape[1]), F32)] * 3
    for r in range(R // n):
        rows = pl.ds(pl.multiple_of(t[0] * R + r * n, n), n)
        e, d = rows_of(rows)
        one_own[r * n:(r + 1) * n, :] = d
        for i, v in enumerate((d, e * scaled[rows, :], e)):
            tot[i] = tot[i] + jnp.sum(v, axis=0, keepdims=True)
    for i in range(3):
        vec[i:i + 1, :] = tot[i]
    vec[3:6, :] = vec2[0:3, :]
    vec[6:7, :] = bup[...]
    vec[7:8, :] = jnp.zeros_like(bup)


def split_blocks(place, full, keep, give):
    n = full.shape[0] // 8
    for q in range(4):
        for mine, ref in ((0, keep), (1, give)):
            b = ((place[1] ^ q) * 2 + (place[0] ^ mine)) * n
            ref[q * n:(q + 1) * n, :] = full[pl.ds(pl.multiple_of(b, 32), n), :]


def grads_ffn_kernel(place, two_low, act, h_low, up_low, keep, give, full):
    H = act.shape[1]
    full[:, 0:H] = dg(two_low[...], act[...], TN)
    full[:, H:] = dg(h_low[...], up_low[...], TN)
    split_blocks(place, full, keep, give)


def grads_attn_kernel(place, tok, dst, one_low, att, cols, vec, keep, give, full):
    W = dst.shape[1]
    full[:, 0:W] = dg(tok[...], dst[...], TN)
    full[:, W:] = dg(one_low[...], att[...], TN)
    n = full.shape[0] // 2
    split_blocks(place, full, keep, give)
    give[n:n + 8, :] = vec[...]
    give[n + 7:n + 8, 0:W // 3] = cols[:, 0:W // 3]
    give[n + 7:n + 8, W // 3:2 * W // 3] = cols[:, 2 * W // 3:]
    keep[n:n + 8, :] = give[n:n + 8, :]


def stage1_kernel(n, extra, keep, got, sx, sy, rest):
    h = n // 2

    def s(a, b):
        return keep[a:b, :] + got[a:b, :]

    sx[0:h, :] = s(3 * n, 3 * n + h)
    sx[h:n, :] = s(n, n + h)
    sy[0:h, :] = s(3 * n + h, 4 * n)
    sy[h:n, :] = s(2 * n + h, 3 * n)
    rest[0:h, :] = s(n + h, 2 * n)
    rest[h:n, :] = s(2 * n, 2 * n + h)
    rest[n:2 * n, :] = s(0, n)
    if extra:
        v = s(4 * n, 4 * n + 8)
        sx[n:n + 8, :] = v
        rest[2 * n:2 * n + 8, :] = v


def stage2_kernel(n, extra, rest, gx, gy, sx, sy, own):
    h = n // 2
    sx[0:h, :] = rest[0:h, :] + gy[0:h, :]
    sy[0:h, :] = rest[h:n, :] + gx[0:h, :]
    own[0:h, :] = rest[n:n + h, :] + gx[h:n, :]
    own[h:n, :] = rest[n + h:2 * n, :] + gy[h:n, :]
    if extra:
        v = rest[2 * n:2 * n + 8, :] + gx[n:n + 8, :]
        sy[h:h + 8, :] = v
        own[n:n + 8, :] = v


def body(n_dp, n_tp, tokens_in, w_qkv, b_qv, w_out, b_out, gain_one, shift_one, w_up, b_up,
         w_down, b_down, gain_two, shift_two, bucket_len, key_mask, block_perm, grad_output):
    T, D = tokens_in.shape
    nh = block_perm.shape[0]
    hw = w_qkv.shape[2]
    H = w_up.shape[1]
    R = T // n_tp
    d = lax.axis_index("dp").astype(jnp.int32)
    t = lax.axis_index("tensor").astype(jnp.int32)[None]
    core, yx = d & 1, (d >> 1) & 3
    J = jnp.stack([core * 4 + yx, core * 2 + (yx & 1), core * 2 + (yx >> 1)])
    place = jnp.stack([core, yx])

    def swap(b, z):
        return [(i * n_tp + k, (i ^ b) * n_tp + (k ^ z)) for i in range(n_dp) for k in range(n_tp)]

    CORE, X, Y = swap(1, 0), swap(2, 0), swap(4, 0)

    def pp(v, perm):
        return lax.ppermute(v, AXES, perm)

    def row(v):
        return v.reshape(1, -1)

    def tie(v, *first):
        return lax.optimization_barrier((v, first))[0]

    pos = jnp.arange(T, dtype=jnp.int32)
    code = pos >> (lax.population_count(bucket_len[0] - 1) - 1)
    kcode = jnp.where(key_mask == 1, code, -1)
    q_col, q_row = code[:, None], code.reshape(2, 1, T // 2)
    k_col, k_row = kcode[:, None], kcode.reshape(2, 1, T // 2)

    def sync(*v):
        return lax.optimization_barrier(v)

    NEXT = [(i * n_tp + k, i * n_tp + (k + 1) % n_tp) for i in range(n_dp) for k in range(n_tp)]
    PREV = [(i * n_tp + (k + 1) % n_tp, i * n_tp + k) for i in range(n_dp) for k in range(n_tp)]

    def attn(pieces, acc):
        acc, qkv, w3, wo = attn_other(nh, J, bucket_len, tokens_in, pieces, q_col, k_row, acc)
        att_saved.append((w3, wo, qkv))
        return acc

    def ffn(a0, pieces, acc, pair=False):
        acc, gp, wu, wd = ffn_other(pair, J, h_low, a0, pieces, acc)
        ffn_saved.append((wu, wd, gp))
        return acc

    a_piece = prep_a(J, block_perm, w_qkv, w_out, b_qv, row(b_up))
    z1 = pp(a_piece, NEXT)
    acc, qkv, attended = attn_own(nh, block_perm, bucket_len, tokens_in, w_qkv, w_out, b_qv, q_col, k_row)
    att_saved = [(w_qkv, w_out, qkv)]

    z1, acc = sync(z1, acc)
    z2, x1, y1 = pp(z1, NEXT), pp(z1, X), pp(z1, Y)

    z2, x1, y1 = sync(z2, x1, y1)
    z3, x2, y2 = pp(a_piece, PREV), pp(z2, X), pp(z2, Y)
    f_piece, u_quarter, d_quarter = prep_f(J, w_up, w_down, z2)

    z3, x2, y2, f_piece, u_quarter, d_quarter = sync(z3, x2, y2, f_piece, u_quarter, d_quarter)
    f1, d2, d1 = pp(f_piece, NEXT), pp(y2, X), pp(x1, Y)

    d1, d2 = sync(d1, d2)
    x3, y3 = pp(z3, X), pp(z3, Y)
    c1 = pp(cat((z1, x1, y1, d1)), CORE)
    c2 = pp(cat((z2, x2, y2, d2), (c1,)), CORE)
    acc = attn((z1, x1, y1, d1, c1), acc)

    x3, y3, f1, c2, acc = sync(x3, y3, f1, c2, acc)
    f2, d3, fy1 = pp(f1, NEXT), pp(y3, X), pp(f1, Y)
    acc = attn((z2, x2, y2, d2, c2), acc)

    f2, d3, fy1, acc = sync(f2, d3, fy1, acc)
    fx1, fy2, zu = pp(f1, X), pp(f2, Y), pp(u_quarter, PREV)
    c3 = pp(cat((z3, x3, y3, d3)), CORE)
    acc = attn((z3, x3, y3, d3, c3), acc)

    fx1, fy2, zu, acc = sync(fx1, fy2, zu, acc)
    fx2, fd1, zd = pp(f2, X), pp(fx1, Y), pp(d_quarter, PREV)
    h_low, scaled_one, inverse_one = pcall(
        ln1_kernel, "ln1", [sds((T, D), BF), sds((T, D), F32), sds((T, 1), F32)], (),
        [tokens_in, acc, row(b_out), row(gain_one), row(shift_one)], us=1e-5)
    acc, gp, act_low = ffn_own(h_low, w_up, w_down, row(b_up))
    ffn_saved = [(w_up, w_down, gp)]

    fx2, fd1, zd, acc = sync(fx2, fd1, zd, acc)
    fd2, yd = pp(fy2, X), pp(zd, Y)
    k1 = pp(cat((f1, fx1, fy1, fd1)), CORE)
    acc = ffn(z1, (f1, fx1, fy1, fd1, k1), acc)

    fd2, yd, acc = sync(fd2, yd, acc)
    xu = pp(zu, X)
    k2 = pp(cat((f2, fx2, fy2, fd2)), CORE)
    acc = ffn(z2, (f2, fx2, fy2, fd2, k2), acc)

    xu, acc = sync(xu, acc)
    k3 = pp(cat((zu, xu, zd, yd)), CORE)
    acc = ffn(z3, (zu, xu, zd, yd, k3), acc, pair=True)
    zs = (z1, z2, z3)
    layer_out, two, two_low, vec_two = pcall(
        ln2_kernel, "ln2", [sds((R, D), F32), sds((T, D), F32), sds((T, D), BF), sds((3, D), F32)], [t],
        [scaled_one, row(gain_one), row(shift_one), acc, row(b_down), row(gain_two), row(shift_two), grad_output], us=4)

    fast = n_dp == 8 and n_tp == 4
    n = D // 8

    def stage1(extra, keep, got):
        e = 8 if extra else 0
        W = keep.shape[1]
        sx, sy, rest = pcall(functools.partial(stage1_kernel, n, extra), "stage1",
                             [sds((n + e, W), F32), sds((n, W), F32), sds((2 * n + e, W), F32)], (), [keep, got], us=1)
        return pp(sx, X), pp(sy, Y), rest

    def stage2(extra, rest, gx, gy):
        e = 8 if extra else 0
        W = rest.shape[1]
        sx, sy, own = pcall(functools.partial(stage2_kernel, n, extra), "stage2",
                            [sds((n // 2, W), F32), sds((n // 2 + e, W), F32), sds((n + e, W), F32)], (), [rest, gx, gy], us=1)
        return pp(sx, X), pp(sy, Y), own

    def grads(kernel, W, e, ins, us):
        keep, give = pcall(kernel, "grads", [sds((D // 2 + e, W), F32)] * 2, [place], ins,
                           scratch=[pltpu.VMEM((D, W), F32)], us=us)
        return keep, pp(give, CORE)

    def plus_tp(v, got):
        return jnp.where(jnp.arange(8)[:, None] < 6, v + got, v)

    def bwd_other(k, acc, one_low):
        return attn_bwd_other(nh, t, bucket_len, one_low, *att_saved[k], q_row, k_col, zs[k - 1], acc)

    acc, up_low, grad_b_up = ffn_bwd(True, two_low, *ffn_saved[0])
    if fast:
        keep, got = grads(grads_ffn_kernel, 2 * H, 0, [two_low, act_low, h_low, up_low], 4)
        two_low = tie(two_low, keep)
    for k in range(1, n_tp):
        (acc,) = ffn_bwd(False, two_low, *ffn_saved[k], acc)
    one_low, total, vec = pcall(
        ln1_back_kernel, "ln1_back", [sds((T, D), BF), sds((R, D), F32), sds((8, D), F32)], [t],
        [two, acc, scaled_one, inverse_one, row(gain_one), vec_two, grad_b_up], us=2)
    if fast:
        tv = pp(vec, swap(0, 1))
        gx, gy, rest = stage1(False, keep, tie(got, one_low))
        one_low = tie(one_low, rest)
    g_low, part, cols = attn_bwd_own(nh, t, block_perm, bucket_len, one_low, *att_saved[0], q_row, k_col, R)
    total = total + part
    if fast:
        vec = plus_tp(vec, tie(tv, g_low))
        tv = pp(vec, swap(0, 2))
        fx, fy, own_f = stage2(False, rest, tie(gx, g_low), gy)
        vec = plus_tp(vec, tie(tv, own_f))
        keep, got = grads(grads_attn_kernel, 4 * hw, 8, [tokens_in, g_low, one_low, attended, cols, vec], 3)
        one_low = tie(one_low, keep)
        acc = bwd_other(1, total, one_low)
        ax, ay, rest = stage1(True, keep, tie(got, acc))
        one_low = tie(one_low, rest)
        acc = bwd_other(2, acc, one_low)
        sx2, sy2, own_a = stage2(True, rest, tie(ax, acc), ay)
        ax, ay = sx2, sy2
        acc = bwd_other(3, acc, tie(one_low, own_a))
    else:
        acc = total
        for k in range(1, n_tp):
            acc = bwd_other(k, acc, one_low)
    grad_tokens = acc

    if fast:
        h = n // 2
        f = own_f + jnp.concatenate([fy, fx])
        a = own_a[:n] + jnp.concatenate([ay[:h], ax])
        vec = own_a[n:] + ay[h:]
    else:
        def scatter(x, y):
            return lax.psum_scatter(dg(x, y, TN), "dp", scatter_dimension=0, tiled=True)

        f = jnp.concatenate([scatter(two_low, act_low), scatter(h_low, up_low)], axis=1)
        a = jnp.concatenate([scatter(tokens_in, g_low), scatter(one_low, attended)], axis=1)
        vec = lax.psum(jnp.concatenate([lax.psum(vec[:6], "tensor"), vec[6:7], jnp.pad(jnp.concatenate([cols[:, :hw], cols[:, 2 * hw:]], 1), ((0, 0), (0, D - 2 * hw)))]), "dp")
    own_qkv = jnp.swapaxes(a[:, :3 * hw].reshape(-1, 3, hw), 0, 1)
    return (layer_out, grad_tokens, own_qkv, vec[7, :2 * hw].reshape(2, hw), a[:, 3 * hw:].T, vec[0], vec[1], vec[2], f[:, H:],
            vec[6, :H], f[:, :H].T, vec[3], vec[4], vec[5])


def solution(mesh):
    n_dp, n_tp = mesh.shape["dp"], mesh.shape["tensor"]
    in_specs = (
        P("dp", None), P(None, None, "tensor"), P(None, "tensor"), P("tensor", None), P(), P(), P(),
        P(None, "tensor"), P("tensor"), P("tensor", None), P(), P(), P(), P("dp"), P("dp"),
        P("tensor", None), P("dp", None),
    )
    out_specs = (
        P(("dp", "tensor"), None), P(("dp", "tensor"), None), P(None, "dp", "tensor"), P(None, "tensor"),
        P("tensor", "dp"), P(), P(), P(), P("dp", "tensor"), P("tensor"), P("tensor", "dp"), P(), P(), P(),
    )
    return jax.shard_map(functools.partial(body, n_dp, n_tp), mesh=mesh, in_specs=in_specs, out_specs=out_specs, check_vma=False)
```

```python
import functools
import jax
import jax.numpy as jnp
from jax import lax
from jax.experimental import pallas as pl
from jax.experimental.pallas import tpu as pltpu
from jax.sharding import PartitionSpec as P

F32 = jnp.float32
BF = jnp.bfloat16
NT = (((1,), (1,)), ((), ()))
NN = (((1,), (0,)), ((), ()))
TN = (((0,), (0,)), ((), ()))
NEG = -1e30
LN_EPS = 1e-06
AXES = ("dp", "tensor")
VM = pl.BlockSpec(memory_space=pltpu.VMEM)
SM = pl.BlockSpec(memory_space=pltpu.SMEM)
ANY = pl.BlockSpec(memory_space=pl.ANY)


def dg(a, b, dn):
    return lax.dot_general(a, b, dn, preferred_element_type=F32)


def sds(shape, dtype):
    return jax.ShapeDtypeStruct(shape, dtype)


def pcall(fn, name, out, smem, ins, scratch=(), alias=None, vmem=12, us=8, after=()):
    n, k = len(smem) + len(ins), len(after)

    def run(*refs):
        fn(*refs[:n], *refs[n + k:])

    return pl.pallas_call(
        run, out_shape=tuple(out), in_specs=[SM] * len(smem) + [VM] * len(ins) + [ANY] * k,
        out_specs=(VM,) * len(out),
        input_output_aliases={len(smem) + i: o for i, o in (alias or {}).items()}, scratch_shapes=list(scratch),
        cost_estimate=pl.CostEstimate(flops=int(us * 8e8), bytes_accessed=int(us * 2e6), transcendentals=0),
        compiler_params=pltpu.CompilerParams(vmem_limit_bytes=vmem << 20), name=name)(*smem, *ins, *after)


def prep_a_kernel(J, perm, w, wo, b_qv, b_up, a):
    hw = b_qv.shape[1]
    n = w.shape[0]
    own = jnp.broadcast_to(J[1] < 3, w.shape)
    a[0:n, :] = jnp.where(own, w[...].astype(F32), wo[...].astype(F32))
    b = b_qv[...].astype(F32)
    a[n:n + 1, 0:hw] = b[0:1]
    a[n:n + 1, hw:2 * hw] = b[1:2]
    a[n:n + 1, 2 * hw:] = jnp.zeros((1, a.shape[1] - 2 * hw), F32)
    a[n + 1:n + 2, :] = b_up[...].astype(F32)
    bits = perm[0, 0]
    for h in range(1, perm.shape[0]):
        bits = bits + (perm[h, 0] << h)
    a[n + 2:n + 8, :] = jnp.full((6, a.shape[1]), bits.astype(F32))


def prep_a(J, perm, wq, wo, b_qv, b_up):
    D = wq.shape[1]
    hw = wo.shape[0]
    return pl.pallas_call(
        prep_a_kernel, out_shape=sds((hw + 8, D), F32),
        grid_spec=pltpu.PrefetchScalarGridSpec(
            num_scalar_prefetch=2, grid=(1,),
            in_specs=[pl.BlockSpec((hw, D), lambda i, J, p: (jnp.minimum(J[1], 2), 0)),
                      pl.BlockSpec((hw, D), lambda i, J, p: (0, 0)),
                      pl.BlockSpec((2, hw), lambda i, J, p: (0, 0)),
                      pl.BlockSpec((1, D), lambda i, J, p: (0, 0))],
            out_specs=pl.BlockSpec((hw + 8, D), lambda i, J, p: (0, 0))),
        cost_estimate=pl.CostEstimate(flops=1000, bytes_accessed=1000, transcendentals=0),
        compiler_params=pltpu.CompilerParams(vmem_limit_bytes=12 << 20), name="prep_a")(J, perm, wq, wo, b_qv, b_up)


def prep_f_kernel(J, wu, wd, wuq, wdq, after, f, uq, dq):
    f[0:96, :] = wu[...].astype(F32)
    f[96:192, :] = wd[...].astype(F32)
    uq[...] = wuq[...].astype(F32)
    dq[...] = wdq[...].astype(F32)


def prep_f(J, w_up, w_down, after):
    D, H = w_up.shape
    return pl.pallas_call(
        prep_f_kernel, out_shape=(sds((192, D), F32), sds((192, H), F32), sds((192, D), F32)),
        grid_spec=pltpu.PrefetchScalarGridSpec(
            num_scalar_prefetch=1, grid=(1,),
            in_specs=[pl.BlockSpec((D // 8, H), lambda i, J: (J[0], 0)), pl.BlockSpec((H // 8, D), lambda i, J: (J[0], 0)),
                      pl.BlockSpec((D // 4, H), lambda i, J: (J[1], 0)), pl.BlockSpec((H // 4, D), lambda i, J: (J[2], 0)), ANY],
            out_specs=(pl.BlockSpec((192, D), lambda i, J: (0, 0)),) * 3),
        cost_estimate=pl.CostEstimate(flops=1000, bytes_accessed=1000, transcendentals=0),
        compiler_params=pltpu.CompilerParams(vmem_limit_bytes=16 << 20), name="prep_f")(J, w_up, w_down, w_up, w_down, after)


def cat_kernel(*refs):
    for i, v in enumerate(refs[:-1]):
        refs[-1][i] = v[...]


def cat(parts, after=()):
    return pcall(cat_kernel, "cat", [sds((len(parts),) + parts[0].shape, F32)], (), parts, us=1e-5, after=after)[0]


def attend_fwd(nh, full, first, qc, kc, qkv, att):
    hw = 64 * nh
    for h in range(nh):
        flag = first(h)
        for i in range(2):
            j = jnp.where(full, flag if i == 0 else 1 - flag, i)
            rj = pl.ds(pl.multiple_of(j * 512, 512), 512)
            q = qkv[i * 512:(i + 1) * 512, h * 64:(h + 1) * 64] * jnp.asarray(0.125, BF)
            s = dg(q, qkv[rj, hw + h * 64:hw + (h + 1) * 64], NT)
            s = jnp.where((qc[i * 512:(i + 1) * 512, :] ^ flag) == kc[j], s, NEG)
            p = jnp.exp(s - jnp.max(s, axis=1, keepdims=True))
            p = (p * (1.0 / jnp.sum(p, axis=1, keepdims=True))).astype(BF)
            att[i * 512:(i + 1) * 512, h * 64:(h + 1) * 64] = dg(p, qkv[rj, 2 * hw + h * 64:2 * hw + (h + 1) * 64], NN).astype(BF)


def project(x, w, bq, bv, qkv, hw):
    qkv[:, 0:hw] = (dg(x[...], w[0:hw, :], NT) + bq).astype(BF)
    qkv[:, hw:2 * hw] = dg(x[...], w[hw:2 * hw, :], NT).astype(BF)
    qkv[:, 2 * hw:3 * hw] = (dg(x[...], w[2 * hw:3 * hw, :], NT) + bv).astype(BF)


def attn_own_kernel(nh, perm, buck, tok, wq, wo, b_qv, qc, kc, acc, qkv, att):
    hw = 64 * nh
    b = b_qv[...].astype(F32)
    project(tok, wq, b[0:1], b[1:2], qkv, hw)
    attend_fwd(nh, buck[0] == 1024, lambda h: perm[h, 0], qc, kc, qkv, att)
    acc[...] = dg(att[...], wo[...], NN)


def piece_bits(rows):
    return jnp.max(rows[2:3, 0:128]).astype(jnp.int32)


def attn_other_kernel(nh, J, buck, tok, c, o, qc, kc, acc_in, acc, qkv, w, info, att):
    hw = 64 * nh
    for half, part in enumerate((c, o)):
        piece = part
        for r in range(2):
            w[pl.ds(pl.multiple_of((J[1] ^ (half * 2 + r)) * hw, 64), hw), :] = piece[r, 0:hw, :].astype(BF)
    rows = c[0, hw:hw + 8, :]
    info[...] = rows
    project(tok, w, rows[0:1, 0:hw], rows[0:1, hw:2 * hw], qkv, hw)
    bits = piece_bits(rows)
    attend_fwd(nh, buck[0] == 1024, lambda h: (bits >> h) & 1, qc, kc, qkv, att)
    acc[...] = acc_in[...] + dg(att[...], w[3 * hw:4 * hw, :], NN)


def attn_own(nh, perm, buck, tok, wq, wo, b_qv, qc, kc):
    T, D = tok.shape
    hw = 64 * nh
    return pcall(functools.partial(attn_own_kernel, nh), "attn_own",
                 [sds((T, D), F32), sds((T, 3 * hw), BF), sds((T, hw), BF)], [perm, buck],
                 [tok, wq, wo, b_qv, qc, kc], us=1e-5)


def attn_other(nh, J, buck, tok, c, o, qc, kc, acc):
    T, D = tok.shape
    hw = 64 * nh
    return pcall(functools.partial(attn_other_kernel, nh), "attn_other",
                 [sds((T, D), F32), sds((T, 3 * hw), BF), sds((4 * hw, D), BF), sds((8, D), F32)],
                 [J, buck], [tok, c, o, qc, kc, acc], scratch=[pltpu.VMEM((T, hw), BF)], alias={5: 0}, us=1e-5)


def attn_bwd_kernel(nh, own, *refs):
    hw = 64 * nh
    if own:
        t, perm, buck, g, qkv, wq, wo, qcr, kcc, acc_in, dst, acc, cols, datt = refs
        wo = wo
    else:
        t, buck, g, qkv, wq, qcr, kcc, c0, acc_in, acc, dst, datt = refs
        bits = piece_bits(c0[...])
        wo = wq.at[3 * hw:4 * hw]
    datt[...] = dg(g[...], wo[...], NT).astype(BF)
    qkv, wq = qkv, wq.at[0:3 * hw]
    full = buck[0] == 1024
    for h in range(nh):
        flag = perm[h, 0] if own else (bits >> h) & 1
        for i in range(2):
            j = jnp.where(full, flag if i == 0 else 1 - flag, i)
            rj = pl.ds(pl.multiple_of(j * 512, 512), 512)
            q = qkv[i * 512:(i + 1) * 512, h * 64:(h + 1) * 64] * jnp.asarray(0.125, BF)
            kj = qkv[rj, hw + h * 64:hw + (h + 1) * 64]
            vj = qkv[rj, 2 * hw + h * 64:2 * hw + (h + 1) * 64]
            do = datt[i * 512:(i + 1) * 512, h * 64:(h + 1) * 64]
            s = dg(kj, q, NT)
            s = jnp.where((qcr[i] ^ flag) == kcc[rj, :], s, NEG)
            p = jnp.exp(s - jnp.max(s, axis=0, keepdims=True))
            p = p * (1.0 / jnp.sum(p, axis=0, keepdims=True))
            dp = dg(vj, do, NT)
            ds = (p * (dp - jnp.sum(p * dp, axis=0, keepdims=True))).astype(BF)
            dst[rj, 2 * hw + h * 64:2 * hw + (h + 1) * 64] = dg(p.astype(BF), do, NN).astype(BF)
            dst[rj, hw + h * 64:hw + (h + 1) * 64] = dg(ds, q, NN).astype(BF)
            dst[i * 512:(i + 1) * 512, h * 64:(h + 1) * 64] = (dg(ds, kj, TN) * 0.125).astype(BF)
    R = acc.shape[0]
    rows = pl.ds(pl.multiple_of(t[0] * R, R), R)
    y = dg(dst[rows, :], wq[...], NN)
    acc[...] = acc_in[...] + y
    if own:
        cols[...] = jnp.sum(dst[...].astype(F32), axis=0, keepdims=True)


def attn_bwd_own(nh, t, perm, buck, g, wq, wo, qkv, qcr, kcc, acc):
    T, D = g.shape
    hw = 64 * nh
    return pcall(functools.partial(attn_bwd_kernel, nh, True), "attn_bwd_own",
                 [sds((T, 3 * hw), BF), sds(acc.shape, F32), sds((1, 3 * hw), F32)], [t, perm, buck],
                 [g, qkv, wq, wo, qcr, kcc, acc], scratch=[pltpu.VMEM((T, hw), BF)], alias={6: 1})


def attn_bwd_other(nh, t, buck, g, w, qkv, qcr, kcc, c, acc):
    T, D = g.shape
    hw = 64 * nh
    return pcall(functools.partial(attn_bwd_kernel, nh, False), "attn_bwd_other", [sds(acc.shape, F32)], [t, buck],
                 [g, qkv, w, qcr, kcc, c, acc],
                 scratch=[pltpu.VMEM((T, 3 * hw), BF), pltpu.VMEM((T, hw), BF)], alias={6: 0})[0]


ERFC_P = 0.3
ERFC = (0.16919777, 0.17054635, 0.14956615, 0.21002719, -0.08287393, 0.53022837, -0.49656831, 0.47774502, -0.1278686)


def phi_pair(v):
    e = jnp.exp(v * v * -0.5)
    t = 1.0 / (1.0 + jnp.abs(v) * (ERFC_P * 0.7071067811865476))
    a = jnp.full_like(t, ERFC[-1])
    for k in ERFC[-2::-1]:
        a = a * t + k
    tail = 0.5 * (a * t * e)
    return jnp.where(v >= 0, 1.0 - tail, tail), e * 0.3989422804014327


def ffn_rows(h, wu, wd, b, acc_in, acc, gp, act):
    n = 256
    for r in range(h.shape[0] // n):
        rows = slice(r * n, (r + 1) * n)
        up = dg(h[rows, :], wu[...], NN) + b
        big, density = phi_pair(up)
        gp[rows, :] = big + up * density
        a = (up * big).astype(BF)
        if act is not None:
            act[rows, :] = a
        y = dg(a, wd[...], NN)
        acc[rows, :] = y if acc_in is None else acc_in[rows, :] + y


def ffn_own_kernel(h, wu, wd, b, acc, gp, act):
    ffn_rows(h, wu, wd, b[...].astype(F32), None, acc, gp, act)


def ffn_other_kernel(pair, J, h, a0, c, o, acc_in, acc, gp, wu, wd):
    for half, part in enumerate((c, o)):
        piece = part
        for r in range(2 if pair else 4):
            if pair:
                m, u, d = 192, piece[r], piece[2 + r]
                at, ad = J[1] ^ (half * 2 + r), J[2] ^ (half * 2 + r)
            else:
                m, u, d = 96, piece[r, 0:96, :], piece[r, 96:192, :]
                at = ad = J[0] ^ (half * 4 + r)
            wu[pl.ds(pl.multiple_of(at * m, 32), m), :] = u.astype(BF)
            wd[pl.ds(pl.multiple_of(ad * m, 32), m), :] = d.astype(BF)
    ffn_rows(h, wu, wd, a0[1:2, :], acc_in, acc, gp, None)


def ffn_own(h, wu, wd, b):
    T, D = h.shape
    H = wu.shape[1]
    return pcall(ffn_own_kernel, "ffn_own", [sds((T, D), F32), sds((T, H), F32), sds((T, H), BF)],
                 (), [h, wu, wd, b], us=1e-5)


def ffn_other(pair, J, h, a, c, o, acc):
    T, D = h.shape
    H = D
    return pcall(functools.partial(ffn_other_kernel, pair), "ffn_other",
                 [sds((T, D), F32), sds((T, H), F32), sds((D, H), BF), sds((H, D), BF)],
                 [J], [h, a, c, o, acc], alias={4: 0}, us=1e-5)


def ffn_bwd_kernel(own, *refs):
    if own:
        g, wd, gp, wu, acc, up_low, bsum = refs
    else:
        g, wd, gp, wu, acc_in, acc = refs
    n = 256
    bs = None
    for r in range(g.shape[0] // n):
        rows = slice(r * n, (r + 1) * n)
        da = dg(g[rows, :], wd[...], NT)
        du = (da * gp[rows, :]).astype(BF)
        if own:
            up_low[rows, :] = du
            s = jnp.sum(du.astype(F32), axis=0, keepdims=True)
            bs = s if bs is None else bs + s
        y = dg(du, wu[...], NT)
        acc[rows, :] = y if own else acc_in[rows, :] + y
    if own:
        bsum[...] = bs


def ffn_bwd(own, g, wu, wd, gp, acc=None):
    T, D = g.shape
    H = gp.shape[1]
    out = [sds((T, D), F32)]
    if own:
        out += [sds((T, H), BF), sds((1, H), F32)]
    return pcall(functools.partial(ffn_bwd_kernel, own), "ffn_bwd", out, (), [g, wd, gp, wu] + ([] if own else [acc]),
                 alias=None if own else {4: 0}, us=4)


def norm(s):
    center = s - jnp.mean(s, axis=-1, keepdims=True)
    inverse = lax.rsqrt(jnp.mean(center * center, axis=-1, keepdims=True) + LN_EPS)
    return center * inverse, inverse


def norm_back(w, scaled, inverse):
    return inverse * (w - jnp.mean(w, axis=-1, keepdims=True) - scaled * jnp.mean(w * scaled, axis=-1, keepdims=True))


def ln1_kernel(tok, acc, b_out, gain, shift, h_low, scaled, inverse):
    n = 128
    for r in range(tok.shape[0] // n):
        rows = slice(r * n, (r + 1) * n)
        x, inv = norm(tok[rows, :].astype(F32) + acc[rows, :] + b_out[...].astype(F32))
        scaled[rows, :] = x
        inverse[rows, :] = inv
        h_low[rows, :] = (x * gain[...] + shift[...]).astype(BF)


def ln2_kernel(t, scaled, gain1, shift1, acc, b_down, gain2, shift2, gy, out, two, two_low, vec):
    R = out.shape[0]

    def rows_of(rows):
        s = scaled[rows, :] * gain1[...] + shift1[...] + acc[rows, :] + b_down[...].astype(F32)
        x, inv = norm(s)
        g = gy[rows, :].astype(F32)
        return x, g, norm_back(g * gain2[...], x, inv)

    n = 128
    for r in range(gy.shape[0] // n):
        rows = slice(r * n, (r + 1) * n)
        _, _, d = rows_of(rows)
        two[rows, :] = d
        two_low[rows, :] = d.astype(BF)
    tot = [jnp.zeros((1, gy.shape[1]), F32)] * 3
    for r in range(R // n):
        rows = pl.ds(pl.multiple_of(t[0] * R + r * n, n), n)
        x, g, d = rows_of(rows)
        out[r * n:(r + 1) * n, :] = x * gain2[...] + shift2[...]
        for i, v in enumerate((d, g * x, g)):
            tot[i] = tot[i] + jnp.sum(v, axis=0, keepdims=True)
    for i in range(3):
        vec[i:i + 1, :] = tot[i]


def ln1_back_kernel(t, two, acc, scaled, inverse, gain1, vec2, bup, one_low, one_own, vec):
    R = one_own.shape[0]
    n = 128

    def rows_of(rows):
        e = two[rows, :] + acc[rows, :]
        return e, norm_back(e * gain1[...], scaled[rows, :], inverse[rows, :])

    for r in range(two.shape[0] // n):
        rows = slice(r * n, (r + 1) * n)
        one_low[rows, :] = rows_of(rows)[1].astype(BF)
    tot = [jnp.zeros((1, two.shape[1]), F32)] * 3
    for r in range(R // n):
        rows = pl.ds(pl.multiple_of(t[0] * R + r * n, n), n)
        e, d = rows_of(rows)
        one_own[r * n:(r + 1) * n, :] = d
        for i, v in enumerate((d, e * scaled[rows, :], e)):
            tot[i] = tot[i] + jnp.sum(v, axis=0, keepdims=True)
    for i in range(3):
        vec[i:i + 1, :] = tot[i]
    vec[3:6, :] = vec2[0:3, :]
    vec[6:7, :] = bup[...]
    vec[7:8, :] = jnp.zeros_like(bup)


def split_blocks(place, full, keep, give):
    n = full.shape[0] // 8
    for q in range(4):
        for mine, ref in ((0, keep), (1, give)):
            b = ((place[1] ^ q) * 2 + (place[0] ^ mine)) * n
            ref[q * n:(q + 1) * n, :] = full[pl.ds(pl.multiple_of(b, 32), n), :]


def grads_ffn_kernel(place, two_low, act, h_low, up_low, keep, give, full):
    H = act.shape[1]
    full[:, 0:H] = dg(two_low[...], act[...], TN)
    full[:, H:] = dg(h_low[...], up_low[...], TN)
    split_blocks(place, full, keep, give)


def grads_attn_kernel(place, tok, dst, one_low, att, cols, vec, keep, give, full):
    W = dst.shape[1]
    full[:, 0:W] = dg(tok[...], dst[...], TN)
    full[:, W:] = dg(one_low[...], att[...], TN)
    n = full.shape[0] // 2
    split_blocks(place, full, keep, give)
    give[n:n + 8, :] = vec[...]
    give[n + 7:n + 8, 0:W // 3] = cols[:, 0:W // 3]
    give[n + 7:n + 8, W // 3:2 * W // 3] = cols[:, 2 * W // 3:]
    keep[n:n + 8, :] = give[n:n + 8, :]


def stage1_kernel(n, extra, keep, got, sx, sy, rest):
    h = n // 2

    def s(a, b):
        return keep[a:b, :] + got[a:b, :]

    sx[0:h, :] = s(3 * n, 3 * n + h)
    sx[h:n, :] = s(n, n + h)
    sy[0:h, :] = s(3 * n + h, 4 * n)
    sy[h:n, :] = s(2 * n + h, 3 * n)
    rest[0:h, :] = s(n + h, 2 * n)
    rest[h:n, :] = s(2 * n, 2 * n + h)
    rest[n:2 * n, :] = s(0, n)
    if extra:
        v = s(4 * n, 4 * n + 8)
        sx[n:n + 8, :] = v
        rest[2 * n:2 * n + 8, :] = v


def stage2_kernel(n, extra, rest, gx, gy, sx, sy, own):
    h = n // 2
    sx[0:h, :] = rest[0:h, :] + gy[0:h, :]
    sy[0:h, :] = rest[h:n, :] + gx[0:h, :]
    own[0:h, :] = rest[n:n + h, :] + gx[h:n, :]
    own[h:n, :] = rest[n + h:2 * n, :] + gy[h:n, :]
    if extra:
        v = rest[2 * n:2 * n + 8, :] + gx[n:n + 8, :]
        sy[h:h + 8, :] = v
        own[n:n + 8, :] = v


def body(n_dp, n_tp, tokens_in, w_qkv, b_qv, w_out, b_out, gain_one, shift_one, w_up, b_up,
         w_down, b_down, gain_two, shift_two, bucket_len, key_mask, block_perm, grad_output):
    T, D = tokens_in.shape
    nh = block_perm.shape[0]
    hw = w_qkv.shape[2]
    H = w_up.shape[1]
    R = T // n_tp
    d = lax.axis_index("dp").astype(jnp.int32)
    t = lax.axis_index("tensor").astype(jnp.int32)[None]
    core, yx = d & 1, (d >> 1) & 3
    J = jnp.stack([core * 4 + yx, core * 2 + (yx & 1), core * 2 + (yx >> 1)])
    place = jnp.stack([core, yx])

    def swap(b, z):
        return [(i * n_tp + k, (i ^ b) * n_tp + (k ^ z)) for i in range(n_dp) for k in range(n_tp)]

    CORE, X, Y = swap(1, 0), swap(2, 0), swap(4, 0)

    def pp(v, perm):
        return lax.ppermute(v, AXES, perm)

    def row(v):
        return v.reshape(1, -1)

    def tie(v, *first):
        return lax.optimization_barrier((v, first))[0]

    pos = jnp.arange(T, dtype=jnp.int32)
    code = pos >> (lax.population_count(bucket_len[0] - 1) - 1)
    kcode = jnp.where(key_mask == 1, code, -1)
    q_col, q_row = code[:, None], code.reshape(2, 1, T // 2)
    k_col, k_row = kcode[:, None], kcode.reshape(2, 1, T // 2)

    def sync(*v):
        return lax.optimization_barrier(v)

    NEXT = [(i * n_tp + k, i * n_tp + (k + 1) % n_tp) for i in range(n_dp) for k in range(n_tp)]
    PREV = [(i * n_tp + (k + 1) % n_tp, i * n_tp + k) for i in range(n_dp) for k in range(n_tp)]

    def attn(pieces, acc):
        acc, qkv, w, info = attn_other(nh, J, bucket_len, tokens_in, *pieces, q_col, k_row, acc)
        att_saved.append((w, qkv))
        infos.append(info)
        return acc

    def ffn(a0, pieces, acc, pair=False):
        acc, gp, wu, wd = ffn_other(pair, J, h_low, a0, *pieces, acc)
        ffn_saved.append((wu, wd, gp))
        return acc

    wq = jnp.swapaxes(w_qkv, 1, 2).reshape(3 * hw, D)
    a_piece = prep_a(J, block_perm, wq, w_out, b_qv, row(b_up))
    z1 = pp(a_piece, NEXT)
    acc, qkv, attended = attn_own(nh, block_perm, bucket_len, tokens_in, wq, w_out, b_qv, q_col, k_row)
    att_saved, infos = [(wq, w_out, qkv)], []

    z1, acc = sync(z1, acc)
    z2, x1 = pp(z1, NEXT), pp(z1, X)
    f_piece, u_quarter, d_quarter = prep_f(J, w_up, w_down, z1)

    z2, x1, f_piece, u_quarter, d_quarter = sync(z2, x1, f_piece, u_quarter, d_quarter)
    z3, x2 = pp(a_piece, PREV), pp(z2, X)
    m1 = cat((z1, x1))
    acc = attn((m1, pp(m1, CORE)), acc)

    z3, x2, acc = sync(z3, x2, acc)
    x3, f1 = pp(z3, X), pp(f_piece, NEXT)
    m2 = cat((z2, x2))
    acc = attn((m2, pp(m2, CORE)), acc)

    x3, f1, acc = sync(x3, f1, acc)
    fx1, fy1, f2 = pp(f1, X), pp(f1, Y), pp(f1, NEXT)
    m3 = cat((z3, x3))
    acc = attn((m3, pp(m3, CORE)), acc)

    fx1, fy1, f2, acc = sync(fx1, fy1, f2, acc)
    fx2, fy2, zu = pp(f2, X), pp(f2, Y), pp(u_quarter, PREV)
    h_low, scaled_one, inverse_one = pcall(
        ln1_kernel, "ln1", [sds((T, D), BF), sds((T, D), F32), sds((T, 1), F32)], (),
        [tokens_in, acc, row(b_out), row(gain_one), row(shift_one)], us=1e-5)
    acc, gp, act_low = ffn_own(h_low, w_up, w_down, row(b_up))
    ffn_saved = [(w_up, w_down, gp)]

    fx2, fy2, zu, acc = sync(fx2, fy2, zu, acc)
    fd1, fd2, zd = pp(fy1, X), pp(fx2, Y), pp(d_quarter, PREV)

    fd1, fd2, zd = sync(fd1, fd2, zd)
    xu, yd = pp(zu, X), pp(zd, Y)
    g1 = cat((f1, fx1, fy1, fd1))
    k1 = pp(g1, CORE)
    g2 = cat((f2, fx2, fy2, fd2), (k1,))
    k2 = pp(g2, CORE)
    acc = ffn(infos[0], (g1, k1), acc)
    acc = ffn(infos[1], (g2, k2), acc)

    xu, yd, acc = sync(xu, yd, acc)
    g3 = cat((zu, xu, zd, yd))
    acc = ffn(infos[2], (g3, pp(g3, CORE)), acc, pair=True)
    layer_out, two, two_low, vec_two = pcall(
        ln2_kernel, "ln2", [sds((R, D), F32), sds((T, D), F32), sds((T, D), BF), sds((3, D), F32)], [t],
        [scaled_one, row(gain_one), row(shift_one), acc, row(b_down), row(gain_two), row(shift_two), grad_output], us=4)

    fast = n_dp == 8 and n_tp == 4
    n = D // 8

    def stage1(extra, keep, got):
        e = 8 if extra else 0
        W = keep.shape[1]
        sx, sy, rest = pcall(functools.partial(stage1_kernel, n, extra), "stage1",
                             [sds((n + e, W), F32), sds((n, W), F32), sds((2 * n + e, W), F32)], (), [keep, got], us=1)
        return pp(sx, X), pp(sy, Y), rest

    def stage2(extra, rest, gx, gy):
        e = 8 if extra else 0
        W = rest.shape[1]
        sx, sy, own = pcall(functools.partial(stage2_kernel, n, extra), "stage2",
                            [sds((n // 2, W), F32), sds((n // 2 + e, W), F32), sds((n + e, W), F32)], (), [rest, gx, gy], us=1)
        return pp(sx, X), pp(sy, Y), own

    def grads(kernel, W, e, ins, us):
        keep, give = pcall(kernel, "grads", [sds((D // 2 + e, W), F32)] * 2, [place], ins,
                           scratch=[pltpu.VMEM((D, W), F32)], us=us)
        return keep, pp(give, CORE)

    def plus_tp(v, got):
        return jnp.where(jnp.arange(8)[:, None] < 6, v + got, v)

    def bwd_other(k, acc, one_low):
        return attn_bwd_other(nh, t, bucket_len, one_low, *att_saved[k], q_row, k_col, infos[k - 1], acc)

    acc, up_low, grad_b_up = ffn_bwd(True, two_low, *ffn_saved[0])
    if fast:
        keep, got = grads(grads_ffn_kernel, 2 * H, 0, [two_low, act_low, h_low, up_low], 4)
        two_low = tie(two_low, keep)
    for k in range(1, n_tp):
        (acc,) = ffn_bwd(False, two_low, *ffn_saved[k], acc)
    one_low, total, vec = pcall(
        ln1_back_kernel, "ln1_back", [sds((T, D), BF), sds((R, D), F32), sds((8, D), F32)], [t],
        [two, acc, scaled_one, inverse_one, row(gain_one), vec_two, grad_b_up], us=2)
    if fast:
        tv = pp(vec, swap(0, 1))
        gx, gy, rest = stage1(False, keep, tie(got, one_low))
        one_low = tie(one_low, rest)
    g_low, total, cols = attn_bwd_own(nh, t, block_perm, bucket_len, one_low, *att_saved[0], q_row, k_col, total)
    if fast:
        vec = plus_tp(vec, tie(tv, g_low))
        tv = pp(vec, swap(0, 2))
        fx, fy, own_f = stage2(False, rest, tie(gx, g_low), gy)
        vec = plus_tp(vec, tie(tv, own_f))
        keep, got = grads(grads_attn_kernel, 4 * hw, 8, [tokens_in, g_low, one_low, attended, cols, vec], 3)
        one_low = tie(one_low, keep)
        acc = bwd_other(1, total, one_low)
        ax, ay, rest = stage1(True, keep, tie(got, acc))
        one_low = tie(one_low, rest)
        acc = bwd_other(2, acc, one_low)
        sx2, sy2, own_a = stage2(True, rest, tie(ax, acc), ay)
        ax, ay = sx2, sy2
        acc = bwd_other(3, acc, tie(one_low, own_a))
    else:
        acc = total
        for k in range(1, n_tp):
            acc = bwd_other(k, acc, one_low)
    grad_tokens = acc

    if fast:
        h = n // 2
        f = own_f + jnp.concatenate([fy, fx])
        a = own_a[:n] + jnp.concatenate([ay[:h], ax])
        vec = own_a[n:] + ay[h:]
    else:
        def scatter(x, y):
            return lax.psum_scatter(dg(x, y, TN), "dp", scatter_dimension=0, tiled=True)

        f = jnp.concatenate([scatter(two_low, act_low), scatter(h_low, up_low)], axis=1)
        a = jnp.concatenate([scatter(tokens_in, g_low), scatter(one_low, attended)], axis=1)
        vec = lax.psum(jnp.concatenate([lax.psum(vec[:6], "tensor"), vec[6:7], jnp.pad(jnp.concatenate([cols[:, :hw], cols[:, 2 * hw:]], 1), ((0, 0), (0, D - 2 * hw)))]), "dp")
    own_qkv = jnp.swapaxes(a[:, :3 * hw].reshape(-1, 3, hw), 0, 1)
    return (layer_out, grad_tokens, own_qkv, vec[7, :2 * hw].reshape(2, hw), a[:, 3 * hw:].T, vec[0], vec[1], vec[2], f[:, H:],
            vec[6, :H], f[:, :H].T, vec[3], vec[4], vec[5])


def solution(mesh):
    n_dp, n_tp = mesh.shape["dp"], mesh.shape["tensor"]
    in_specs = (
        P("dp", None), P(None, None, "tensor"), P(None, "tensor"), P("tensor", None), P(), P(), P(),
        P(None, "tensor"), P("tensor"), P("tensor", None), P(), P(), P(), P("dp"), P("dp"),
        P("tensor", None), P("dp", None),
    )
    out_specs = (
        P(("dp", "tensor"), None), P(("dp", "tensor"), None), P(None, "dp", "tensor"), P(None, "tensor"),
        P("tensor", "dp"), P(), P(), P(), P("dp", "tensor"), P("tensor"), P("tensor", "dp"), P(), P(), P(),
    )
    return jax.shard_map(functools.partial(body, n_dp, n_tp), mesh=mesh, in_specs=in_specs, out_specs=out_specs, check_vma=False)
```

```python
import functools
import jax
import jax.numpy as jnp
from jax import lax
from jax.experimental import pallas as pl
from jax.experimental.pallas import tpu as pltpu
from jax.sharding import PartitionSpec as P

F32 = jnp.float32
BF = jnp.bfloat16
NT = (((1,), (1,)), ((), ()))
NN = (((1,), (0,)), ((), ()))
TN = (((0,), (0,)), ((), ()))
NEG = -1e30
LN_EPS = 1e-06
AXES = ("dp", "tensor")
VM = pl.BlockSpec(memory_space=pltpu.VMEM)
SM = pl.BlockSpec(memory_space=pltpu.SMEM)
ANY = pl.BlockSpec(memory_space=pl.ANY)


def dg(a, b, dn):
    return lax.dot_general(a, b, dn, preferred_element_type=F32)


def sds(shape, dtype):
    return jax.ShapeDtypeStruct(shape, dtype)


class Far:
    def __init__(self, what, part=None, sends=1, raw=False):
        self.what, self.part, self.sends, self.raw = what, part, sends, raw


class Load:
    def __init__(self, src, buf, sem):
        self.buf, self.copy = buf, pltpu.make_async_copy(src, buf, sem)
        self.copy.start()
        self.here = False

    def get(self):
        if not self.here:
            self.copy.wait()
            self.here = True
        return self.buf


class Store:
    def __init__(self, buf, dst, sems):
        self.buf, self.dst, self.sems, self.out = buf, dst, sems, []

    def send(self, rows=None):
        if rows is None:
            self.put(self.buf, self.dst)
        else:
            self.put(self.buf.at[rows], self.dst.at[rows])

    def put(self, src, dst):
        copy = pltpu.make_async_copy(src, dst, self.sems.at[len(self.out)])
        copy.start()
        self.out.append(copy)


def pcall(fn, name, out, smem, ins, scratch=(), alias=None, vmem=16, us=8, after=()):
    n, m, k, o, c = len(smem), len(ins), len(after), len(out), len(scratch)
    loads = [i for i, v in enumerate(ins) if isinstance(v, Far)]
    stores = [i for i, v in enumerate(out) if isinstance(v, Far)]

    def shape_of(v):
        x = v.what
        if v.part is None:
            return x.shape
        return tuple(p.stop - p.start for p in v.part if isinstance(p, slice)) + x.shape[len(v.part):]

    own = [pltpu.VMEM(shape_of(ins[i]), ins[i].what.dtype) for i in loads]
    bufs = [i for i in stores if not out[i].raw]
    own += [pltpu.VMEM(out[i].what.shape, out[i].what.dtype) for i in bufs]
    own += [pltpu.SemaphoreType.DMA((max(1, len(loads)),))] + [pltpu.SemaphoreType.DMA((out[i].sends,)) for i in stores]

    def run(*refs):
        args, outs = list(refs[:n + m]), list(refs[n + m + k:n + m + k + o])
        tmp, rest = refs[n + m + k + o:n + m + k + o + c], refs[n + m + k + o + c:]
        sems = rest[len(loads) + len(bufs):]
        for q, i in enumerate(loads):
            src = args[n + i] if ins[i].part is None else args[n + i].at[ins[i].part]
            args[n + i] = Load(src, rest[q], sems[0].at[q])
        for q, i in enumerate(stores):
            outs[i] = Store(None if out[i].raw else rest[len(loads) + bufs.index(i)], outs[i], sems[1 + q])
        fn(*args, *outs, *tmp)
        for i in loads:
            args[n + i].get()
        for i in stores:
            for copy in outs[i].out:
                copy.wait()

    hbm = pl.BlockSpec(memory_space=pltpu.HBM)
    return pl.pallas_call(
        run, out_shape=tuple(pltpu.HBM(v.what.shape, v.what.dtype) if isinstance(v, Far) else v for v in out),
        in_specs=[SM] * n + [hbm if isinstance(v, Far) else VM for v in ins] + [ANY] * k,
        out_specs=tuple(hbm if isinstance(v, Far) else VM for v in out),
        input_output_aliases={n + i: q for i, q in (alias or {}).items()}, scratch_shapes=list(scratch) + own,
        cost_estimate=pl.CostEstimate(flops=int(us * 8e8), bytes_accessed=int(us * 2e6), transcendentals=0),
        compiler_params=pltpu.CompilerParams(vmem_limit_bytes=vmem << 20), name=name)(
            *smem, *[pltpu.with_memory_space_constraint(v.what, pltpu.HBM) if isinstance(v, Far) else v for v in ins], *after)


def prep_a_kernel(J, perm, w, wo, b_qv, b_up, a):
    hw = b_qv.shape[1]
    n = w.shape[0]
    own = jnp.broadcast_to(J[1] < 3, w.shape)
    a[0:n, :] = jnp.where(own, w[...].astype(F32), wo[...].astype(F32))
    b = b_qv[...].astype(F32)
    a[n:n + 1, 0:hw] = b[0:1]
    a[n:n + 1, hw:2 * hw] = b[1:2]
    a[n:n + 1, 2 * hw:] = jnp.zeros((1, a.shape[1] - 2 * hw), F32)
    a[n + 1:n + 2, :] = b_up[...].astype(F32)
    bits = perm[0, 0]
    for h in range(1, perm.shape[0]):
        bits = bits + (perm[h, 0] << h)
    a[n + 2:n + 8, :] = jnp.full((6, a.shape[1]), bits.astype(F32))


def prep_a(J, perm, wq, wo, b_qv, b_up):
    D = wq.shape[1]
    hw = wo.shape[0]
    return pl.pallas_call(
        prep_a_kernel, out_shape=sds((hw + 8, D), F32),
        grid_spec=pltpu.PrefetchScalarGridSpec(
            num_scalar_prefetch=2, grid=(1,),
            in_specs=[pl.BlockSpec((hw, D), lambda i, J, p: (jnp.minimum(J[1], 2), 0)),
                      pl.BlockSpec((hw, D), lambda i, J, p: (0, 0)),
                      pl.BlockSpec((2, hw), lambda i, J, p: (0, 0)),
                      pl.BlockSpec((1, D), lambda i, J, p: (0, 0))],
            out_specs=pl.BlockSpec((hw + 8, D), lambda i, J, p: (0, 0))),
        cost_estimate=pl.CostEstimate(flops=1000, bytes_accessed=1000, transcendentals=0),
        compiler_params=pltpu.CompilerParams(vmem_limit_bytes=12 << 20), name="prep_a")(J, perm, wq, wo, b_qv, b_up)


def prep_f_kernel(J, wu, wd, wuq, wdq, after, f, uq, dq):
    f[0:96, :] = wu[...].astype(F32)
    f[96:192, :] = wd[...].astype(F32)
    uq[...] = wuq[...].astype(F32)
    dq[...] = wdq[...].astype(F32)


def prep_f(J, w_up, w_down, after):
    D, H = w_up.shape
    return pl.pallas_call(
        prep_f_kernel, out_shape=(sds((192, D), F32), sds((192, H), F32), sds((192, D), F32)),
        grid_spec=pltpu.PrefetchScalarGridSpec(
            num_scalar_prefetch=1, grid=(1,),
            in_specs=[pl.BlockSpec((D // 8, H), lambda i, J: (J[0], 0)), pl.BlockSpec((H // 8, D), lambda i, J: (J[0], 0)),
                      pl.BlockSpec((D // 4, H), lambda i, J: (J[1], 0)), pl.BlockSpec((H // 4, D), lambda i, J: (J[2], 0)), ANY],
            out_specs=(pl.BlockSpec((192, D), lambda i, J: (0, 0)),) * 3),
        cost_estimate=pl.CostEstimate(flops=1000, bytes_accessed=1000, transcendentals=0),
        compiler_params=pltpu.CompilerParams(vmem_limit_bytes=16 << 20), name="prep_f")(J, w_up, w_down, w_up, w_down, after)


def cat_kernel(*refs):
    for i, v in enumerate(refs[:-1]):
        refs[-1][i] = v[...]


def cat(parts, after=()):
    return pcall(cat_kernel, "cat", [sds((len(parts),) + parts[0].shape, F32)], (), parts, us=1e-5, after=after)[0]


def attend_fwd(nh, full, first, qc, kc, qkv, att):
    hw = 64 * nh
    for h in range(nh):
        flag = first(h)
        for i in range(2):
            j = jnp.where(full, flag if i == 0 else 1 - flag, i)
            rj = pl.ds(pl.multiple_of(j * 512, 512), 512)
            q = qkv[i * 512:(i + 1) * 512, h * 64:(h + 1) * 64] * jnp.asarray(0.125, BF)
            s = dg(q, qkv[rj, hw + h * 64:hw + (h + 1) * 64], NT)
            s = jnp.where((qc[i * 512:(i + 1) * 512, :] ^ flag) == kc[j], s, NEG)
            p = jnp.exp(s - jnp.max(s, axis=1, keepdims=True))
            p = (p * (1.0 / jnp.sum(p, axis=1, keepdims=True))).astype(BF)
            att[i * 512:(i + 1) * 512, h * 64:(h + 1) * 64] = dg(p, qkv[rj, 2 * hw + h * 64:2 * hw + (h + 1) * 64], NN).astype(BF)


def project(x, w, bq, bv, qkv, hw):
    qkv[:, 0:hw] = (dg(x[...], w[0:hw, :], NT) + bq).astype(BF)
    qkv[:, hw:2 * hw] = dg(x[...], w[hw:2 * hw, :], NT).astype(BF)
    qkv[:, 2 * hw:3 * hw] = (dg(x[...], w[2 * hw:3 * hw, :], NT) + bv).astype(BF)


def attn_own_kernel(nh, perm, buck, tok, wq, wo, b_qv, qc, kc, acc, qkv, att):
    hw = 64 * nh
    b = b_qv[...].astype(F32)
    project(tok, wq, b[0:1], b[1:2], qkv.buf, hw)
    qkv.send()
    attend_fwd(nh, buck[0] == 1024, lambda h: perm[h, 0], qc, kc, qkv.buf, att.buf)
    att.send()
    acc[...] = dg(att.buf[...], wo[...], NN)


def piece_bits(rows):
    return jnp.max(rows[2:3, 0:128]).astype(jnp.int32)


def attn_other_kernel(nh, J, buck, tok, c, o, qc, kc, acc_in, acc, qkv, w, info, att):
    hw = 64 * nh
    for half, part in enumerate((c, o)):
        piece = part
        for r in range(2):
            w.buf[pl.ds(pl.multiple_of((J[1] ^ (half * 2 + r)) * hw, 64), hw), :] = piece[r, 0:hw, :].astype(BF)
    w.send()
    rows = c[0, hw:hw + 8, :]
    info[...] = rows
    project(tok, w.buf, rows[0:1, 0:hw], rows[0:1, hw:2 * hw], qkv.buf, hw)
    qkv.send()
    bits = piece_bits(rows)
    attend_fwd(nh, buck[0] == 1024, lambda h: (bits >> h) & 1, qc, kc, qkv.buf, att)
    acc[...] = acc_in[...] + dg(att[...], w.buf[3 * hw:4 * hw, :], NN)


def attn_own(nh, perm, buck, tok, wq, wo, b_qv, qc, kc):
    T, D = tok.shape
    hw = 64 * nh
    return pcall(functools.partial(attn_own_kernel, nh), "attn_own",
                 [sds((T, D), F32), Far(sds((T, 3 * hw), BF)), Far(sds((T, hw), BF))], [perm, buck],
                 [tok, wq, wo, b_qv, qc, kc], us=1e-5)


def attn_other(nh, J, buck, tok, c, o, qc, kc, acc):
    T, D = tok.shape
    hw = 64 * nh
    return pcall(functools.partial(attn_other_kernel, nh), "attn_other",
                 [sds((T, D), F32), Far(sds((T, 3 * hw), BF)), Far(sds((4 * hw, D), BF)), sds((8, D), F32)],
                 [J, buck], [tok, c, o, qc, kc, acc], scratch=[pltpu.VMEM((T, hw), BF)], alias={5: 0}, us=1e-5)


def attn_bwd_kernel(nh, own, *refs):
    hw = 64 * nh
    if own:
        t, perm, buck, g, qkv, wq, wo, qcr, kcc, acc_in, dst, acc, cols, datt = refs
        wo = wo
    else:
        t, buck, g, qkv, wq, qcr, kcc, c0, acc_in, acc, dst, datt = refs
        bits = piece_bits(c0[...])
        wo = wq.at[3 * hw:4 * hw]
    datt[...] = dg(g[...], wo[...], NT).astype(BF)
    qkv, wq = qkv, wq.at[0:3 * hw]
    full = buck[0] == 1024
    for h in range(nh):
        flag = perm[h, 0] if own else (bits >> h) & 1
        for i in range(2):
            j = jnp.where(full, flag if i == 0 else 1 - flag, i)
            rj = pl.ds(pl.multiple_of(j * 512, 512), 512)
            q = qkv[i * 512:(i + 1) * 512, h * 64:(h + 1) * 64] * jnp.asarray(0.125, BF)
            kj = qkv[rj, hw + h * 64:hw + (h + 1) * 64]
            vj = qkv[rj, 2 * hw + h * 64:2 * hw + (h + 1) * 64]
            do = datt[i * 512:(i + 1) * 512, h * 64:(h + 1) * 64]
            s = dg(kj, q, NT)
            s = jnp.where((qcr[i] ^ flag) == kcc[rj, :], s, NEG)
            p = jnp.exp(s - jnp.max(s, axis=0, keepdims=True))
            p = p * (1.0 / jnp.sum(p, axis=0, keepdims=True))
            dp = dg(vj, do, NT)
            ds = (p * (dp - jnp.sum(p * dp, axis=0, keepdims=True))).astype(BF)
            dst[rj, 2 * hw + h * 64:2 * hw + (h + 1) * 64] = dg(p.astype(BF), do, NN).astype(BF)
            dst[rj, hw + h * 64:hw + (h + 1) * 64] = dg(ds, q, NN).astype(BF)
            dst[i * 512:(i + 1) * 512, h * 64:(h + 1) * 64] = (dg(ds, kj, TN) * 0.125).astype(BF)
    R = acc.shape[0]
    rows = pl.ds(pl.multiple_of(t[0] * R, R), R)
    y = dg(dst[rows, :], wq[...], NN)
    acc[...] = acc_in[...] + y
    if own:
        cols[...] = jnp.sum(dst[...].astype(F32), axis=0, keepdims=True)


def attn_bwd_own(nh, t, perm, buck, g, wq, wo, qkv, qcr, kcc, acc):
    T, D = g.shape
    hw = 64 * nh
    return pcall(functools.partial(attn_bwd_kernel, nh, True), "attn_bwd_own",
                 [sds((T, 3 * hw), BF), sds(acc.shape, F32), sds((1, 3 * hw), F32)], [t, perm, buck],
                 [g, qkv, wq, wo, qcr, kcc, acc], scratch=[pltpu.VMEM((T, hw), BF)], alias={6: 1})


def attn_bwd_other(nh, t, buck, g, w, qkv, qcr, kcc, c, acc):
    T, D = g.shape
    hw = 64 * nh
    return pcall(functools.partial(attn_bwd_kernel, nh, False), "attn_bwd_other", [sds(acc.shape, F32)], [t, buck],
                 [g, qkv, w, qcr, kcc, c, acc],
                 scratch=[pltpu.VMEM((T, 3 * hw), BF), pltpu.VMEM((T, hw), BF)], alias={6: 0})[0]


ERFC_P = 0.3
ERFC = (0.16919777, 0.17054635, 0.14956615, 0.21002719, -0.08287393, 0.53022837, -0.49656831, 0.47774502, -0.1278686)


def phi_pair(v):
    e = jnp.exp(v * v * -0.5)
    t = 1.0 / (1.0 + jnp.abs(v) * (ERFC_P * 0.7071067811865476))
    a = jnp.full_like(t, ERFC[-1])
    for k in ERFC[-2::-1]:
        a = a * t + k
    tail = 0.5 * (a * t * e)
    return jnp.where(v >= 0, 1.0 - tail, tail), e * 0.3989422804014327


def ffn_rows(h, wu, wd, b, acc_in, acc, gp, act):
    n = 256
    for r in range(h.shape[0] // n):
        rows = slice(r * n, (r + 1) * n)
        up = dg(h[rows, :], wu[...], NN) + b
        big, density = phi_pair(up)
        gp.buf[rows, :] = big + up * density
        gp.send(rows)
        a = (up * big).astype(BF)
        if act is not None:
            act.buf[rows, :] = a
            act.send(rows)
        y = dg(a, wd[...], NN)
        acc[rows, :] = y if acc_in is None else acc_in[rows, :] + y


def ffn_own_kernel(h, wu, wd, b, acc, gp, act):
    ffn_rows(h, wu, wd, b[...].astype(F32), None, acc, gp, act)


def ffn_other_kernel(pair, J, h, a0, c, o, acc_in, acc, gp, wu, wd):
    for half, part in enumerate((c, o)):
        piece = part
        for r in range(2 if pair else 4):
            if pair:
                m, u, d = 192, piece[r], piece[2 + r]
                at, ad = J[1] ^ (half * 2 + r), J[2] ^ (half * 2 + r)
            else:
                m, u, d = 96, piece[r, 0:96, :], piece[r, 96:192, :]
                at = ad = J[0] ^ (half * 4 + r)
            wu.buf[pl.ds(pl.multiple_of(at * m, 32), m), :] = u.astype(BF)
            wd.buf[pl.ds(pl.multiple_of(ad * m, 32), m), :] = d.astype(BF)
    wu.send()
    wd.send()
    ffn_rows(h, wu.buf, wd.buf, a0[1:2, :], acc_in, acc, gp, None)


def ffn_own(h, wu, wd, b):
    T, D = h.shape
    H = wu.shape[1]
    return pcall(ffn_own_kernel, "ffn_own", [sds((T, D), F32), Far(sds((T, H), F32), sends=T // 256), Far(sds((T, H), BF), sends=T // 256)],
                 (), [h, wu, wd, b], us=1e-5)


def ffn_other(pair, J, h, a, c, o, acc):
    T, D = h.shape
    H = D
    return pcall(functools.partial(ffn_other_kernel, pair), "ffn_other",
                 [sds((T, D), F32), Far(sds((T, H), F32), sends=T // 256), Far(sds((D, H), BF)), Far(sds((H, D), BF))],
                 [J], [h, a, c, o, acc], alias={4: 0}, us=1e-5)


def ffn_bwd_kernel(own, far, *refs):
    if own:
        g, wd, gp, wu, acc, up_low, bsum = refs
    else:
        g, wd, *gps, wu, acc_in, acc = refs
        if far:
            g, wd = g.get(), wd.get()
        else:
            gp = gps[0]
    n = 256
    bs = None
    for r in range(g.shape[0] // n):
        rows = slice(r * n, (r + 1) * n)
        da = dg(g[rows, :], wd[...], NT)
        du = (da * (gps[r].get()[...] if far else gp[rows, :])).astype(BF)
        if own:
            up_low[rows, :] = du
            s = jnp.sum(du.astype(F32), axis=0, keepdims=True)
            bs = s if bs is None else bs + s
        if far and r == 0:
            wu = wu.get()
        y = dg(du, wu[...], NT)
        acc[rows, :] = y if own else acc_in[rows, :] + y
    if own:
        bsum[...] = bs


def ffn_bwd(own, g, wu, wd, gp, acc=None, far=False):
    T, D = g.shape
    H = gp.shape[1]
    gps = [gp]
    if far:
        g, wd, wu = Far(g), Far(wd), Far(wu)
        gps = [Far(gp, (slice(r, r + 256),)) for r in range(0, T, 256)]
    out = [sds((T, D), F32)]
    if own:
        out += [sds((T, H), BF), sds((1, H), F32)]
    return pcall(functools.partial(ffn_bwd_kernel, own, far), "ffn_bwd", out, (), [g, wd, *gps, wu] + ([] if own else [acc]),
                 alias=None if own else {3 + len(gps): 0}, us=4)


def norm(s):
    center = s - jnp.mean(s, axis=-1, keepdims=True)
    inverse = lax.rsqrt(jnp.mean(center * center, axis=-1, keepdims=True) + LN_EPS)
    return center * inverse, inverse


def norm_back(w, scaled, inverse):
    return inverse * (w - jnp.mean(w, axis=-1, keepdims=True) - scaled * jnp.mean(w * scaled, axis=-1, keepdims=True))


def ln1_kernel(tok, acc, b_out, gain, shift, h_low, scaled, inverse):
    n = 128
    for r in range(tok.shape[0] // n):
        rows = slice(r * n, (r + 1) * n)
        x, inv = norm(tok[rows, :].astype(F32) + acc[rows, :] + b_out[...].astype(F32))
        scaled.buf[rows, :] = x
        scaled.send(rows)
        inverse[rows, :] = inv
        h_low[rows, :] = (x * gain[...] + shift[...]).astype(BF)


def ln2_kernel(t, scaled, gain1, shift1, acc, b_down, gain2, shift2, gy, out, two, two_low, vec):
    R = out.shape[0]

    def rows_of(rows):
        s = scaled[rows, :] * gain1[...] + shift1[...] + acc[rows, :] + b_down[...].astype(F32)
        x, inv = norm(s)
        g = gy[rows, :].astype(F32)
        return x, g, norm_back(g * gain2[...], x, inv)

    n = 128
    for r in range(gy.shape[0] // n):
        rows = slice(r * n, (r + 1) * n)
        _, _, d = rows_of(rows)
        two.buf[rows, :] = d
        two.send(rows)
        two_low[rows, :] = d.astype(BF)
    tot = [jnp.zeros((1, gy.shape[1]), F32)] * 3
    for r in range(R // n):
        rows = pl.ds(pl.multiple_of(t[0] * R + r * n, n), n)
        x, g, d = rows_of(rows)
        out[r * n:(r + 1) * n, :] = x * gain2[...] + shift2[...]
        for i, v in enumerate((d, g * x, g)):
            tot[i] = tot[i] + jnp.sum(v, axis=0, keepdims=True)
    for i in range(3):
        vec[i:i + 1, :] = tot[i]


def ln1_back_kernel(t, two, acc, scaled, inverse, gain1, vec2, bup, one_low, one_own, vec):
    R = one_own.shape[0]
    n = 128

    def rows_of(rows):
        e = two[rows, :] + acc[rows, :]
        return e, norm_back(e * gain1[...], scaled[rows, :], inverse[rows, :])

    for r in range(two.shape[0] // n):
        rows = slice(r * n, (r + 1) * n)
        one_low[rows, :] = rows_of(rows)[1].astype(BF)
    tot = [jnp.zeros((1, two.shape[1]), F32)] * 3
    for r in range(R // n):
        rows = pl.ds(pl.multiple_of(t[0] * R + r * n, n), n)
        e, d = rows_of(rows)
        one_own[r * n:(r + 1) * n, :] = d
        for i, v in enumerate((d, e * scaled[rows, :], e)):
            tot[i] = tot[i] + jnp.sum(v, axis=0, keepdims=True)
    for i in range(3):
        vec[i:i + 1, :] = tot[i]
    vec[3:6, :] = vec2[0:3, :]
    vec[6:7, :] = bup[...]
    vec[7:8, :] = jnp.zeros_like(bup)


def split_blocks(place, full, keep, give):
    n = full.shape[0] // 8

    def block(q, mine):
        return pl.ds(pl.multiple_of(((place[1] ^ q) * 2 + (place[0] ^ mine)) * n, 32), n)

    for q in range(4):
        keep[q * n:(q + 1) * n, :] = full[block(q, 0), :]
        give[q * n:(q + 1) * n, :] = full[block(q, 1), :]


def grads_ffn_kernel(place, two_low, act, h_low, up_low, keep, give, full):
    H = act.shape[1]
    full[:, 0:H] = dg(two_low[...], act[...], TN)
    full[:, H:] = dg(h_low[...], up_low[...], TN)
    split_blocks(place, full, keep, give)


def grads_attn_kernel(place, tok, dst, one_low, att, cols, vec, keep, give, full):
    W = dst.shape[1]
    full[:, 0:W] = dg(tok[...], dst[...], TN)
    full[:, W:] = dg(one_low[...], att[...], TN)
    n = full.shape[0] // 2
    split_blocks(place, full, keep, give)
    give[n:n + 8, :] = vec[...]
    give[n + 7:n + 8, 0:W // 3] = cols[:, 0:W // 3]
    give[n + 7:n + 8, W // 3:2 * W // 3] = cols[:, 2 * W // 3:]
    keep[n:n + 8, :] = give[n:n + 8, :]


def stage1_kernel(n, extra, keep, got, sx, sy, rest):
    h = n // 2

    def s(a, b):
        return keep[a:b, :] + got[a:b, :]

    sx[0:h, :] = s(3 * n, 3 * n + h)
    sx[h:n, :] = s(n, n + h)
    sy[0:h, :] = s(3 * n + h, 4 * n)
    sy[h:n, :] = s(2 * n + h, 3 * n)
    rest[0:h, :] = s(n + h, 2 * n)
    rest[h:n, :] = s(2 * n, 2 * n + h)
    rest[n:2 * n, :] = s(0, n)
    if extra:
        v = s(4 * n, 4 * n + 8)
        sx[n:n + 8, :] = v
        rest[2 * n:2 * n + 8, :] = v


def stage2_kernel(n, extra, rest, gx, gy, sx, sy, own):
    h = n // 2
    sx[0:h, :] = rest[0:h, :] + gy[0:h, :]
    sy[0:h, :] = rest[h:n, :] + gx[0:h, :]
    own[0:h, :] = rest[n:n + h, :] + gx[h:n, :]
    own[h:n, :] = rest[n + h:2 * n, :] + gy[h:n, :]
    if extra:
        v = rest[2 * n:2 * n + 8, :] + gx[n:n + 8, :]
        sy[h:h + 8, :] = v
        own[n:n + 8, :] = v


def body(n_dp, n_tp, tokens_in, w_qkv, b_qv, w_out, b_out, gain_one, shift_one, w_up, b_up,
         w_down, b_down, gain_two, shift_two, bucket_len, key_mask, block_perm, grad_output):
    T, D = tokens_in.shape
    nh = block_perm.shape[0]
    hw = w_qkv.shape[2]
    H = w_up.shape[1]
    R = T // n_tp
    d = lax.axis_index("dp").astype(jnp.int32)
    t = lax.axis_index("tensor").astype(jnp.int32)[None]
    core, yx = d & 1, (d >> 1) & 3
    J = jnp.stack([core * 4 + yx, core * 2 + (yx & 1), core * 2 + (yx >> 1)])
    place = jnp.stack([core, yx])

    def swap(b, z):
        return [(i * n_tp + k, (i ^ b) * n_tp + (k ^ z)) for i in range(n_dp) for k in range(n_tp)]

    CORE, X, Y = swap(1, 0), swap(2, 0), swap(4, 0)

    def pp(v, perm):
        return lax.ppermute(v, AXES, perm)

    def row(v):
        return v.reshape(1, -1)

    def tie(v, *first):
        return lax.optimization_barrier((v, first))[0]

    pos = jnp.arange(T, dtype=jnp.int32)
    code = pos >> (lax.population_count(bucket_len[0] - 1) - 1)
    kcode = jnp.where(key_mask == 1, code, -1)
    q_col, q_row = code[:, None], code.reshape(2, 1, T // 2)
    k_col, k_row = kcode[:, None], kcode.reshape(2, 1, T // 2)

    def sync(*v):
        return lax.optimization_barrier(v)

    NEXT = [(i * n_tp + k, i * n_tp + (k + 1) % n_tp) for i in range(n_dp) for k in range(n_tp)]
    PREV = [(i * n_tp + (k + 1) % n_tp, i * n_tp + k) for i in range(n_dp) for k in range(n_tp)]

    def attn(pieces, acc):
        acc, qkv, w, info = attn_other(nh, J, bucket_len, tokens_in, *pieces, q_col, k_row, acc)
        att_saved.append((w, qkv))
        infos.append(info)
        return acc

    def ffn(a0, pieces, acc, pair=False):
        acc, gp, wu, wd = ffn_other(pair, J, h_low, a0, *pieces, acc)
        ffn_saved.append((wu, wd, gp))
        return acc

    wq = jnp.swapaxes(w_qkv, 1, 2).reshape(3 * hw, D)
    a_piece = prep_a(J, block_perm, wq, w_out, b_qv, row(b_up))
    z1 = pp(a_piece, NEXT)
    acc, qkv, attended = attn_own(nh, block_perm, bucket_len, tokens_in, wq, w_out, b_qv, q_col, k_row)
    att_saved, infos = [(wq, w_out, qkv)], []

    z1, acc = sync(z1, acc)
    z2, x1 = pp(z1, NEXT), pp(z1, X)
    f_piece, u_quarter, d_quarter = prep_f(J, w_up, w_down, z1)

    z2, x1, f_piece, u_quarter, d_quarter, k_col = sync(z2, x1, f_piece, u_quarter, d_quarter, k_col)
    z3, x2 = pp(a_piece, PREV), pp(z2, X)
    m1 = cat((z1, x1))
    acc = attn((m1, pp(m1, CORE)), acc)

    z3, x2, acc = sync(z3, x2, acc)
    x3, f1 = pp(z3, X), pp(f_piece, NEXT)
    m2 = cat((z2, x2))
    acc = attn((m2, pp(m2, CORE)), acc)

    x3, f1, acc = sync(x3, f1, acc)
    fx1, fy1, f2 = pp(f1, X), pp(f1, Y), pp(f1, NEXT)
    m3 = cat((z3, x3))
    acc = attn((m3, pp(m3, CORE)), acc)

    fx1, fy1, f2, acc = sync(fx1, fy1, f2, acc)
    fx2, fy2, zu = pp(f2, X), pp(f2, Y), pp(u_quarter, PREV)
    h_low, scaled_one, inverse_one = pcall(
        ln1_kernel, "ln1", [sds((T, D), BF), Far(sds((T, D), F32), sends=T // 128), sds((T, 1), F32)], (),
        [tokens_in, acc, row(b_out), row(gain_one), row(shift_one)], us=1e-5)
    acc, gp, act_low = ffn_own(h_low, w_up, w_down, row(b_up))
    ffn_saved = [(w_up, w_down, gp)]

    fx2, fy2, zu, acc = sync(fx2, fy2, zu, acc)
    fd1, fd2, zd = pp(fy1, X), pp(fx2, Y), pp(d_quarter, PREV)

    fd1, fd2, zd = sync(fd1, fd2, zd)
    xu, yd = pp(zu, X), pp(zd, Y)
    g1 = cat((f1, fx1, fy1, fd1))
    k1 = pp(g1, CORE)
    g2 = cat((f2, fx2, fy2, fd2), (k1,))
    k2 = pp(g2, CORE)
    acc = ffn(infos[0], (g1, k1), acc)
    acc = ffn(infos[1], (g2, k2), acc)

    xu, yd, acc = sync(xu, yd, acc)
    g3 = cat((zu, xu, zd, yd))
    acc = ffn(infos[2], (g3, pp(g3, CORE)), acc, pair=True)
    layer_out, two, two_low, vec_two = pcall(
        ln2_kernel, "ln2", [sds((R, D), F32), Far(sds((T, D), F32), sends=T // 128), sds((T, D), BF), sds((3, D), F32)], [t],
        [scaled_one, row(gain_one), row(shift_one), acc, row(b_down), row(gain_two), row(shift_two), grad_output], us=4)

    fast = n_dp == 8 and n_tp == 4
    n = D // 8

    def stage1(extra, keep, got):
        e = 8 if extra else 0
        W = keep.shape[1]
        sx, sy, rest = pcall(functools.partial(stage1_kernel, n, extra), "stage1",
                             [sds((n + e, W), F32), sds((n, W), F32), sds((2 * n + e, W), F32)], (), [keep, got], us=1)
        return pp(sx, X), pp(sy, Y), rest

    def stage2(extra, rest, gx, gy):
        e = 8 if extra else 0
        W = rest.shape[1]
        sx, sy, own = pcall(functools.partial(stage2_kernel, n, extra), "stage2",
                            [sds((n // 2, W), F32), sds((n // 2 + e, W), F32), sds((n + e, W), F32)], (), [rest, gx, gy], us=1)
        return pp(sx, X), pp(sy, Y), own

    def grads(kernel, W, e, ins, us):
        keep, give = pcall(kernel, "grads", [sds((D // 2 + e, W), F32)] * 2, [place], ins,
                           scratch=[pltpu.VMEM((D, W), F32)], us=us)
        return keep, pp(give, CORE)

    def plus_tp(v, got):
        return jnp.where(jnp.arange(8)[:, None] < 6, v + got, v)

    def bwd_other(k, acc, one_low):
        return attn_bwd_other(nh, t, bucket_len, one_low, *att_saved[k], q_row, k_col, infos[k - 1], acc)

    acc, up_low, grad_b_up = ffn_bwd(True, two_low, *ffn_saved[0])
    if fast:
        keep, got = grads(grads_ffn_kernel, 2 * H, 0, [two_low, act_low, h_low, up_low], 4)
        two_low = tie(two_low, keep)
    for k in range(1, n_tp):
        (acc,) = ffn_bwd(False, two_low, *ffn_saved[k], acc, far=k == 1)
    one_low, total, vec = pcall(
        ln1_back_kernel, "ln1_back", [sds((T, D), BF), sds((R, D), F32), sds((8, D), F32)], [t],
        [two, acc, scaled_one, inverse_one, row(gain_one), vec_two, grad_b_up], us=2)
    if fast:
        tv = pp(vec, swap(0, 1))
        gx, gy, rest = stage1(False, keep, tie(got, one_low))
        one_low = tie(one_low, rest)
    g_low, total, cols = attn_bwd_own(nh, t, block_perm, bucket_len, one_low, *att_saved[0], q_row, k_col, total)
    if fast:
        vec = plus_tp(vec, tie(tv, g_low))
        tv = pp(vec, swap(0, 2))
        fx, fy, own_f = stage2(False, rest, tie(gx, g_low), gy)
        vec = plus_tp(vec, tie(tv, own_f))
        keep, got = grads(grads_attn_kernel, 4 * hw, 8, [tokens_in, g_low, one_low, attended, cols, vec], 3)
        one_low = tie(one_low, keep)
        acc = bwd_other(1, total, one_low)
        ax, ay, rest = stage1(True, keep, tie(got, acc))
        one_low = tie(one_low, rest)
        acc = bwd_other(2, acc, one_low)
        sx2, sy2, own_a = stage2(True, rest, tie(ax, acc), ay)
        ax, ay = sx2, sy2
        acc = bwd_other(3, acc, tie(one_low, own_a))
    else:
        acc = total
        for k in range(1, n_tp):
            acc = bwd_other(k, acc, one_low)
    grad_tokens = acc

    if fast:
        h = n // 2
        f = own_f + jnp.concatenate([fy, fx])
        a = own_a[:n] + jnp.concatenate([ay[:h], ax])
        vec = own_a[n:] + ay[h:]
    else:
        def scatter(x, y):
            return lax.psum_scatter(dg(x, y, TN), "dp", scatter_dimension=0, tiled=True)

        f = jnp.concatenate([scatter(two_low, act_low), scatter(h_low, up_low)], axis=1)
        a = jnp.concatenate([scatter(tokens_in, g_low), scatter(one_low, attended)], axis=1)
        vec = lax.psum(jnp.concatenate([lax.psum(vec[:6], "tensor"), vec[6:7], jnp.pad(jnp.concatenate([cols[:, :hw], cols[:, 2 * hw:]], 1), ((0, 0), (0, D - 2 * hw)))]), "dp")
    own_qkv = jnp.swapaxes(a[:, :3 * hw].reshape(-1, 3, hw), 0, 1)
    return (layer_out, grad_tokens, own_qkv, vec[7, :2 * hw].reshape(2, hw), a[:, 3 * hw:].T, vec[0], vec[1], vec[2], f[:, H:],
            vec[6, :H], f[:, :H].T, vec[3], vec[4], vec[5])


def solution(mesh):
    n_dp, n_tp = mesh.shape["dp"], mesh.shape["tensor"]
    in_specs = (
        P("dp", None), P(None, None, "tensor"), P(None, "tensor"), P("tensor", None), P(), P(), P(),
        P(None, "tensor"), P("tensor"), P("tensor", None), P(), P(), P(), P("dp"), P("dp"),
        P("tensor", None), P("dp", None),
    )
    out_specs = (
        P(("dp", "tensor"), None), P(("dp", "tensor"), None), P(None, "dp", "tensor"), P(None, "tensor"),
        P("tensor", "dp"), P(), P(), P(), P("dp", "tensor"), P("tensor"), P("tensor", "dp"), P(), P(), P(),
    )
    return jax.shard_map(functools.partial(body, n_dp, n_tp), mesh=mesh, in_specs=in_specs, out_specs=out_specs, check_vma=False)
```

```python
import functools
import jax
import jax.numpy as jnp
from jax import lax
from jax.experimental import pallas as pl
from jax.experimental.pallas import tpu as pltpu
from jax.sharding import PartitionSpec as P

F32 = jnp.float32
BF = jnp.bfloat16
NT = (((1,), (1,)), ((), ()))
NN = (((1,), (0,)), ((), ()))
TN = (((0,), (0,)), ((), ()))
NEG = -1e30
LN_EPS = 1e-06
AXES = ("dp", "tensor")
VM = pl.BlockSpec(memory_space=pltpu.VMEM)
SM = pl.BlockSpec(memory_space=pltpu.SMEM)
ANY = pl.BlockSpec(memory_space=pl.ANY)


def dg(a, b, dn):
    return lax.dot_general(a, b, dn, preferred_element_type=F32)


def sds(shape, dtype):
    return jax.ShapeDtypeStruct(shape, dtype)


class Far:
    def __init__(self, what, part=None, sends=1, raw=False):
        self.what, self.part, self.sends, self.raw = what, part, sends, raw


class Load:
    def __init__(self, src, buf, sem):
        self.buf, self.copy = buf, pltpu.make_async_copy(src, buf, sem)
        self.copy.start()
        self.here = False

    def get(self):
        if not self.here:
            self.copy.wait()
            self.here = True
        return self.buf


class Store:
    def __init__(self, buf, dst, sems):
        self.buf, self.dst, self.sems, self.out = buf, dst, sems, []

    def send(self, rows=None):
        if rows is None:
            self.put(self.buf, self.dst)
        else:
            self.put(self.buf.at[rows], self.dst.at[rows])

    def put(self, src, dst):
        copy = pltpu.make_async_copy(src, dst, self.sems.at[len(self.out)])
        copy.start()
        self.out.append(copy)


def pcall(fn, name, out, smem, ins, scratch=(), alias=None, vmem=16, us=8, after=()):
    n, m, k, o, c = len(smem), len(ins), len(after), len(out), len(scratch)
    loads = [i for i, v in enumerate(ins) if isinstance(v, Far)]
    stores = [i for i, v in enumerate(out) if isinstance(v, Far)]

    def shape_of(v):
        x = v.what
        if v.part is None:
            return x.shape
        return tuple(p.stop - p.start for p in v.part if isinstance(p, slice)) + x.shape[len(v.part):]

    own = [pltpu.VMEM(shape_of(ins[i]), ins[i].what.dtype) for i in loads]
    bufs = [i for i in stores if not out[i].raw]
    own += [pltpu.VMEM(out[i].what.shape, out[i].what.dtype) for i in bufs]
    own += [pltpu.SemaphoreType.DMA((max(1, len(loads)),))] + [pltpu.SemaphoreType.DMA((out[i].sends,)) for i in stores]

    def run(*refs):
        args, outs = list(refs[:n + m]), list(refs[n + m + k:n + m + k + o])
        tmp, rest = refs[n + m + k + o:n + m + k + o + c], refs[n + m + k + o + c:]
        sems = rest[len(loads) + len(bufs):]
        for q, i in enumerate(loads):
            src = args[n + i] if ins[i].part is None else args[n + i].at[ins[i].part]
            args[n + i] = Load(src, rest[q], sems[0].at[q])
        for q, i in enumerate(stores):
            outs[i] = Store(None if out[i].raw else rest[len(loads) + bufs.index(i)], outs[i], sems[1 + q])
        fn(*args, *outs, *tmp)
        for i in loads:
            args[n + i].get()
        for i in stores:
            for copy in outs[i].out:
                copy.wait()

    hbm = pl.BlockSpec(memory_space=pltpu.HBM)
    return pl.pallas_call(
        run, out_shape=tuple(pltpu.HBM(v.what.shape, v.what.dtype) if isinstance(v, Far) else v for v in out),
        in_specs=[SM] * n + [hbm if isinstance(v, Far) else VM for v in ins] + [ANY] * k,
        out_specs=tuple(hbm if isinstance(v, Far) else VM for v in out),
        input_output_aliases={n + i: q for i, q in (alias or {}).items()}, scratch_shapes=list(scratch) + own,
        cost_estimate=pl.CostEstimate(flops=int(us * 8e8), bytes_accessed=int(us * 2e6), transcendentals=0),
        compiler_params=pltpu.CompilerParams(vmem_limit_bytes=vmem << 20), name=name)(
            *smem, *[pltpu.with_memory_space_constraint(v.what, pltpu.HBM) if isinstance(v, Far) else v for v in ins], *after)


def prep_a_kernel(J, perm, w, wo, b_qv, b_up, a):
    hw = b_qv.shape[1]
    n = w.shape[0]
    own = jnp.broadcast_to(J[1] < 3, w.shape)
    a[0:n, :] = jnp.where(own, w[...].astype(F32), wo[...].astype(F32))
    b = b_qv[...].astype(F32)
    a[n:n + 1, 0:hw] = b[0:1]
    a[n:n + 1, hw:2 * hw] = b[1:2]
    a[n:n + 1, 2 * hw:] = jnp.zeros((1, a.shape[1] - 2 * hw), F32)
    a[n + 1:n + 2, :] = b_up[...].astype(F32)
    bits = perm[0, 0]
    for h in range(1, perm.shape[1]):
        bits = bits + (perm[0, h] << h)
    a[n + 2:n + 8, :] = jnp.full((6, a.shape[1]), bits.astype(F32))


def prep_a(J, perm, wq, wo, b_qv, b_up):
    D = wq.shape[1]
    hw = wo.shape[0]
    return pl.pallas_call(
        prep_a_kernel, out_shape=sds((hw + 8, D), F32),
        grid_spec=pltpu.PrefetchScalarGridSpec(
            num_scalar_prefetch=2, grid=(1,),
            in_specs=[pl.BlockSpec((hw, D), lambda i, J, p: (jnp.minimum(J[1], 2), 0)),
                      pl.BlockSpec((hw, D), lambda i, J, p: (0, 0)),
                      pl.BlockSpec((2, hw), lambda i, J, p: (0, 0)),
                      pl.BlockSpec((1, D), lambda i, J, p: (0, 0))],
            out_specs=pl.BlockSpec((hw + 8, D), lambda i, J, p: (0, 0))),
        cost_estimate=pl.CostEstimate(flops=1000, bytes_accessed=1000, transcendentals=0),
        compiler_params=pltpu.CompilerParams(vmem_limit_bytes=12 << 20), name="prep_a")(
            J, perm, *[pltpu.with_memory_space_constraint(v, pltpu.HBM) for v in (wq, wo)], b_qv, b_up)


def prep_f_kernel(J, wu, wd, wuq, wdq, after, f, uq, dq):
    f[0:96, :] = wu[...].astype(F32)
    f[96:192, :] = wd[...].astype(F32)
    uq[...] = wuq[...].astype(F32)
    dq[...] = wdq[...].astype(F32)


def prep_f(J, w_up, w_down, after):
    D, H = w_up.shape
    return pl.pallas_call(
        prep_f_kernel, out_shape=(sds((192, D), F32), sds((192, H), F32), sds((192, D), F32)),
        grid_spec=pltpu.PrefetchScalarGridSpec(
            num_scalar_prefetch=1, grid=(1,),
            in_specs=[pl.BlockSpec((D // 8, H), lambda i, J: (J[0], 0)), pl.BlockSpec((H // 8, D), lambda i, J: (J[0], 0)),
                      pl.BlockSpec((D // 4, H), lambda i, J: (J[1], 0)), pl.BlockSpec((H // 4, D), lambda i, J: (J[2], 0)), ANY],
            out_specs=(pl.BlockSpec((192, D), lambda i, J: (0, 0)),) * 3),
        cost_estimate=pl.CostEstimate(flops=1000, bytes_accessed=1000, transcendentals=0),
        compiler_params=pltpu.CompilerParams(vmem_limit_bytes=16 << 20), name="prep_f")(J, w_up, w_down, w_up, w_down, after)


def cat_kernel(*refs):
    for i, v in enumerate(refs[:-1]):
        refs[-1][i] = v[...]


def cat(parts, after=()):
    return pcall(cat_kernel, "cat", [sds((len(parts),) + parts[0].shape, F32)], (), parts, us=1e-5, after=after)[0]


def attend_fwd(nh, full, first, qc, kc, qkv, att):
    hw = 64 * nh
    for h in range(nh):
        flag = first(h)
        for i in range(2):
            j = jnp.where(full, flag if i == 0 else 1 - flag, i)
            rj = pl.ds(pl.multiple_of(j * 512, 512), 512)
            q = qkv[i * 512:(i + 1) * 512, h * 64:(h + 1) * 64] * jnp.asarray(0.125, BF)
            s = dg(q, qkv[rj, hw + h * 64:hw + (h + 1) * 64], NT)
            s = jnp.where((qc[i * 512:(i + 1) * 512, :] ^ flag) == kc[j], s, NEG)
            p = jnp.exp(s - jnp.max(s, axis=1, keepdims=True))
            p = (p * (1.0 / jnp.sum(p, axis=1, keepdims=True))).astype(BF)
            att[i * 512:(i + 1) * 512, h * 64:(h + 1) * 64] = dg(p, qkv[rj, 2 * hw + h * 64:2 * hw + (h + 1) * 64], NN).astype(BF)


def project(x, w, bq, bv, qkv, hw):
    qkv[:, 0:hw] = (dg(x[...], w[0:hw, :], NT) + bq).astype(BF)
    qkv[:, hw:2 * hw] = dg(x[...], w[hw:2 * hw, :], NT).astype(BF)
    qkv[:, 2 * hw:3 * hw] = (dg(x[...], w[2 * hw:3 * hw, :], NT) + bv).astype(BF)


def attn_own_kernel(nh, perm, buck, tok, wq, wo, b_qv, qc, kc, acc, qkv, att):
    hw = 64 * nh
    b = b_qv[...].astype(F32)
    project(tok, wq.get(), b[0:1], b[1:2], qkv.buf, hw)
    qkv.send()
    attend_fwd(nh, buck[0] == 1024, lambda h: perm[0, h], qc, kc, qkv.buf, att.buf)
    att.send()
    acc[...] = dg(att.buf[...], wo.get()[...], NN)


def piece_bits(rows):
    return jnp.max(rows[2:3, 0:128]).astype(jnp.int32)


def attn_other_kernel(nh, J, buck, tok, c, o, qc, kc, acc_in, acc, qkv, w, info, att):
    hw = 64 * nh
    for half, part in enumerate((c, o)):
        piece = part
        for r in range(2):
            w.buf[pl.ds(pl.multiple_of((J[1] ^ (half * 2 + r)) * hw, 64), hw), :] = piece[r, 0:hw, :].astype(BF)
    w.send()
    rows = c[0, hw:hw + 8, :]
    info[...] = rows
    project(tok, w.buf, rows[0:1, 0:hw], rows[0:1, hw:2 * hw], qkv.buf, hw)
    qkv.send()
    bits = piece_bits(rows)
    attend_fwd(nh, buck[0] == 1024, lambda h: (bits >> h) & 1, qc, kc, qkv.buf, att)
    acc[...] = acc_in[...] + dg(att[...], w.buf[3 * hw:4 * hw, :], NN)


def attn_own(nh, perm, buck, tok, wq, wo, b_qv, qc, kc):
    T, D = tok.shape
    hw = 64 * nh
    return pcall(functools.partial(attn_own_kernel, nh), "attn_own",
                 [sds((T, D), F32), Far(sds((T, 3 * hw), BF)), Far(sds((T, hw), BF))], [perm, buck],
                 [tok, Far(wq), Far(wo), b_qv, qc, kc], us=1e-5)


def attn_other(nh, J, buck, tok, c, o, qc, kc, acc):
    T, D = tok.shape
    hw = 64 * nh
    return pcall(functools.partial(attn_other_kernel, nh), "attn_other",
                 [sds((T, D), F32), Far(sds((T, 3 * hw), BF)), Far(sds((4 * hw, D), BF)), sds((8, D), F32)],
                 [J, buck], [tok, c, o, qc, kc, acc], scratch=[pltpu.VMEM((T, hw), BF)], alias={5: 0}, us=1e-5)


def attn_bwd_kernel(nh, own, *refs):
    hw = 64 * nh
    if own:
        t, perm, buck, g, qkv, wq, wo, qcr, kcc, acc_in, dst, acc, cols, datt = refs
        wo = wo
    else:
        t, buck, g, qkv, wq, qcr, kcc, c0, acc_in, acc, dst, datt = refs
        bits = piece_bits(c0[...])
        wo = wq.at[3 * hw:4 * hw]
    datt[...] = dg(g[...], wo[...], NT).astype(BF)
    qkv, wq = qkv, wq.at[0:3 * hw]
    full = buck[0] == 1024
    for h in range(nh):
        flag = perm[0, h] if own else (bits >> h) & 1
        for i in range(2):
            j = jnp.where(full, flag if i == 0 else 1 - flag, i)
            rj = pl.ds(pl.multiple_of(j * 512, 512), 512)
            q = qkv[i * 512:(i + 1) * 512, h * 64:(h + 1) * 64] * jnp.asarray(0.125, BF)
            kj = qkv[rj, hw + h * 64:hw + (h + 1) * 64]
            vj = qkv[rj, 2 * hw + h * 64:2 * hw + (h + 1) * 64]
            do = datt[i * 512:(i + 1) * 512, h * 64:(h + 1) * 64]
            s = dg(kj, q, NT)
            s = jnp.where((qcr[i] ^ flag) == kcc[rj, :], s, NEG)
            p = jnp.exp(s - jnp.max(s, axis=0, keepdims=True))
            p = p * (1.0 / jnp.sum(p, axis=0, keepdims=True))
            dp = dg(vj, do, NT)
            ds = (p * (dp - jnp.sum(p * dp, axis=0, keepdims=True))).astype(BF)
            dst[rj, 2 * hw + h * 64:2 * hw + (h + 1) * 64] = dg(p.astype(BF), do, NN).astype(BF)
            dst[rj, hw + h * 64:hw + (h + 1) * 64] = dg(ds, q, NN).astype(BF)
            dst[i * 512:(i + 1) * 512, h * 64:(h + 1) * 64] = (dg(ds, kj, TN) * 0.125).astype(BF)
    R = acc.shape[0]
    rows = pl.ds(pl.multiple_of(t[0] * R, R), R)
    y = dg(dst[rows, :], wq[...], NN)
    acc[...] = acc_in[...] + y
    if own:
        cols[...] = jnp.sum(dst[...].astype(F32), axis=0, keepdims=True)


def attn_bwd_own(nh, t, perm, buck, g, wq, wo, qkv, qcr, kcc, acc):
    T, D = g.shape
    hw = 64 * nh
    return pcall(functools.partial(attn_bwd_kernel, nh, True), "attn_bwd_own",
                 [sds((T, 3 * hw), BF), sds(acc.shape, F32), sds((1, 3 * hw), F32)], [t, perm, buck],
                 [g, qkv, wq, wo, qcr, kcc, acc], scratch=[pltpu.VMEM((T, hw), BF)], alias={6: 1})


def attn_bwd_other(nh, t, buck, g, w, qkv, qcr, kcc, c, acc):
    T, D = g.shape
    hw = 64 * nh
    return pcall(functools.partial(attn_bwd_kernel, nh, False), "attn_bwd_other", [sds(acc.shape, F32)], [t, buck],
                 [g, qkv, w, qcr, kcc, c, acc],
                 scratch=[pltpu.VMEM((T, 3 * hw), BF), pltpu.VMEM((T, hw), BF)], alias={6: 0})[0]


ERFC_P = 0.3
ERFC = (0.16919777, 0.17054635, 0.14956615, 0.21002719, -0.08287393, 0.53022837, -0.49656831, 0.47774502, -0.1278686)


def phi_pair(v):
    e = jnp.exp(v * v * -0.5)
    t = 1.0 / (1.0 + jnp.abs(v) * (ERFC_P * 0.7071067811865476))
    a = jnp.full_like(t, ERFC[-1])
    for k in ERFC[-2::-1]:
        a = a * t + k
    tail = 0.5 * (a * t * e)
    return jnp.where(v >= 0, 1.0 - tail, tail), e * 0.3989422804014327


def ffn_rows(h, wu, wd, b, acc_in, acc, gp, act):
    n = 256
    for r in range(h.shape[0] // n):
        rows = slice(r * n, (r + 1) * n)
        up = dg(h[rows, :], wu[...], NN) + b
        big, density = phi_pair(up)
        gp.buf[rows, :] = big + up * density
        gp.send(rows)
        a = (up * big).astype(BF)
        if act is not None:
            act.buf[rows, :] = a
            act.send(rows)
        y = dg(a, wd[...], NN)
        acc[rows, :] = y if acc_in is None else acc_in[rows, :] + y


def ffn_own_kernel(h, wu, wd, b, acc, gp, act):
    ffn_rows(h, wu, wd, b[...].astype(F32), None, acc, gp, act)


def ffn_other_kernel(pair, k, J, h, a0, pa, oa, pd, od, acc_in, acc, gp, wu, wd):
    for half, (early, late) in enumerate(((pa, pd), (oa, od))):
        for r in range(2 if pair else 4):
            if pair:
                m, (u, d) = 192, ((early[0], early[1]) if r == 0 else (late[0], late[1]))
                at, ad = J[1] ^ (half * 2 + r), J[2] ^ (half * 2 + r)
            else:
                m, v = 96, early.at[r] if r < 3 else late.at[k]
                u, d = v[0:96, :], v[96:192, :]
                at = ad = J[0] ^ (half * 4 + r)
            wu.buf[pl.ds(pl.multiple_of(at * m, 32), m), :] = u.astype(BF)
            wd.buf[pl.ds(pl.multiple_of(ad * m, 32), m), :] = d.astype(BF)
    wu.send()
    wd.send()
    ffn_rows(h, wu.buf, wd.buf, a0[1:2, :], acc_in, acc, gp, None)


def ffn_own(h, wu, wd, b):
    T, D = h.shape
    H = wu.shape[1]
    return pcall(ffn_own_kernel, "ffn_own", [sds((T, D), F32), Far(sds((T, H), F32), sends=T // 256), Far(sds((T, H), BF), sends=T // 256)],
                 (), [h, wu, wd, b], us=1e-5)


def ffn_other(pair, k, J, h, a0, pieces, acc):
    T, D = h.shape
    H = D
    return pcall(functools.partial(ffn_other_kernel, pair, k), "ffn_other",
                 [sds((T, D), F32), Far(sds((T, H), F32), sends=T // 256), Far(sds((D, H), BF)), Far(sds((H, D), BF))],
                 [J], [h, a0, *pieces, acc], alias={6: 0}, us=1e-5)


def ffn_bwd_kernel(own, far, *refs):
    if own:
        g, wd, gp, wu, acc, up_low, bsum = refs
    else:
        g, wd, *gps, wu, acc_in, acc = refs
        if far:
            g, wd = g.get(), wd.get()
        else:
            gp = gps[0]
    n = 256
    bs = None
    for r in range(g.shape[0] // n):
        rows = slice(r * n, (r + 1) * n)
        da = dg(g[rows, :], wd[...], NT)
        du = (da * (gps[r].get()[...] if far else gp[rows, :])).astype(BF)
        if own:
            up_low[rows, :] = du
            s = jnp.sum(du.astype(F32), axis=0, keepdims=True)
            bs = s if bs is None else bs + s
        if far and r == 0:
            wu = wu.get()
        y = dg(du, wu[...], NT)
        acc[rows, :] = y if own else acc_in[rows, :] + y
    if own:
        bsum[...] = bs


def ffn_bwd(own, g, wu, wd, gp, acc=None, far=False):
    T, D = g.shape
    H = gp.shape[1]
    gps = [gp]
    if far:
        g, wd, wu = Far(g), Far(wd), Far(wu)
        gps = [Far(gp, (slice(r, r + 256),)) for r in range(0, T, 256)]
    out = [sds((T, D), F32)]
    if own:
        out += [sds((T, H), BF), sds((1, H), F32)]
    return pcall(functools.partial(ffn_bwd_kernel, own, far), "ffn_bwd", out, (), [g, wd, *gps, wu] + ([] if own else [acc]),
                 alias=None if own else {3 + len(gps): 0}, us=4)


def norm(s):
    center = s - jnp.mean(s, axis=-1, keepdims=True)
    inverse = lax.rsqrt(jnp.mean(center * center, axis=-1, keepdims=True) + LN_EPS)
    return center * inverse, inverse


def norm_back(w, scaled, inverse):
    return inverse * (w - jnp.mean(w, axis=-1, keepdims=True) - scaled * jnp.mean(w * scaled, axis=-1, keepdims=True))


def ln1_kernel(tok, acc, b_out, gain, shift, h_low, scaled, inverse):
    n = 128
    for r in range(tok.shape[0] // n):
        rows = slice(r * n, (r + 1) * n)
        x, inv = norm(tok[rows, :].astype(F32) + acc[rows, :] + b_out[...].astype(F32))
        scaled.buf[rows, :] = x
        scaled.send(rows)
        inverse[rows, :] = inv
        h_low[rows, :] = (x * gain[...] + shift[...]).astype(BF)


def ln2_kernel(t, scaled, gain1, shift1, acc, b_down, gain2, shift2, gy, out, two, two_low, vec):
    R = out.shape[0]

    def rows_of(rows):
        s = scaled[rows, :] * gain1[...] + shift1[...] + acc[rows, :] + b_down[...].astype(F32)
        x, inv = norm(s)
        g = gy[rows, :].astype(F32)
        return x, g, norm_back(g * gain2[...], x, inv)

    n = 128
    for r in range(gy.shape[0] // n):
        rows = slice(r * n, (r + 1) * n)
        _, _, d = rows_of(rows)
        two.buf[rows, :] = d
        two.send(rows)
        two_low[rows, :] = d.astype(BF)
    tot = [jnp.zeros((1, gy.shape[1]), F32)] * 3
    for r in range(R // n):
        rows = pl.ds(pl.multiple_of(t[0] * R + r * n, n), n)
        x, g, d = rows_of(rows)
        out[r * n:(r + 1) * n, :] = x * gain2[...] + shift2[...]
        for i, v in enumerate((d, g * x, g)):
            tot[i] = tot[i] + jnp.sum(v, axis=0, keepdims=True)
    for i in range(3):
        vec[i:i + 1, :] = tot[i]


def ln1_back_kernel(t, two, acc, scaled, inverse, gain1, vec2, bup, one_low, one_own, vec):
    R = one_own.shape[0]
    n = 128

    def rows_of(rows):
        e = two[rows, :] + acc[rows, :]
        return e, norm_back(e * gain1[...], scaled[rows, :], inverse[rows, :])

    for r in range(two.shape[0] // n):
        rows = slice(r * n, (r + 1) * n)
        one_low[rows, :] = rows_of(rows)[1].astype(BF)
    tot = [jnp.zeros((1, two.shape[1]), F32)] * 3
    for r in range(R // n):
        rows = pl.ds(pl.multiple_of(t[0] * R + r * n, n), n)
        e, d = rows_of(rows)
        one_own[r * n:(r + 1) * n, :] = d
        for i, v in enumerate((d, e * scaled[rows, :], e)):
            tot[i] = tot[i] + jnp.sum(v, axis=0, keepdims=True)
    for i in range(3):
        vec[i:i + 1, :] = tot[i]
    vec[3:6, :] = vec2[0:3, :]
    vec[6:7, :] = bup[...]
    vec[7:8, :] = jnp.zeros_like(bup)


def split_blocks(place, full, keep, give):
    n = full.shape[0] // 8

    def block(q, mine):
        return pl.ds(pl.multiple_of(((place[1] ^ q) * 2 + (place[0] ^ mine)) * n, 32), n)

    for q in range(4):
        keep[q * n:(q + 1) * n, :] = full[block(q, 0), :]
        give[q * n:(q + 1) * n, :] = full[block(q, 1), :]


def grads_ffn_kernel(place, two_low, act, h_low, up_low, keep, give, full):
    H = act.shape[1]
    full[:, 0:H] = dg(two_low[...], act[...], TN)
    full[:, H:] = dg(h_low[...], up_low[...], TN)
    split_blocks(place, full, keep, give)


def grads_attn_kernel(place, tok, dst, one_low, att, cols, vec, keep, give, full):
    W = dst.shape[1]
    full[:, 0:W] = dg(tok[...], dst[...], TN)
    full[:, W:] = dg(one_low[...], att[...], TN)
    n = full.shape[0] // 2
    split_blocks(place, full, keep, give)
    give[n:n + 8, :] = vec[...]
    give[n + 7:n + 8, 0:W // 3] = cols[:, 0:W // 3]
    give[n + 7:n + 8, W // 3:2 * W // 3] = cols[:, 2 * W // 3:]
    keep[n:n + 8, :] = give[n:n + 8, :]


def stage1_kernel(n, extra, keep, got, sx, sy, rest):
    h = n // 2

    def s(a, b):
        return keep[a:b, :] + got[a:b, :]

    sx[0:h, :] = s(3 * n, 3 * n + h)
    sx[h:n, :] = s(n, n + h)
    sy[0:h, :] = s(3 * n + h, 4 * n)
    sy[h:n, :] = s(2 * n + h, 3 * n)
    rest[0:h, :] = s(n + h, 2 * n)
    rest[h:n, :] = s(2 * n, 2 * n + h)
    rest[n:2 * n, :] = s(0, n)
    if extra:
        v = s(4 * n, 4 * n + 8)
        sx[n:n + 8, :] = v
        rest[2 * n:2 * n + 8, :] = v


def stage2_kernel(n, extra, rest, gx, gy, sx, sy, own):
    h = n // 2
    sx[0:h, :] = rest[0:h, :] + gy[0:h, :]
    sy[0:h, :] = rest[h:n, :] + gx[0:h, :]
    own[0:h, :] = rest[n:n + h, :] + gx[h:n, :]
    own[h:n, :] = rest[n + h:2 * n, :] + gy[h:n, :]
    if extra:
        v = rest[2 * n:2 * n + 8, :] + gx[n:n + 8, :]
        sy[h:h + 8, :] = v
        own[n:n + 8, :] = v


def body(n_dp, n_tp, tokens_in, w_qkv, b_qv, w_out, b_out, gain_one, shift_one, w_up, b_up,
         w_down, b_down, gain_two, shift_two, bucket_len, key_mask, block_perm, grad_output):
    T, D = tokens_in.shape
    nh = block_perm.shape[0]
    hw = w_qkv.shape[2]
    H = w_up.shape[1]
    R = T // n_tp
    d = lax.axis_index("dp").astype(jnp.int32)
    t = lax.axis_index("tensor").astype(jnp.int32)[None]
    core, yx = d & 1, (d >> 1) & 3
    J = jnp.stack([core * 4 + yx, core * 2 + (yx & 1), core * 2 + (yx >> 1)])
    place = jnp.stack([core, yx])

    def swap(b, z):
        return [(i * n_tp + k, (i ^ b) * n_tp + (k ^ z)) for i in range(n_dp) for k in range(n_tp)]

    CORE, X, Y = swap(1, 0), swap(2, 0), swap(4, 0)

    def pp(v, perm):
        return lax.ppermute(v, AXES, perm)

    def row(v):
        return v.reshape(1, -1)

    def tie(v, *first):
        return lax.optimization_barrier((v, first))[0]

    pos = jnp.arange(T, dtype=jnp.int32)
    code = pos >> (lax.population_count(bucket_len[0] - 1) - 1)
    kcode = jnp.where(key_mask == 1, code, -1)
    q_col, q_row = code[:, None], code.reshape(2, 1, T // 2)
    k_col, k_row = kcode[:, None], kcode.reshape(2, 1, T // 2)

    def sync(*v):
        return lax.optimization_barrier(v)

    NEXT = [(i * n_tp + k, i * n_tp + (k + 1) % n_tp) for i in range(n_dp) for k in range(n_tp)]
    PREV = [(i * n_tp + (k + 1) % n_tp, i * n_tp + k) for i in range(n_dp) for k in range(n_tp)]

    def attn(pieces, acc):
        acc, qkv, w, info = attn_other(nh, J, bucket_len, tokens_in, *pieces, q_col, k_row, acc)
        att_saved.append((w, qkv))
        infos.append(info)
        return acc

    def ffn(a0, pieces, acc, k=0, pair=False):
        acc, gp, wu, wd = ffn_other(pair, k, J, h_low, a0, pieces, acc)
        ffn_saved.append((wu, wd, gp))
        return acc

    wq = jnp.swapaxes(w_qkv, 1, 2).reshape(3 * hw, D)
    first = block_perm.T
    a_piece = prep_a(J, first, wq, w_out, b_qv, row(b_up))
    z1 = pp(a_piece, NEXT)
    acc, qkv, attended = attn_own(nh, first, bucket_len, tokens_in, wq, w_out, b_qv, q_col, k_row)
    att_saved, infos = [(wq, w_out, qkv)], []

    z1, acc = sync(z1, acc)
    z2, x1 = pp(z1, NEXT), pp(z1, X)
    f_piece, u_quarter, d_quarter = prep_f(J, w_up, w_down, z1)

    z2, x1, f_piece, u_quarter, d_quarter, k_col = sync(z2, x1, f_piece, u_quarter, d_quarter, k_col)
    z3, x2 = pp(a_piece, PREV), pp(z2, X)
    m1 = cat((z1, x1))
    acc = attn((m1, pp(m1, CORE)), acc)

    z3, x2, acc = sync(z3, x2, acc)
    x3, f1 = pp(z3, X), pp(f_piece, NEXT)
    m2 = cat((z2, x2))
    acc = attn((m2, pp(m2, CORE)), acc)

    x3, f1, acc = sync(x3, f1, acc)
    fx1, fy1, f2 = pp(f1, X), pp(f1, Y), pp(f1, NEXT)
    m3 = cat((z3, x3))
    acc = attn((m3, pp(m3, CORE)), acc)

    fx1, fy1, f2, acc = sync(fx1, fy1, f2, acc)
    fx2, fy2, zu = pp(f2, X), pp(f2, Y), pp(u_quarter, PREV)
    h_low, scaled_one, inverse_one = pcall(
        ln1_kernel, "ln1", [sds((T, D), BF), Far(sds((T, D), F32), sends=T // 128), sds((T, 1), F32)], (),
        [tokens_in, acc, row(b_out), row(gain_one), row(shift_one)], us=1e-5)
    acc, gp, act_low = ffn_own(h_low, w_up, w_down, row(b_up))
    ffn_saved = [(w_up, w_down, gp)]

    fx2, fy2, zu, acc = sync(fx2, fy2, zu, acc)
    fd1, fd2, zd = pp(fy1, X), pp(fx2, Y), pp(d_quarter, PREV)
    g1 = cat((f1, fx1, fy1))
    k1 = pp(g1, CORE)
    g2 = cat((f2, fx2, fy2))
    k2 = pp(g2, CORE)

    fd1, fd2, zd = sync(fd1, fd2, zd)
    gd = cat((fd1, fd2))
    kd = pp(gd, CORE)
    xu, yd = pp(zu, X), pp(zd, Y)
    gz = cat((zu, zd))
    kz = pp(gz, CORE)
    acc = ffn(infos[0], (g1, k1, gd, kd), acc)
    acc = ffn(infos[1], (g2, k2, gd, kd), tie(acc, kz), k=1)

    xu, yd, acc = sync(xu, yd, acc)
    gx = cat((xu, yd))
    acc = ffn(infos[2], (gz, kz, gx, pp(gx, CORE)), acc, pair=True)
    layer_out, two, two_low, vec_two = pcall(
        ln2_kernel, "ln2", [sds((R, D), F32), Far(sds((T, D), F32), sends=T // 128), sds((T, D), BF), sds((3, D), F32)], [t],
        [scaled_one, row(gain_one), row(shift_one), acc, row(b_down), row(gain_two), row(shift_two), grad_output], us=4)

    fast = n_dp == 8 and n_tp == 4
    n = D // 8

    def stage1(extra, keep, got):
        e = 8 if extra else 0
        W = keep.shape[1]
        sx, sy, rest = pcall(functools.partial(stage1_kernel, n, extra), "stage1",
                             [sds((n + e, W), F32), sds((n, W), F32), sds((2 * n + e, W), F32)], (), [keep, got], us=1)
        return pp(sx, X), pp(sy, Y), rest

    def stage2(extra, rest, gx, gy):
        e = 8 if extra else 0
        W = rest.shape[1]
        sx, sy, own = pcall(functools.partial(stage2_kernel, n, extra), "stage2",
                            [sds((n // 2, W), F32), sds((n // 2 + e, W), F32), sds((n + e, W), F32)], (), [rest, gx, gy], us=1)
        return pp(sx, X), pp(sy, Y), own

    def grads(kernel, W, e, ins, us):
        keep, give = pcall(kernel, "grads", [sds((D // 2 + e, W), F32)] * 2, [place], ins,
                           scratch=[pltpu.VMEM((D, W), F32)], us=us)
        return keep, pp(give, CORE)

    def plus_tp(v, got):
        return jnp.where(jnp.arange(8)[:, None] < 6, v + got, v)

    def bwd_other(k, acc, one_low):
        return attn_bwd_other(nh, t, bucket_len, one_low, *att_saved[k], q_row, k_col, infos[k - 1], acc)

    acc, up_low, grad_b_up = ffn_bwd(True, two_low, *ffn_saved[0])
    if fast:
        keep, got = grads(grads_ffn_kernel, 2 * H, 0, [two_low, act_low, h_low, up_low], 4)
        two_low = tie(two_low, keep)
    for k in range(1, n_tp):
        (acc,) = ffn_bwd(False, two_low, *ffn_saved[k], acc, far=k == 1)
    one_low, total, vec = pcall(
        ln1_back_kernel, "ln1_back", [sds((T, D), BF), sds((R, D), F32), sds((8, D), F32)], [t],
        [two, acc, scaled_one, inverse_one, row(gain_one), vec_two, grad_b_up], us=2)
    if fast:
        tv = pp(vec, swap(0, 1))
        gx, gy, rest = stage1(False, keep, tie(got, one_low))
        one_low = tie(one_low, rest)
    g_low, total, cols = attn_bwd_own(nh, t, first, bucket_len, one_low, *att_saved[0], q_row, k_col, total)
    if fast:
        vec = plus_tp(vec, tie(tv, g_low))
        tv = pp(vec, swap(0, 2))
        fx, fy, own_f = stage2(False, rest, tie(gx, g_low), gy)
        vec = plus_tp(vec, tie(tv, own_f))
        keep, got = grads(grads_attn_kernel, 4 * hw, 8, [tokens_in, g_low, one_low, attended, cols, vec], 3)
        one_low = tie(one_low, keep)
        acc = bwd_other(1, total, one_low)
        ax, ay, rest = stage1(True, keep, tie(got, acc))
        one_low = tie(one_low, rest)
        acc = bwd_other(2, acc, one_low)
        sx2, sy2, own_a = stage2(True, rest, tie(ax, acc), ay)
        ax, ay = sx2, sy2
        acc = bwd_other(3, acc, tie(one_low, own_a))
    else:
        acc = total
        for k in range(1, n_tp):
            acc = bwd_other(k, acc, one_low)
    grad_tokens = acc

    if fast:
        h = n // 2
        f = own_f + jnp.concatenate([fy, fx])
        a = own_a[:n] + jnp.concatenate([ay[:h], ax])
        vec = own_a[n:] + ay[h:]
    else:
        def scatter(x, y):
            return lax.psum_scatter(dg(x, y, TN), "dp", scatter_dimension=0, tiled=True)

        f = jnp.concatenate([scatter(two_low, act_low), scatter(h_low, up_low)], axis=1)
        a = jnp.concatenate([scatter(tokens_in, g_low), scatter(one_low, attended)], axis=1)
        vec = lax.psum(jnp.concatenate([lax.psum(vec[:6], "tensor"), vec[6:7], jnp.pad(jnp.concatenate([cols[:, :hw], cols[:, 2 * hw:]], 1), ((0, 0), (0, D - 2 * hw)))]), "dp")
    own_qkv = jnp.swapaxes(a[:, :3 * hw].reshape(-1, 3, hw), 0, 1)
    return (layer_out, grad_tokens, own_qkv, vec[7, :2 * hw].reshape(2, hw), a[:, 3 * hw:].T, vec[0], vec[1], vec[2], f[:, H:],
            vec[6, :H], f[:, :H].T, vec[3], vec[4], vec[5])


def solution(mesh):
    n_dp, n_tp = mesh.shape["dp"], mesh.shape["tensor"]
    in_specs = (
        P("dp", None), P(None, None, "tensor"), P(None, "tensor"), P("tensor", None), P(), P(), P(),
        P(None, "tensor"), P("tensor"), P("tensor", None), P(), P(), P(), P("dp"), P("dp"),
        P("tensor", None), P("dp", None),
    )
    out_specs = (
        P(("dp", "tensor"), None), P(("dp", "tensor"), None), P(None, "dp", "tensor"), P(None, "tensor"),
        P("tensor", "dp"), P(), P(), P(), P("dp", "tensor"), P("tensor"), P("tensor", "dp"), P(), P(), P(),
    )
    return jax.shard_map(functools.partial(body, n_dp, n_tp), mesh=mesh, in_specs=in_specs, out_specs=out_specs, check_vma=False)
```

```python
import functools
import jax
import jax.numpy as jnp
from jax import lax
from jax.experimental import pallas as pl
from jax.experimental.pallas import tpu as pltpu
from jax.sharding import PartitionSpec as P

F32 = jnp.float32
BF = jnp.bfloat16
NT = (((1,), (1,)), ((), ()))
NN = (((1,), (0,)), ((), ()))
TN = (((0,), (0,)), ((), ()))
NEG = -1e30
LN_EPS = 1e-06
AXES = ("dp", "tensor")
VM = pl.BlockSpec(memory_space=pltpu.VMEM)
SM = pl.BlockSpec(memory_space=pltpu.SMEM)
ANY = pl.BlockSpec(memory_space=pl.ANY)


def dg(a, b, dn):
    return lax.dot_general(a, b, dn, preferred_element_type=F32)


def sds(shape, dtype):
    return jax.ShapeDtypeStruct(shape, dtype)


class Far:
    def __init__(self, what, part=None, sends=1, raw=False):
        self.what, self.part, self.sends, self.raw = what, part, sends, raw


class Load:
    def __init__(self, src, buf, sem):
        self.buf, self.copy = buf, pltpu.make_async_copy(src, buf, sem)
        self.copy.start()
        self.here = False

    def get(self):
        if not self.here:
            self.copy.wait()
            self.here = True
        return self.buf


class Store:
    def __init__(self, buf, dst, sems):
        self.buf, self.dst, self.sems, self.out = buf, dst, sems, []

    def send(self, rows=None):
        if rows is None:
            self.put(self.buf, self.dst)
        else:
            self.put(self.buf.at[rows], self.dst.at[rows])

    def put(self, src, dst):
        copy = pltpu.make_async_copy(src, dst, self.sems.at[len(self.out)])
        copy.start()
        self.out.append(copy)


def pcall(fn, name, out, smem, ins, scratch=(), alias=None, vmem=16, us=8, after=()):
    n, m, k, o, c = len(smem), len(ins), len(after), len(out), len(scratch)
    loads = [i for i, v in enumerate(ins) if isinstance(v, Far)]
    stores = [i for i, v in enumerate(out) if isinstance(v, Far)]

    def shape_of(v):
        x = v.what
        if v.part is None:
            return x.shape
        return tuple(p.stop - p.start for p in v.part if isinstance(p, slice)) + x.shape[len(v.part):]

    own = [pltpu.VMEM(shape_of(ins[i]), ins[i].what.dtype) for i in loads]
    bufs = [i for i in stores if not out[i].raw]
    own += [pltpu.VMEM(out[i].what.shape, out[i].what.dtype) for i in bufs]
    own += [pltpu.SemaphoreType.DMA((max(1, len(loads)),))] + [pltpu.SemaphoreType.DMA((out[i].sends,)) for i in stores]

    def run(*refs):
        args, outs = list(refs[:n + m]), list(refs[n + m + k:n + m + k + o])
        tmp, rest = refs[n + m + k + o:n + m + k + o + c], refs[n + m + k + o + c:]
        sems = rest[len(loads) + len(bufs):]
        for q, i in enumerate(loads):
            src = args[n + i] if ins[i].part is None else args[n + i].at[ins[i].part]
            args[n + i] = Load(src, rest[q], sems[0].at[q])
        for q, i in enumerate(stores):
            outs[i] = Store(None if out[i].raw else rest[len(loads) + bufs.index(i)], outs[i], sems[1 + q])
        fn(*args, *outs, *tmp)
        for i in loads:
            args[n + i].get()
        for i in stores:
            for copy in outs[i].out:
                copy.wait()

    hbm = pl.BlockSpec(memory_space=pltpu.HBM)
    return pl.pallas_call(
        run, out_shape=tuple(pltpu.HBM(v.what.shape, v.what.dtype) if isinstance(v, Far) else v for v in out),
        in_specs=[SM] * n + [hbm if isinstance(v, Far) else VM for v in ins] + [ANY] * k,
        out_specs=tuple(hbm if isinstance(v, Far) else VM for v in out),
        input_output_aliases={n + i: q for i, q in (alias or {}).items()}, scratch_shapes=list(scratch) + own,
        cost_estimate=pl.CostEstimate(flops=int(us * 8e8), bytes_accessed=int(us * 2e6), transcendentals=0),
        compiler_params=pltpu.CompilerParams(vmem_limit_bytes=vmem << 20), name=name)(
            *smem, *[pltpu.with_memory_space_constraint(v.what, pltpu.HBM) if isinstance(v, Far) else v for v in ins], *after)


def prep_a_kernel(J, perm, w, wo, b_qv, b_up, a):
    hw = b_qv.shape[1]
    n = w.shape[0]
    own = jnp.broadcast_to(J[1] < 3, w.shape)
    a[0:n, :] = jnp.where(own, w[...].astype(F32), wo[...].astype(F32))
    b = b_qv[...].astype(F32)
    a[n:n + 1, 0:hw] = b[0:1]
    a[n:n + 1, hw:2 * hw] = b[1:2]
    a[n:n + 1, 2 * hw:] = jnp.zeros((1, a.shape[1] - 2 * hw), F32)
    a[n + 1:n + 2, :] = b_up[...].astype(F32)
    bits = perm[0, 0]
    for h in range(1, perm.shape[1]):
        bits = bits + (perm[0, h] << h)
    a[n + 2:n + 8, :] = jnp.full((6, a.shape[1]), bits.astype(F32))


def prep_a(J, perm, wq, wo, b_qv, b_up):
    D = wq.shape[1]
    hw = wo.shape[0]
    return pl.pallas_call(
        prep_a_kernel, out_shape=sds((hw + 8, D), F32),
        grid_spec=pltpu.PrefetchScalarGridSpec(
            num_scalar_prefetch=2, grid=(1,),
            in_specs=[pl.BlockSpec((hw, D), lambda i, J, p: (jnp.minimum(J[1], 2), 0)),
                      pl.BlockSpec((hw, D), lambda i, J, p: (0, 0)),
                      pl.BlockSpec((2, hw), lambda i, J, p: (0, 0)),
                      pl.BlockSpec((1, D), lambda i, J, p: (0, 0))],
            out_specs=pl.BlockSpec((hw + 8, D), lambda i, J, p: (0, 0))),
        cost_estimate=pl.CostEstimate(flops=1000, bytes_accessed=1000, transcendentals=0),
        compiler_params=pltpu.CompilerParams(vmem_limit_bytes=12 << 20), name="prep_a")(
            J, perm, *[pltpu.with_memory_space_constraint(v, pltpu.HBM) for v in (wq, wo)], b_qv, b_up)


def prep_f_kernel(J, wu, wd, wuq, wdq, after, f, uq, dq):
    f[0:96, :] = wu[...].astype(F32)
    f[96:192, :] = wd[...].astype(F32)
    uq[...] = wuq[...].astype(F32)
    dq[...] = wdq[...].astype(F32)


def prep_f(J, w_up, w_down, after):
    D, H = w_up.shape
    return pl.pallas_call(
        prep_f_kernel, out_shape=(sds((192, D), F32), sds((192, H), F32), sds((192, D), F32)),
        grid_spec=pltpu.PrefetchScalarGridSpec(
            num_scalar_prefetch=1, grid=(1,),
            in_specs=[pl.BlockSpec((D // 8, H), lambda i, J: (J[0], 0)), pl.BlockSpec((H // 8, D), lambda i, J: (J[0], 0)),
                      pl.BlockSpec((D // 4, H), lambda i, J: (J[1], 0)), pl.BlockSpec((H // 4, D), lambda i, J: (J[2], 0)), ANY],
            out_specs=(pl.BlockSpec((192, D), lambda i, J: (0, 0)),) * 3),
        cost_estimate=pl.CostEstimate(flops=1000, bytes_accessed=1000, transcendentals=0),
        compiler_params=pltpu.CompilerParams(vmem_limit_bytes=16 << 20), name="prep_f")(J, w_up, w_down, w_up, w_down, after)


def cat_kernel(*refs):
    for i, v in enumerate(refs[:-1]):
        refs[-1][i] = v[...]


def cat(parts, after=()):
    return pcall(cat_kernel, "cat", [sds((len(parts),) + parts[0].shape, F32)], (), parts, us=1e-5, after=after)[0]


def attend_fwd(nh, full, first, qc, kc, qkv, att):
    hw = 64 * nh
    for h in range(nh):
        flag = first(h)
        for i in range(2):
            j = jnp.where(full, flag if i == 0 else 1 - flag, i)
            rj = pl.ds(pl.multiple_of(j * 512, 512), 512)
            q = qkv[i * 512:(i + 1) * 512, h * 64:(h + 1) * 64] * jnp.asarray(0.125, BF)
            s = dg(q, qkv[rj, hw + h * 64:hw + (h + 1) * 64], NT)
            s = jnp.where((qc[i * 512:(i + 1) * 512, :] ^ flag) == kc[j], s, NEG)
            p = jnp.exp(s - jnp.max(s, axis=1, keepdims=True))
            p = (p * (1.0 / jnp.sum(p, axis=1, keepdims=True))).astype(BF)
            att[i * 512:(i + 1) * 512, h * 64:(h + 1) * 64] = dg(p, qkv[rj, 2 * hw + h * 64:2 * hw + (h + 1) * 64], NN).astype(BF)


def project(x, w, bq, bv, qkv, hw):
    qkv[:, 0:hw] = (dg(x[...], w[0:hw, :], NT) + bq).astype(BF)
    qkv[:, hw:2 * hw] = dg(x[...], w[hw:2 * hw, :], NT).astype(BF)
    qkv[:, 2 * hw:3 * hw] = (dg(x[...], w[2 * hw:3 * hw, :], NT) + bv).astype(BF)


def attn_own_kernel(nh, perm, buck, tok, wq, wo, b_qv, qc, kc, acc, qkv, att):
    hw = 64 * nh
    b = b_qv[...].astype(F32)
    project(tok, wq.get(), b[0:1], b[1:2], qkv.buf, hw)
    qkv.send()
    attend_fwd(nh, buck[0] == 1024, lambda h: perm[0, h], qc, kc, qkv.buf, att.buf)
    att.send()
    acc[...] = dg(att.buf[...], wo.get()[...], NN)


def piece_bits(rows):
    return jnp.max(rows[2:3, 0:128]).astype(jnp.int32)


def attn_other_kernel(nh, J, buck, tok, c, o, qc, kc, acc_in, acc, qkv, w, info, att):
    hw = 64 * nh
    for half, part in enumerate((c, o)):
        piece = part
        for r in range(2):
            w.buf[pl.ds(pl.multiple_of((J[1] ^ (half * 2 + r)) * hw, 64), hw), :] = piece[r, 0:hw, :].astype(BF)
    w.send()
    rows = c[0, hw:hw + 8, :]
    info[...] = rows
    project(tok, w.buf, rows[0:1, 0:hw], rows[0:1, hw:2 * hw], qkv.buf, hw)
    qkv.send()
    bits = piece_bits(rows)
    attend_fwd(nh, buck[0] == 1024, lambda h: (bits >> h) & 1, qc, kc, qkv.buf, att)
    acc[...] = acc_in[...] + dg(att[...], w.buf[3 * hw:4 * hw, :], NN)


def attn_own(nh, perm, buck, tok, wq, wo, b_qv, qc, kc):
    T, D = tok.shape
    hw = 64 * nh
    return pcall(functools.partial(attn_own_kernel, nh), "attn_own",
                 [sds((T, D), F32), Far(sds((T, 3 * hw), BF)), Far(sds((T, hw), BF))], [perm, buck],
                 [tok, Far(wq), Far(wo), b_qv, qc, kc], us=1e-5)


def attn_other(nh, J, buck, tok, c, o, qc, kc, acc):
    T, D = tok.shape
    hw = 64 * nh
    return pcall(functools.partial(attn_other_kernel, nh), "attn_other",
                 [sds((T, D), F32), Far(sds((T, 3 * hw), BF)), Far(sds((4 * hw, D), BF)), sds((8, D), F32)],
                 [J, buck], [tok, c, o, qc, kc, acc], scratch=[pltpu.VMEM((T, hw), BF)], alias={5: 0}, us=1e-5)


def attn_bwd_kernel(nh, own, *refs):
    hw = 64 * nh
    if own:
        t, perm, buck, g, qkv, wq, wo, qcr, kcc, acc_in, dst, acc, cols, datt = refs
        wo = wo
    else:
        t, buck, g, qkv, wq, qcr, kcc, c0, q_own, acc_in, acc, dst, datt = refs
        bits = piece_bits(c0[...])
        wo = wq.at[3 * hw:4 * hw]
    datt[...] = dg(g[...], wo[...], NT).astype(BF)
    qkv, wq = qkv, wq.at[0:3 * hw]
    full = buck[0] == 1024
    R = acc.shape[0]

    def tile(h, flag, i, for_q, for_kv, ri, codes):
        rj = pl.ds(pl.multiple_of(jnp.where(full, flag ^ i, i) * 512, 512), 512)
        q = qkv[ri, h * 64:(h + 1) * 64] * jnp.asarray(0.125, BF)
        kj = qkv[rj, hw + h * 64:hw + (h + 1) * 64]
        vj = qkv[rj, 2 * hw + h * 64:2 * hw + (h + 1) * 64]
        do = datt[ri, h * 64:(h + 1) * 64]
        s = dg(kj, q, NT)
        s = jnp.where((codes ^ flag) == kcc[rj, :], s, NEG)
        p = jnp.exp(s - jnp.max(s, axis=0, keepdims=True))
        p = p * (1.0 / jnp.sum(p, axis=0, keepdims=True))
        dp = dg(vj, do, NT)
        ds = (p * (dp - jnp.sum(p * dp, axis=0, keepdims=True))).astype(BF)
        if for_kv:
            dst[rj, 2 * hw + h * 64:2 * hw + (h + 1) * 64] = dg(p.astype(BF), do, NN).astype(BF)
            dst[rj, hw + h * 64:hw + (h + 1) * 64] = dg(ds, q, NN).astype(BF)
        if for_q:
            dst[ri, h * 64:(h + 1) * 64] = (dg(ds, kj, TN) * 0.125).astype(BF)

    flags = [perm[0, h] if own else (bits >> h) & 1 for h in range(nh)]
    def whole(h, i, for_q):
        tile(h, flags[h], i, for_q, True, pl.ds(pl.multiple_of(i * 512, 512), 512), qcr[i])

    if own:
        for h in range(nh):
            for i in range(2):
                whole(h, jnp.int32(i), True)
    else:
        half = (t[0] * R) // 512

        def apart(h):
            tile(h, flags[h], half, True, False, pl.ds(pl.multiple_of(t[0] * R, R), R), q_own[...])
            whole(h, 1 - half, False)

        for h in range(nh):
            crossed = jnp.logical_and(full, flags[h] == 1)
            pl.when(jnp.logical_not(crossed))(functools.partial(whole, h, half, True))
            pl.when(crossed)(functools.partial(apart, h))
    rows = pl.ds(pl.multiple_of(t[0] * R, R), R)
    y = dg(dst[rows, :], wq[...], NN)
    acc[...] = acc_in[...] + y
    if own:
        cols[...] = jnp.sum(dst[...].astype(F32), axis=0, keepdims=True)


def attn_bwd_own(nh, t, perm, buck, g, wq, wo, qkv, qcr, kcc, acc):
    T, D = g.shape
    hw = 64 * nh
    return pcall(functools.partial(attn_bwd_kernel, nh, True), "attn_bwd_own",
                 [sds((T, 3 * hw), BF), sds(acc.shape, F32), sds((1, 3 * hw), F32)], [t, perm, buck],
                 [g, qkv, wq, wo, qcr, kcc, acc], scratch=[pltpu.VMEM((T, hw), BF)], alias={6: 1})


def attn_bwd_other(nh, t, buck, g, w, qkv, qcr, kcc, c, q_own, acc):
    T, D = g.shape
    hw = 64 * nh
    return pcall(functools.partial(attn_bwd_kernel, nh, False), "attn_bwd_other", [sds(acc.shape, F32)], [t, buck],
                 [g, qkv, w, qcr, kcc, c, q_own, acc],
                 scratch=[pltpu.VMEM((T, 3 * hw), BF), pltpu.VMEM((T, hw), BF)], alias={7: 0})[0]


ERFC_P = 0.3
ERFC = (0.16919777, 0.17054635, 0.14956615, 0.21002719, -0.08287393, 0.53022837, -0.49656831, 0.47774502, -0.1278686)


def phi_pair(v):
    e = jnp.exp(v * v * -0.5)
    t = 1.0 / (1.0 + jnp.abs(v) * (ERFC_P * 0.7071067811865476))
    a = jnp.full_like(t, ERFC[-1])
    for k in ERFC[-2::-1]:
        a = a * t + k
    tail = 0.5 * (a * t * e)
    return jnp.where(v >= 0, 1.0 - tail, tail), e * 0.3989422804014327


def ffn_rows(h, wu, wd, b, acc_in, acc, gp, act):
    n = 256
    for r in range(h.shape[0] // n):
        rows = slice(r * n, (r + 1) * n)
        up = dg(h[rows, :], wu[...], NN) + b
        big, density = phi_pair(up)
        gp.buf[rows, :] = big + up * density
        gp.send(rows)
        a = (up * big).astype(BF)
        if act is not None:
            act.buf[rows, :] = a
            act.send(rows)
        y = dg(a, wd[...], NN)
        acc[rows, :] = y if acc_in is None else acc_in[rows, :] + y


def ffn_own_kernel(h, wu, wd, b, acc, gp, act):
    ffn_rows(h, wu, wd, b[...].astype(F32), None, acc, gp, act)


def ffn_other_kernel(pair, k, J, h, a0, pa, oa, pd, od, acc_in, acc, gp, wu, wd):
    for half, (early, late) in enumerate(((pa, pd), (oa, od))):
        for r in range(2 if pair else 4):
            if pair:
                m, (u, d) = 192, ((early[0], early[1]) if r == 0 else (late[0], late[1]))
                at, ad = J[1] ^ (half * 2 + r), J[2] ^ (half * 2 + r)
            else:
                m, v = 96, early.at[r] if r < 3 else late.at[k]
                u, d = v[0:96, :], v[96:192, :]
                at = ad = J[0] ^ (half * 4 + r)
            wu.buf[pl.ds(pl.multiple_of(at * m, 32), m), :] = u.astype(BF)
            wd.buf[pl.ds(pl.multiple_of(ad * m, 32), m), :] = d.astype(BF)
    wu.send()
    wd.send()
    ffn_rows(h, wu.buf, wd.buf, a0[1:2, :], acc_in, acc, gp, None)


def ffn_own(h, wu, wd, b):
    T, D = h.shape
    H = wu.shape[1]
    return pcall(ffn_own_kernel, "ffn_own", [sds((T, D), F32), Far(sds((T, H), F32), sends=T // 256), Far(sds((T, H), BF), sends=T // 256)],
                 (), [h, wu, wd, b], us=1e-5)


def ffn_other(pair, k, J, h, a0, pieces, acc):
    T, D = h.shape
    H = D
    return pcall(functools.partial(ffn_other_kernel, pair, k), "ffn_other",
                 [sds((T, D), F32), Far(sds((T, H), F32), sends=T // 256), Far(sds((D, H), BF)), Far(sds((H, D), BF))],
                 [J], [h, a0, *pieces, acc], alias={6: 0}, us=1e-5)


def ffn_bwd_kernel(own, far, *refs):
    if own:
        g, wd, gp, wu, acc, up_low, bsum = refs
    else:
        g, wd, *gps, wu, acc_in, acc = refs
        if far:
            g, wd = g.get(), wd.get()
        else:
            gp = gps[0]
    n = 256
    bs = None
    for r in range(g.shape[0] // n):
        rows = slice(r * n, (r + 1) * n)
        da = dg(g[rows, :], wd[...], NT)
        du = (da * (gps[r].get()[...] if far else gp[rows, :])).astype(BF)
        if own:
            up_low[rows, :] = du
            s = jnp.sum(du.astype(F32), axis=0, keepdims=True)
            bs = s if bs is None else bs + s
        if far and r == 0:
            wu = wu.get()
        y = dg(du, wu[...], NT)
        acc[rows, :] = y if own else acc_in[rows, :] + y
    if own:
        bsum[...] = bs


def ffn_bwd(own, g, wu, wd, gp, acc=None, far=False):
    T, D = g.shape
    H = gp.shape[1]
    gps = [gp]
    if far:
        g, wd, wu = Far(g), Far(wd), Far(wu)
        gps = [Far(gp, (slice(r, r + 256),)) for r in range(0, T, 256)]
    out = [sds((T, D), F32)]
    if own:
        out += [sds((T, H), BF), sds((1, H), F32)]
    return pcall(functools.partial(ffn_bwd_kernel, own, far), "ffn_bwd", out, (), [g, wd, *gps, wu] + ([] if own else [acc]),
                 alias=None if own else {3 + len(gps): 0}, us=4)


def norm(s):
    center = s - jnp.mean(s, axis=-1, keepdims=True)
    inverse = lax.rsqrt(jnp.mean(center * center, axis=-1, keepdims=True) + LN_EPS)
    return center * inverse, inverse


def norm_back(w, scaled, inverse):
    return inverse * (w - jnp.mean(w, axis=-1, keepdims=True) - scaled * jnp.mean(w * scaled, axis=-1, keepdims=True))


def ln1_kernel(tok, acc, b_out, gain, shift, h_low, scaled, inverse):
    n = 128
    for r in range(tok.shape[0] // n):
        rows = slice(r * n, (r + 1) * n)
        x, inv = norm(tok[rows, :].astype(F32) + acc[rows, :] + b_out[...].astype(F32))
        scaled.buf[rows, :] = x
        scaled.send(rows)
        inverse[rows, :] = inv
        h_low[rows, :] = (x * gain[...] + shift[...]).astype(BF)


def ln2_kernel(t, scaled, gain1, shift1, acc, b_down, gain2, shift2, gy, out, two, two_low, vec):
    R = out.shape[0]

    def rows_of(rows):
        s = scaled[rows, :] * gain1[...] + shift1[...] + acc[rows, :] + b_down[...].astype(F32)
        x, inv = norm(s)
        g = gy[rows, :].astype(F32)
        return x, g, norm_back(g * gain2[...], x, inv)

    n = 128
    for r in range(gy.shape[0] // n):
        rows = slice(r * n, (r + 1) * n)
        _, _, d = rows_of(rows)
        two.buf[rows, :] = d
        two.send(rows)
        two_low[rows, :] = d.astype(BF)
    tot = [jnp.zeros((1, gy.shape[1]), F32)] * 3
    for r in range(R // n):
        rows = pl.ds(pl.multiple_of(t[0] * R + r * n, n), n)
        x, g, d = rows_of(rows)
        out[r * n:(r + 1) * n, :] = x * gain2[...] + shift2[...]
        for i, v in enumerate((d, g * x, g)):
            tot[i] = tot[i] + jnp.sum(v, axis=0, keepdims=True)
    for i in range(3):
        vec[i:i + 1, :] = tot[i]


def ln1_back_kernel(t, two, acc, scaled, inverse, gain1, vec2, bup, one_low, one_own, vec):
    R = one_own.shape[0]
    n = 128

    def rows_of(rows):
        e = two[rows, :] + acc[rows, :]
        return e, norm_back(e * gain1[...], scaled[rows, :], inverse[rows, :])

    for r in range(two.shape[0] // n):
        rows = slice(r * n, (r + 1) * n)
        one_low[rows, :] = rows_of(rows)[1].astype(BF)
    tot = [jnp.zeros((1, two.shape[1]), F32)] * 3
    for r in range(R // n):
        rows = pl.ds(pl.multiple_of(t[0] * R + r * n, n), n)
        e, d = rows_of(rows)
        one_own[r * n:(r + 1) * n, :] = d
        for i, v in enumerate((d, e * scaled[rows, :], e)):
            tot[i] = tot[i] + jnp.sum(v, axis=0, keepdims=True)
    for i in range(3):
        vec[i:i + 1, :] = tot[i]
    vec[3:6, :] = vec2[0:3, :]
    vec[6:7, :] = bup[...]
    vec[7:8, :] = jnp.zeros_like(bup)


def split_blocks(place, full, keep, give):
    n = full.shape[0] // 8

    def block(q, mine):
        return pl.ds(pl.multiple_of(((place[1] ^ q) * 2 + (place[0] ^ mine)) * n, 32), n)

    for q in range(4):
        keep[q * n:(q + 1) * n, :] = full[block(q, 0), :]
        give[q * n:(q + 1) * n, :] = full[block(q, 1), :]


def grads_ffn_kernel(place, two_low, act, h_low, up_low, keep, give, full):
    H = act.shape[1]
    full[:, 0:H] = dg(two_low[...], act[...], TN)
    full[:, H:] = dg(h_low[...], up_low[...], TN)
    split_blocks(place, full, keep, give)


def grads_attn_kernel(place, tok, dst, one_low, att, cols, vec, keep, give, full):
    W = dst.shape[1]
    full[:, 0:W] = dg(tok[...], dst[...], TN)
    full[:, W:] = dg(one_low[...], att[...], TN)
    n = full.shape[0] // 2
    split_blocks(place, full, keep, give)
    give[n:n + 8, :] = vec[...]
    give[n + 7:n + 8, 0:W // 3] = cols[:, 0:W // 3]
    give[n + 7:n + 8, W // 3:2 * W // 3] = cols[:, 2 * W // 3:]
    keep[n:n + 8, :] = give[n:n + 8, :]


def stage1_kernel(n, extra, keep, got, sx, sy, rest):
    h = n // 2

    def s(a, b):
        return keep[a:b, :] + got[a:b, :]

    sx[0:h, :] = s(3 * n, 3 * n + h)
    sx[h:n, :] = s(n, n + h)
    sy[0:h, :] = s(3 * n + h, 4 * n)
    sy[h:n, :] = s(2 * n + h, 3 * n)
    rest[0:h, :] = s(n + h, 2 * n)
    rest[h:n, :] = s(2 * n, 2 * n + h)
    rest[n:2 * n, :] = s(0, n)
    if extra:
        v = s(4 * n, 4 * n + 8)
        sx[n:n + 8, :] = v
        rest[2 * n:2 * n + 8, :] = v


def stage2_kernel(n, extra, rest, gx, gy, sx, sy, own):
    h = n // 2
    sx[0:h, :] = rest[0:h, :] + gy[0:h, :]
    sy[0:h, :] = rest[h:n, :] + gx[0:h, :]
    own[0:h, :] = rest[n:n + h, :] + gx[h:n, :]
    own[h:n, :] = rest[n + h:2 * n, :] + gy[h:n, :]
    if extra:
        v = rest[2 * n:2 * n + 8, :] + gx[n:n + 8, :]
        sy[h:h + 8, :] = v
        own[n:n + 8, :] = v


def body(n_dp, n_tp, tokens_in, w_qkv, b_qv, w_out, b_out, gain_one, shift_one, w_up, b_up,
         w_down, b_down, gain_two, shift_two, bucket_len, key_mask, block_perm, grad_output):
    T, D = tokens_in.shape
    nh = block_perm.shape[0]
    hw = w_qkv.shape[2]
    H = w_up.shape[1]
    R = T // n_tp
    d = lax.axis_index("dp").astype(jnp.int32)
    t = lax.axis_index("tensor").astype(jnp.int32)[None]
    core, yx = d & 1, (d >> 1) & 3
    J = jnp.stack([core * 4 + yx, core * 2 + (yx & 1), core * 2 + (yx >> 1)])
    place = jnp.stack([core, yx])

    def swap(b, z):
        return [(i * n_tp + k, (i ^ b) * n_tp + (k ^ z)) for i in range(n_dp) for k in range(n_tp)]

    CORE, X, Y = swap(1, 0), swap(2, 0), swap(4, 0)

    def pp(v, perm):
        return lax.ppermute(v, AXES, perm)

    def row(v):
        return v.reshape(1, -1)

    def tie(v, *first):
        return lax.optimization_barrier((v, first))[0]

    pos = jnp.arange(T, dtype=jnp.int32)
    code = pos >> (lax.population_count(bucket_len[0] - 1) - 1)
    kcode = jnp.where(key_mask == 1, code, -1)
    q_col, q_row = code[:, None], code.reshape(2, 1, T // 2)
    k_col, k_row = kcode[:, None], kcode.reshape(2, 1, T // 2)
    q_own = lax.dynamic_slice_in_dim(code, t[0] * R, R)[None]

    def sync(*v):
        return lax.optimization_barrier(v)

    NEXT = [(i * n_tp + k, i * n_tp + (k + 1) % n_tp) for i in range(n_dp) for k in range(n_tp)]
    PREV = [(i * n_tp + (k + 1) % n_tp, i * n_tp + k) for i in range(n_dp) for k in range(n_tp)]

    def attn(pieces, acc):
        acc, qkv, w, info = attn_other(nh, J, bucket_len, tokens_in, *pieces, q_col, k_row, acc)
        att_saved.append((w, qkv))
        infos.append(info)
        return acc

    def ffn(a0, pieces, acc, k=0, pair=False):
        acc, gp, wu, wd = ffn_other(pair, k, J, h_low, a0, pieces, acc)
        ffn_saved.append((wu, wd, gp))
        return acc

    wq = jnp.swapaxes(w_qkv, 1, 2).reshape(3 * hw, D)
    first = block_perm.T
    a_piece = prep_a(J, first, wq, w_out, b_qv, row(b_up))
    z1 = pp(a_piece, NEXT)
    acc, qkv, attended = attn_own(nh, first, bucket_len, tokens_in, wq, w_out, b_qv, q_col, k_row)
    att_saved, infos = [(wq, w_out, qkv)], []

    z1, acc = sync(z1, acc)
    z2, x1 = pp(z1, NEXT), pp(z1, X)
    f_piece, u_quarter, d_quarter = prep_f(J, w_up, w_down, z1)

    z2, x1, f_piece, u_quarter, d_quarter, k_col = sync(z2, x1, f_piece, u_quarter, d_quarter, k_col)
    z3, x2 = pp(a_piece, PREV), pp(z2, X)
    m1 = cat((z1, x1))
    acc = attn((m1, pp(m1, CORE)), acc)

    z3, x2, acc = sync(z3, x2, acc)
    x3, f1 = pp(z3, X), pp(f_piece, NEXT)
    m2 = cat((z2, x2))
    acc = attn((m2, pp(m2, CORE)), acc)

    x3, f1, acc = sync(x3, f1, acc)
    fx1, fy1, f2 = pp(f1, X), pp(f1, Y), pp(f1, NEXT)
    m3 = cat((z3, x3))
    acc = attn((m3, pp(m3, CORE)), acc)

    fx1, fy1, f2, acc = sync(fx1, fy1, f2, acc)
    fx2, fy2, zu = pp(f2, X), pp(f2, Y), pp(u_quarter, PREV)
    h_low, scaled_one, inverse_one = pcall(
        ln1_kernel, "ln1", [sds((T, D), BF), Far(sds((T, D), F32), sends=T // 128), sds((T, 1), F32)], (),
        [tokens_in, acc, row(b_out), row(gain_one), row(shift_one)], us=1e-5)
    acc, gp, act_low = ffn_own(h_low, w_up, w_down, row(b_up))
    ffn_saved = [(w_up, w_down, gp)]

    fx2, fy2, zu, acc = sync(fx2, fy2, zu, acc)
    fd1, fd2, zd = pp(fy1, X), pp(fx2, Y), pp(d_quarter, PREV)
    g1 = cat((f1, fx1, fy1))
    k1 = pp(g1, CORE)
    g2 = cat((f2, fx2, fy2))
    k2 = pp(g2, CORE)

    fd1, fd2, zd = sync(fd1, fd2, zd)
    gd = cat((fd1, fd2))
    kd = pp(gd, CORE)
    xu, yd = pp(zu, X), pp(zd, Y)
    gz = cat((zu, zd))
    kz = pp(gz, CORE)
    acc = ffn(infos[0], (g1, k1, gd, kd), acc)
    acc = ffn(infos[1], (g2, k2, gd, kd), tie(acc, kz), k=1)

    xu, yd, acc = sync(xu, yd, acc)
    gx = cat((xu, yd))
    acc = ffn(infos[2], (gz, kz, gx, pp(gx, CORE)), acc, pair=True)
    layer_out, two, two_low, vec_two = pcall(
        ln2_kernel, "ln2", [sds((R, D), F32), Far(sds((T, D), F32), sends=T // 128), sds((T, D), BF), sds((3, D), F32)], [t],
        [scaled_one, row(gain_one), row(shift_one), acc, row(b_down), row(gain_two), row(shift_two), grad_output], us=4)

    fast = n_dp == 8 and n_tp == 4
    n = D // 8

    def stage1(extra, keep, got):
        e = 8 if extra else 0
        W = keep.shape[1]
        sx, sy, rest = pcall(functools.partial(stage1_kernel, n, extra), "stage1",
                             [sds((n + e, W), F32), sds((n, W), F32), sds((2 * n + e, W), F32)], (), [keep, got], us=1)
        return pp(sx, X), pp(sy, Y), rest

    def stage2(extra, rest, gx, gy):
        e = 8 if extra else 0
        W = rest.shape[1]
        sx, sy, own = pcall(functools.partial(stage2_kernel, n, extra), "stage2",
                            [sds((n // 2, W), F32), sds((n // 2 + e, W), F32), sds((n + e, W), F32)], (), [rest, gx, gy], us=1)
        return pp(sx, X), pp(sy, Y), own

    def grads(kernel, W, e, ins, us):
        keep, give = pcall(kernel, "grads", [sds((D // 2 + e, W), F32)] * 2, [place], ins,
                           scratch=[pltpu.VMEM((D, W), F32)], us=us)
        return keep, pp(give, CORE)

    def plus_tp(v, got):
        return jnp.where(jnp.arange(8)[:, None] < 6, v + got, v)

    def bwd_other(k, acc, one_low):
        return attn_bwd_other(nh, t, bucket_len, one_low, *att_saved[k], q_row, k_col, infos[k - 1], q_own, acc)

    acc, up_low, grad_b_up = ffn_bwd(True, two_low, *ffn_saved[0])
    if fast:
        keep, got = grads(grads_ffn_kernel, 2 * H, 0, [two_low, act_low, h_low, up_low], 4)
        two_low = tie(two_low, keep)
    for k in range(1, n_tp):
        (acc,) = ffn_bwd(False, two_low, *ffn_saved[k], acc, far=k == 1)
    one_low, total, vec = pcall(
        ln1_back_kernel, "ln1_back", [sds((T, D), BF), sds((R, D), F32), sds((8, D), F32)], [t],
        [two, acc, scaled_one, inverse_one, row(gain_one), vec_two, grad_b_up], us=2)
    if fast:
        tv = pp(vec, swap(0, 1))
        gx, gy, rest = stage1(False, keep, tie(got, one_low))
        one_low = tie(one_low, rest)
    g_low, total, cols = attn_bwd_own(nh, t, first, bucket_len, one_low, *att_saved[0], q_row, k_col, total)
    if fast:
        vec = plus_tp(vec, tie(tv, g_low))
        tv = pp(vec, swap(0, 2))
        fx, fy, own_f = stage2(False, rest, tie(gx, g_low), gy)
        vec = plus_tp(vec, tie(tv, own_f))
        keep, got = grads(grads_attn_kernel, 4 * hw, 8, [tokens_in, g_low, one_low, attended, cols, vec], 3)
        one_low = tie(one_low, keep)
        acc = bwd_other(1, total, one_low)
        ax, ay, rest = stage1(True, keep, tie(got, acc))
        one_low = tie(one_low, rest)
        acc = bwd_other(2, acc, one_low)
        sx2, sy2, own_a = stage2(True, rest, tie(ax, acc), ay)
        ax, ay = sx2, sy2
        acc = bwd_other(3, acc, tie(one_low, own_a))
    else:
        acc = total
        for k in range(1, n_tp):
            acc = bwd_other(k, acc, one_low)
    grad_tokens = acc

    if fast:
        h = n // 2
        f = own_f + jnp.concatenate([fy, fx])
        a = own_a[:n] + jnp.concatenate([ay[:h], ax])
        vec = own_a[n:] + ay[h:]
    else:
        def scatter(x, y):
            return lax.psum_scatter(dg(x, y, TN), "dp", scatter_dimension=0, tiled=True)

        f = jnp.concatenate([scatter(two_low, act_low), scatter(h_low, up_low)], axis=1)
        a = jnp.concatenate([scatter(tokens_in, g_low), scatter(one_low, attended)], axis=1)
        vec = lax.psum(jnp.concatenate([lax.psum(vec[:6], "tensor"), vec[6:7], jnp.pad(jnp.concatenate([cols[:, :hw], cols[:, 2 * hw:]], 1), ((0, 0), (0, D - 2 * hw)))]), "dp")
    own_qkv = jnp.swapaxes(a[:, :3 * hw].reshape(-1, 3, hw), 0, 1)
    return (layer_out, grad_tokens, own_qkv, vec[7, :2 * hw].reshape(2, hw), a[:, 3 * hw:].T, vec[0], vec[1], vec[2], f[:, H:],
            vec[6, :H], f[:, :H].T, vec[3], vec[4], vec[5])


def solution(mesh):
    n_dp, n_tp = mesh.shape["dp"], mesh.shape["tensor"]
    in_specs = (
        P("dp", None), P(None, None, "tensor"), P(None, "tensor"), P("tensor", None), P(), P(), P(),
        P(None, "tensor"), P("tensor"), P("tensor", None), P(), P(), P(), P("dp"), P("dp"),
        P("tensor", None), P("dp", None),
    )
    out_specs = (
        P(("dp", "tensor"), None), P(("dp", "tensor"), None), P(None, "dp", "tensor"), P(None, "tensor"),
        P("tensor", "dp"), P(), P(), P(), P("dp", "tensor"), P("tensor"), P("tensor", "dp"), P(), P(), P(),
    )
    return jax.shard_map(functools.partial(body, n_dp, n_tp), mesh=mesh, in_specs=in_specs, out_specs=out_specs, check_vma=False)
```

```python
import functools
import jax
import jax.numpy as jnp
from jax import lax
from jax.experimental import pallas as pl
from jax.experimental.pallas import tpu as pltpu
from jax.sharding import PartitionSpec as P

F32 = jnp.float32
BF = jnp.bfloat16
NT = (((1,), (1,)), ((), ()))
NN = (((1,), (0,)), ((), ()))
TN = (((0,), (0,)), ((), ()))
NEG = -1e30
LN_EPS = 1e-06
AXES = ("dp", "tensor")
VM = pl.BlockSpec(memory_space=pltpu.VMEM)
SM = pl.BlockSpec(memory_space=pltpu.SMEM)
ANY = pl.BlockSpec(memory_space=pl.ANY)


def dg(a, b, dn):
    return lax.dot_general(a, b, dn, preferred_element_type=F32)


def sds(shape, dtype):
    return jax.ShapeDtypeStruct(shape, dtype)


class Far:
    def __init__(self, what, part=None, sends=1, raw=False):
        self.what, self.part, self.sends, self.raw = what, part, sends, raw


class Load:
    def __init__(self, src, buf, sem):
        self.buf, self.copy = buf, pltpu.make_async_copy(src, buf, sem)
        self.copy.start()
        self.here = False

    def get(self):
        if not self.here:
            self.copy.wait()
            self.here = True
        return self.buf


class Store:
    def __init__(self, buf, dst, sems):
        self.buf, self.dst, self.sems, self.out = buf, dst, sems, []

    def send(self, rows=None):
        if rows is None:
            self.put(self.buf, self.dst)
        else:
            self.put(self.buf.at[rows], self.dst.at[rows])

    def put(self, src, dst):
        copy = pltpu.make_async_copy(src, dst, self.sems.at[len(self.out)])
        copy.start()
        self.out.append(copy)


def pcall(fn, name, out, smem, ins, scratch=(), alias=None, vmem=16, us=8, after=()):
    n, m, k, o, c = len(smem), len(ins), len(after), len(out), len(scratch)
    loads = [i for i, v in enumerate(ins) if isinstance(v, Far)]
    stores = [i for i, v in enumerate(out) if isinstance(v, Far)]

    def shape_of(v):
        x = v.what
        if v.part is None:
            return x.shape
        return tuple(p.stop - p.start for p in v.part if isinstance(p, slice)) + x.shape[len(v.part):]

    own = [pltpu.VMEM(shape_of(ins[i]), ins[i].what.dtype) for i in loads]
    bufs = [i for i in stores if not out[i].raw]
    own += [pltpu.VMEM(out[i].what.shape, out[i].what.dtype) for i in bufs]
    own += [pltpu.SemaphoreType.DMA((max(1, len(loads)),))] + [pltpu.SemaphoreType.DMA((out[i].sends,)) for i in stores]

    def run(*refs):
        args, outs = list(refs[:n + m]), list(refs[n + m + k:n + m + k + o])
        tmp, rest = refs[n + m + k + o:n + m + k + o + c], refs[n + m + k + o + c:]
        sems = rest[len(loads) + len(bufs):]
        for q, i in enumerate(loads):
            src = args[n + i] if ins[i].part is None else args[n + i].at[ins[i].part]
            args[n + i] = Load(src, rest[q], sems[0].at[q])
        for q, i in enumerate(stores):
            outs[i] = Store(None if out[i].raw else rest[len(loads) + bufs.index(i)], outs[i], sems[1 + q])
        fn(*args, *outs, *tmp)
        for i in loads:
            args[n + i].get()
        for i in stores:
            for copy in outs[i].out:
                copy.wait()

    hbm = pl.BlockSpec(memory_space=pltpu.HBM)
    return pl.pallas_call(
        run, out_shape=tuple(pltpu.HBM(v.what.shape, v.what.dtype) if isinstance(v, Far) else v for v in out),
        in_specs=[SM] * n + [hbm if isinstance(v, Far) else VM for v in ins] + [ANY] * k,
        out_specs=tuple(hbm if isinstance(v, Far) else VM for v in out),
        input_output_aliases={n + i: q for i, q in (alias or {}).items()}, scratch_shapes=list(scratch) + own,
        cost_estimate=pl.CostEstimate(flops=int(us * 8e8), bytes_accessed=int(us * 2e6), transcendentals=0),
        compiler_params=pltpu.CompilerParams(vmem_limit_bytes=vmem << 20), name=name)(
            *smem, *[pltpu.with_memory_space_constraint(v.what, pltpu.HBM) if isinstance(v, Far) else v for v in ins], *after)


def prep_a_kernel(J, perm, w, wo, b_qv, b_up, a):
    hw = b_qv.shape[1]
    n = w.shape[0]
    own = jnp.broadcast_to(J[1] < 3, w.shape)
    a[0:n, :] = jnp.where(own, w[...].astype(F32), wo[...].astype(F32))
    b = b_qv[...].astype(F32)
    a[n:n + 1, 0:hw] = b[0:1]
    a[n:n + 1, hw:2 * hw] = b[1:2]
    a[n:n + 1, 2 * hw:] = jnp.zeros((1, a.shape[1] - 2 * hw), F32)
    a[n + 1:n + 2, :] = b_up[...].astype(F32)
    bits = perm[0, 0]
    for h in range(1, perm.shape[1]):
        bits = bits + (perm[0, h] << h)
    a[n + 2:n + 8, :] = jnp.full((6, a.shape[1]), bits.astype(F32))


def prep_a(J, perm, wq, wo, b_qv, b_up):
    D = wq.shape[1]
    hw = wo.shape[0]
    return pl.pallas_call(
        prep_a_kernel, out_shape=sds((hw + 8, D), F32),
        grid_spec=pltpu.PrefetchScalarGridSpec(
            num_scalar_prefetch=2, grid=(1,),
            in_specs=[pl.BlockSpec((hw, D), lambda i, J, p: (jnp.minimum(J[1], 2), 0)),
                      pl.BlockSpec((hw, D), lambda i, J, p: (0, 0)),
                      pl.BlockSpec((2, hw), lambda i, J, p: (0, 0)),
                      pl.BlockSpec((1, D), lambda i, J, p: (0, 0))],
            out_specs=pl.BlockSpec((hw + 8, D), lambda i, J, p: (0, 0))),
        cost_estimate=pl.CostEstimate(flops=1000, bytes_accessed=1000, transcendentals=0),
        compiler_params=pltpu.CompilerParams(vmem_limit_bytes=12 << 20), name="prep_a")(
            J, perm, *[pltpu.with_memory_space_constraint(v, pltpu.HBM) for v in (wq, wo, b_qv, b_up)])


def prep_f_kernel(J, wu, wd, wuq, wdq, after, f, uq, dq):
    f[0:96, :] = wu[...].astype(F32)
    f[96:192, :] = wd[...].astype(F32)
    uq[...] = wuq[...].astype(F32)
    dq[...] = wdq[...].astype(F32)


def prep_f(J, w_up, w_down, after):
    D, H = w_up.shape
    return pl.pallas_call(
        prep_f_kernel, out_shape=(sds((192, D), F32), sds((192, H), F32), sds((192, D), F32)),
        grid_spec=pltpu.PrefetchScalarGridSpec(
            num_scalar_prefetch=1, grid=(1,),
            in_specs=[pl.BlockSpec((D // 8, H), lambda i, J: (J[0], 0)), pl.BlockSpec((H // 8, D), lambda i, J: (J[0], 0)),
                      pl.BlockSpec((D // 4, H), lambda i, J: (J[1], 0)), pl.BlockSpec((H // 4, D), lambda i, J: (J[2], 0)), ANY],
            out_specs=(pl.BlockSpec((192, D), lambda i, J: (0, 0)),) * 3),
        cost_estimate=pl.CostEstimate(flops=1000, bytes_accessed=1000, transcendentals=0),
        compiler_params=pltpu.CompilerParams(vmem_limit_bytes=16 << 20), name="prep_f")(J, w_up, w_down, w_up, w_down, after)


def cat_kernel(*refs):
    for i, v in enumerate(refs[:-1]):
        refs[-1][i] = v[...]


def cat(parts, after=()):
    return pcall(cat_kernel, "cat", [sds((len(parts),) + parts[0].shape, F32)], (), parts, us=1e-5, after=after)[0]


def attend_fwd(nh, full, first, qc, kc, qkv, att):
    hw = 64 * nh
    for h in range(nh):
        flag = first(h)
        for i in range(2):
            j = jnp.where(full, flag if i == 0 else 1 - flag, i)
            rj = pl.ds(pl.multiple_of(j * 512, 512), 512)
            q = qkv[i * 512:(i + 1) * 512, h * 64:(h + 1) * 64] * jnp.asarray(0.125, BF)
            s = dg(q, qkv[rj, hw + h * 64:hw + (h + 1) * 64], NT)
            s = jnp.where((qc[i * 512:(i + 1) * 512, :] ^ flag) == kc[j], s, NEG)
            p = jnp.exp(s - jnp.max(s, axis=1, keepdims=True))
            p = (p * (1.0 / jnp.sum(p, axis=1, keepdims=True))).astype(BF)
            att[i * 512:(i + 1) * 512, h * 64:(h + 1) * 64] = dg(p, qkv[rj, 2 * hw + h * 64:2 * hw + (h + 1) * 64], NN).astype(BF)


def project(x, w, bq, bv, qkv, hw):
    qkv[:, 0:hw] = (dg(x[...], w[0:hw, :], NT) + bq).astype(BF)
    qkv[:, hw:2 * hw] = dg(x[...], w[hw:2 * hw, :], NT).astype(BF)
    qkv[:, 2 * hw:3 * hw] = (dg(x[...], w[2 * hw:3 * hw, :], NT) + bv).astype(BF)


def attn_own_kernel(nh, perm, buck, tok, wq, wo, b_qv, qc, kc, acc, qkv, att):
    hw = 64 * nh
    b = b_qv[...].astype(F32)
    project(tok, wq.get(), b[0:1], b[1:2], qkv.buf, hw)
    qkv.send()
    attend_fwd(nh, buck[0] == 1024, lambda h: perm[0, h], qc, kc, qkv.buf, att.buf)
    att.send()
    acc[...] = dg(att.buf[...], wo.get()[...], NN)


def piece_bits(rows):
    return jnp.max(rows[2:3, 0:128]).astype(jnp.int32)


def attn_other_kernel(nh, J, buck, tok, c, o, qc, kc, acc_in, acc, qkv, w, info, att):
    hw = 64 * nh
    for half, part in enumerate((c, o)):
        piece = part
        for r in range(2):
            w.buf[pl.ds(pl.multiple_of((J[1] ^ (half * 2 + r)) * hw, 64), hw), :] = piece[r, 0:hw, :].astype(BF)
    w.send()
    rows = c[0, hw:hw + 8, :]
    info[...] = rows
    project(tok, w.buf, rows[0:1, 0:hw], rows[0:1, hw:2 * hw], qkv.buf, hw)
    qkv.send()
    bits = piece_bits(rows)
    attend_fwd(nh, buck[0] == 1024, lambda h: (bits >> h) & 1, qc, kc, qkv.buf, att)
    acc[...] = acc_in[...] + dg(att[...], w.buf[3 * hw:4 * hw, :], NN)


def attn_own(nh, perm, buck, tok, wq, wo, b_qv, qc, kc):
    T, D = tok.shape
    hw = 64 * nh
    return pcall(functools.partial(attn_own_kernel, nh), "attn_own",
                 [sds((T, D), F32), Far(sds((T, 3 * hw), BF)), Far(sds((T, hw), BF))], [perm, buck],
                 [tok, Far(wq), Far(wo), b_qv, qc, kc], us=1e-5)


def attn_other(nh, J, buck, tok, c, o, qc, kc, acc):
    T, D = tok.shape
    hw = 64 * nh
    return pcall(functools.partial(attn_other_kernel, nh), "attn_other",
                 [sds((T, D), F32), Far(sds((T, 3 * hw), BF)), Far(sds((4 * hw, D), BF)), sds((8, D), F32)],
                 [J, buck], [tok, c, o, qc, kc, acc], scratch=[pltpu.VMEM((T, hw), BF)], alias={5: 0}, us=1e-5)


def attn_bwd_kernel(nh, own, *refs):
    hw = 64 * nh
    if own:
        t, perm, buck, g, qkv, wq, wo, qcr, kcc, acc_in, dst, acc, cols, datt = refs
        wo = wo
    else:
        t, buck, g, qkv, wq, qcr, kcc, c0, q_own, acc_in, acc, dst, datt = refs
        bits = piece_bits(c0[...])
        wo = wq.at[3 * hw:4 * hw]
    datt[...] = dg(g[...], wo[...], NT).astype(BF)
    qkv, wq = qkv, wq.at[0:3 * hw]
    full = buck[0] == 1024
    R = acc.shape[0]

    def tile(h, flag, i, for_q, for_kv, ri, codes):
        rj = pl.ds(pl.multiple_of(jnp.where(full, flag ^ i, i) * 512, 512), 512)
        q = qkv[ri, h * 64:(h + 1) * 64] * jnp.asarray(0.125, BF)
        kj = qkv[rj, hw + h * 64:hw + (h + 1) * 64]
        vj = qkv[rj, 2 * hw + h * 64:2 * hw + (h + 1) * 64]
        do = datt[ri, h * 64:(h + 1) * 64]
        s = dg(kj, q, NT)
        s = jnp.where((codes ^ flag) == kcc[rj, :], s, NEG)
        p = jnp.exp(s - jnp.max(s, axis=0, keepdims=True))
        p = p * (1.0 / jnp.sum(p, axis=0, keepdims=True))
        dp = dg(vj, do, NT)
        ds = (p * (dp - jnp.sum(p * dp, axis=0, keepdims=True))).astype(BF)
        if for_kv:
            dst[rj, 2 * hw + h * 64:2 * hw + (h + 1) * 64] = dg(p.astype(BF), do, NN).astype(BF)
            dst[rj, hw + h * 64:hw + (h + 1) * 64] = dg(ds, q, NN).astype(BF)
        if for_q:
            dst[ri, h * 64:(h + 1) * 64] = (dg(ds, kj, TN) * 0.125).astype(BF)

    flags = [perm[0, h] if own else (bits >> h) & 1 for h in range(nh)]
    def whole(h, i, for_q):
        tile(h, flags[h], i, for_q, True, pl.ds(pl.multiple_of(i * 512, 512), 512), qcr[i])

    if own:
        for h in range(nh):
            for i in range(2):
                whole(h, jnp.int32(i), True)
    else:
        half = (t[0] * R) // 512

        def apart(h):
            tile(h, flags[h], half, True, False, pl.ds(pl.multiple_of(t[0] * R, R), R), q_own[...])
            whole(h, 1 - half, False)

        for h in range(nh):
            crossed = jnp.logical_and(full, flags[h] == 1)
            pl.when(jnp.logical_not(crossed))(functools.partial(whole, h, half, True))
            pl.when(crossed)(functools.partial(apart, h))
    rows = pl.ds(pl.multiple_of(t[0] * R, R), R)
    y = dg(dst[rows, :], wq[...], NN)
    acc[...] = acc_in[...] + y
    if own:
        cols[...] = jnp.sum(dst[...].astype(F32), axis=0, keepdims=True)


def attn_bwd_own(nh, t, perm, buck, g, wq, wo, qkv, qcr, kcc, acc):
    T, D = g.shape
    hw = 64 * nh
    return pcall(functools.partial(attn_bwd_kernel, nh, True), "attn_bwd_own",
                 [sds((T, 3 * hw), BF), sds(acc.shape, F32), sds((1, 3 * hw), F32)], [t, perm, buck],
                 [g, qkv, wq, wo, qcr, kcc, acc], scratch=[pltpu.VMEM((T, hw), BF)], alias={6: 1})


def attn_bwd_other(nh, t, buck, g, w, qkv, qcr, kcc, c, q_own, acc):
    T, D = g.shape
    hw = 64 * nh
    return pcall(functools.partial(attn_bwd_kernel, nh, False), "attn_bwd_other", [sds(acc.shape, F32)], [t, buck],
                 [g, qkv, w, qcr, kcc, c, q_own, acc],
                 scratch=[pltpu.VMEM((T, 3 * hw), BF), pltpu.VMEM((T, hw), BF)], alias={7: 0})[0]


ERFC_P = 0.3
ERFC = (0.16919777, 0.17054635, 0.14956615, 0.21002719, -0.08287393, 0.53022837, -0.49656831, 0.47774502, -0.1278686)


def phi_pair(v):
    e = jnp.exp(v * v * -0.5)
    t = 1.0 / (1.0 + jnp.abs(v) * (ERFC_P * 0.7071067811865476))
    a = jnp.full_like(t, ERFC[-1])
    for k in ERFC[-2::-1]:
        a = a * t + k
    tail = 0.5 * (a * t * e)
    return jnp.where(v >= 0, 1.0 - tail, tail), e * 0.3989422804014327


def ffn_rows(h, wu, wd, b, acc_in, acc, gp, act):
    n = 256
    for r in range(h.shape[0] // n):
        rows = slice(r * n, (r + 1) * n)
        up = dg(h[rows, :], wu[...], NN) + b
        big, density = phi_pair(up)
        gp.buf[rows, :] = big + up * density
        gp.send(rows)
        a = (up * big).astype(BF)
        if act is not None:
            act.buf[rows, :] = a
            act.send(rows)
        y = dg(a, wd[...], NN)
        acc[rows, :] = y if acc_in is None else acc_in[rows, :] + y


def ffn_own_kernel(h, wu, wd, b, acc, gp, act):
    ffn_rows(h, wu, wd, b[...].astype(F32), None, acc, gp, act)


def ffn_other_kernel(pair, k, J, h, a0, pa, oa, pd, od, acc_in, acc, gp, wu, wd):
    for half, (early, late) in enumerate(((pa, pd), (oa, od))):
        for r in range(2 if pair else 4):
            if pair:
                m, (u, d) = 192, ((early[0], early[1]) if r == 0 else (late[0], late[1]))
                at, ad = J[1] ^ (half * 2 + r), J[2] ^ (half * 2 + r)
            else:
                m, v = 96, early.at[r] if r < 3 else late.at[k]
                u, d = v[0:96, :], v[96:192, :]
                at = ad = J[0] ^ (half * 4 + r)
            wu.buf[pl.ds(pl.multiple_of(at * m, 32), m), :] = u.astype(BF)
            wd.buf[pl.ds(pl.multiple_of(ad * m, 32), m), :] = d.astype(BF)
    wu.send()
    wd.send()
    ffn_rows(h, wu.buf, wd.buf, a0[1:2, :], acc_in, acc, gp, None)


def ffn_own(h, wu, wd, b):
    T, D = h.shape
    H = wu.shape[1]
    return pcall(ffn_own_kernel, "ffn_own", [sds((T, D), F32), Far(sds((T, H), F32), sends=T // 256), Far(sds((T, H), BF), sends=T // 256)],
                 (), [h, wu, wd, b], us=1e-5)


def ffn_other(pair, k, J, h, a0, pieces, acc):
    T, D = h.shape
    H = D
    return pcall(functools.partial(ffn_other_kernel, pair, k), "ffn_other",
                 [sds((T, D), F32), Far(sds((T, H), F32), sends=T // 256), Far(sds((D, H), BF)), Far(sds((H, D), BF))],
                 [J], [h, a0, *pieces, acc], alias={6: 0}, us=1e-5)


def ffn_bwd_kernel(own, far, *refs):
    if own:
        g, wd, gp, wu, acc, up_low, bsum = refs
    else:
        g, wd, *gps, wu, acc_in, acc = refs
        if far:
            g, wd = g.get(), wd.get()
        else:
            gp = gps[0]
    n = 256
    bs = None
    for r in range(g.shape[0] // n):
        rows = slice(r * n, (r + 1) * n)
        da = dg(g[rows, :], wd[...], NT)
        du = (da * (gps[r].get()[...] if far else gp[rows, :])).astype(BF)
        if own:
            up_low[rows, :] = du
            s = jnp.sum(du.astype(F32), axis=0, keepdims=True)
            bs = s if bs is None else bs + s
        if far and r == 0:
            wu = wu.get()
        y = dg(du, wu[...], NT)
        acc[rows, :] = y if own else acc_in[rows, :] + y
    if own:
        bsum[...] = bs


def ffn_bwd(own, g, wu, wd, gp, acc=None, far=False):
    T, D = g.shape
    H = gp.shape[1]
    gps = [gp]
    if far:
        g, wd, wu = Far(g), Far(wd), Far(wu)
        gps = [Far(gp, (slice(r, r + 256),)) for r in range(0, T, 256)]
    out = [sds((T, D), F32)]
    if own:
        out += [sds((T, H), BF), sds((1, H), F32)]
    return pcall(functools.partial(ffn_bwd_kernel, own, far), "ffn_bwd", out, (), [g, wd, *gps, wu] + ([] if own else [acc]),
                 alias=None if own else {3 + len(gps): 0}, us=4)


def norm(s):
    center = s - jnp.mean(s, axis=-1, keepdims=True)
    inverse = lax.rsqrt(jnp.mean(center * center, axis=-1, keepdims=True) + LN_EPS)
    return center * inverse, inverse


def norm_back(w, scaled, inverse):
    return inverse * (w - jnp.mean(w, axis=-1, keepdims=True) - scaled * jnp.mean(w * scaled, axis=-1, keepdims=True))


def ln1_kernel(tok, acc, b_out, gain, shift, h_low, scaled, inverse):
    n = 128
    for r in range(tok.shape[0] // n):
        rows = slice(r * n, (r + 1) * n)
        x, inv = norm(tok[rows, :].astype(F32) + acc[rows, :] + b_out[...].astype(F32))
        scaled.buf[rows, :] = x
        scaled.send(rows)
        inverse[rows, :] = inv
        h_low[rows, :] = (x * gain[...] + shift[...]).astype(BF)


def ln2_kernel(t, scaled, gain1, shift1, acc, b_down, gain2, shift2, gy, out, two, two_low, vec):
    R = out.shape[0]

    def rows_of(rows):
        s = scaled[rows, :] * gain1[...] + shift1[...] + acc[rows, :] + b_down[...].astype(F32)
        x, inv = norm(s)
        g = gy[rows, :].astype(F32)
        return x, g, norm_back(g * gain2[...], x, inv)

    n = 128
    for r in range(gy.shape[0] // n):
        rows = slice(r * n, (r + 1) * n)
        _, _, d = rows_of(rows)
        two.buf[rows, :] = d
        two.send(rows)
        two_low[rows, :] = d.astype(BF)
    tot = [jnp.zeros((1, gy.shape[1]), F32)] * 3
    for r in range(R // n):
        rows = pl.ds(pl.multiple_of(t[0] * R + r * n, n), n)
        x, g, d = rows_of(rows)
        out[r * n:(r + 1) * n, :] = x * gain2[...] + shift2[...]
        for i, v in enumerate((d, g * x, g)):
            tot[i] = tot[i] + jnp.sum(v, axis=0, keepdims=True)
    for i in range(3):
        vec[i:i + 1, :] = tot[i]


def ln1_back_kernel(t, two, acc, scaled, inverse, gain1, vec2, bup, one_low, one_own, vec):
    R = one_own.shape[0]
    n = 128

    def rows_of(rows):
        e = two[rows, :] + acc[rows, :]
        return e, norm_back(e * gain1[...], scaled[rows, :], inverse[rows, :])

    for r in range(two.shape[0] // n):
        rows = slice(r * n, (r + 1) * n)
        one_low[rows, :] = rows_of(rows)[1].astype(BF)
    tot = [jnp.zeros((1, two.shape[1]), F32)] * 3
    for r in range(R // n):
        rows = pl.ds(pl.multiple_of(t[0] * R + r * n, n), n)
        e, d = rows_of(rows)
        one_own[r * n:(r + 1) * n, :] = d
        for i, v in enumerate((d, e * scaled[rows, :], e)):
            tot[i] = tot[i] + jnp.sum(v, axis=0, keepdims=True)
    for i in range(3):
        vec[i:i + 1, :] = tot[i]
    vec[3:6, :] = vec2[0:3, :]
    vec[6:7, :] = bup[...]
    vec[7:8, :] = jnp.zeros_like(bup)


def split_blocks(place, full, keep, give):
    n = full.shape[0] // 8

    def block(q, mine):
        return pl.ds(pl.multiple_of(((place[1] ^ q) * 2 + (place[0] ^ mine)) * n, 32), n)

    for q in range(4):
        keep[q * n:(q + 1) * n, :] = full[block(q, 0), :]
        give[q * n:(q + 1) * n, :] = full[block(q, 1), :]


def grads_ffn_kernel(place, two_low, act, h_low, up_low, keep, give, full):
    H = act.shape[1]
    full[:, 0:H] = dg(two_low[...], act[...], TN)
    full[:, H:] = dg(h_low[...], up_low[...], TN)
    split_blocks(place, full, keep, give)


def grads_attn_kernel(place, tok, dst, one_low, att, cols, vec, keep, give, full):
    W = dst.shape[1]
    full[:, 0:W] = dg(tok[...], dst[...], TN)
    full[:, W:] = dg(one_low[...], att[...], TN)
    n = full.shape[0] // 2
    split_blocks(place, full, keep, give)
    give[n:n + 8, :] = vec[...]
    give[n + 7:n + 8, 0:W // 3] = cols[:, 0:W // 3]
    give[n + 7:n + 8, W // 3:2 * W // 3] = cols[:, 2 * W // 3:]
    keep[n:n + 8, :] = give[n:n + 8, :]


def stage1_kernel(n, extra, keep, got, sx, sy, rest):
    h = n // 2

    def s(a, b):
        return keep[a:b, :] + got[a:b, :]

    sx[0:h, :] = s(3 * n, 3 * n + h)
    sx[h:n, :] = s(n, n + h)
    sy[0:h, :] = s(3 * n + h, 4 * n)
    sy[h:n, :] = s(2 * n + h, 3 * n)
    rest[0:h, :] = s(n + h, 2 * n)
    rest[h:n, :] = s(2 * n, 2 * n + h)
    rest[n:2 * n, :] = s(0, n)
    if extra:
        v = s(4 * n, 4 * n + 8)
        sx[n:n + 8, :] = v
        rest[2 * n:2 * n + 8, :] = v


def stage2_kernel(n, extra, rest, gx, gy, sx, sy, own):
    h = n // 2
    sx[0:h, :] = rest[0:h, :] + gy[0:h, :]
    sy[0:h, :] = rest[h:n, :] + gx[0:h, :]
    own[0:h, :] = rest[n:n + h, :] + gx[h:n, :]
    own[h:n, :] = rest[n + h:2 * n, :] + gy[h:n, :]
    if extra:
        v = rest[2 * n:2 * n + 8, :] + gx[n:n + 8, :]
        sy[h:h + 8, :] = v
        own[n:n + 8, :] = v


def body(n_dp, n_tp, tokens_in, w_qkv, b_qv, w_out, b_out, gain_one, shift_one, w_up, b_up,
         w_down, b_down, gain_two, shift_two, bucket_len, key_mask, block_perm, grad_output):
    T, D = tokens_in.shape
    nh = block_perm.shape[0]
    hw = w_qkv.shape[2]
    H = w_up.shape[1]
    R = T // n_tp
    d = lax.axis_index("dp").astype(jnp.int32)
    t = lax.axis_index("tensor").astype(jnp.int32)[None]
    core, yx = d & 1, (d >> 1) & 3
    J = jnp.stack([core * 4 + yx, core * 2 + (yx & 1), core * 2 + (yx >> 1)])
    place = jnp.stack([core, yx])

    def swap(b, z):
        return [(i * n_tp + k, (i ^ b) * n_tp + (k ^ z)) for i in range(n_dp) for k in range(n_tp)]

    CORE, X, Y = swap(1, 0), swap(2, 0), swap(4, 0)

    def pp(v, perm):
        return lax.ppermute(v, AXES, perm)

    def row(v):
        return v.reshape(1, -1)

    def tie(v, *first):
        return lax.optimization_barrier((v, first))[0]

    pos = jnp.arange(T, dtype=jnp.int32)
    code = pos >> (lax.population_count(bucket_len[0] - 1) - 1)
    kcode = jnp.where(key_mask == 1, code, -1)
    q_col, q_row = code[:, None], code.reshape(2, 1, T // 2)
    k_col, k_row = kcode[:, None], kcode.reshape(2, 1, T // 2)
    q_own = lax.dynamic_slice_in_dim(code, t[0] * R, R)[None]

    def sync(*v):
        return lax.optimization_barrier(v)

    NEXT = [(i * n_tp + k, i * n_tp + (k + 1) % n_tp) for i in range(n_dp) for k in range(n_tp)]
    PREV = [(i * n_tp + (k + 1) % n_tp, i * n_tp + k) for i in range(n_dp) for k in range(n_tp)]

    def attn(pieces, acc):
        acc, qkv, w, info = attn_other(nh, J, bucket_len, tokens_in, *pieces, q_col, k_row, acc)
        att_saved.append((w, qkv))
        infos.append(info)
        return acc

    def ffn(a0, pieces, acc, k=0, pair=False):
        acc, gp, wu, wd = ffn_other(pair, k, J, h_low, a0, pieces, acc)
        ffn_saved.append((wu, wd, gp))
        return acc

    wq = jnp.swapaxes(w_qkv, 1, 2).reshape(3 * hw, D)
    first = block_perm.T
    a_piece = prep_a(J, first, wq, w_out, b_qv, row(b_up))
    z1 = pp(a_piece, NEXT)
    acc, qkv, attended = attn_own(nh, first, bucket_len, tokens_in, wq, w_out, b_qv, q_col, k_row)
    att_saved, infos = [(wq, w_out, qkv)], []

    z1, acc = sync(z1, acc)
    z2, x1 = pp(z1, NEXT), pp(z1, X)
    f_piece, u_quarter, d_quarter = prep_f(J, w_up, w_down, z1)

    z2, x1, f_piece, u_quarter, d_quarter, k_col = sync(z2, x1, f_piece, u_quarter, d_quarter, k_col)
    z3, x2 = pp(a_piece, PREV), pp(z2, X)
    m1 = cat((z1, x1))
    acc = attn((m1, pp(m1, CORE)), acc)

    z3, x2, acc = sync(z3, x2, acc)
    x3, f1 = pp(z3, X), pp(f_piece, NEXT)
    m2 = cat((z2, x2))
    acc = attn((m2, pp(m2, CORE)), acc)

    x3, f1, acc = sync(x3, f1, acc)
    fx1, fy1, f2 = pp(f1, X), pp(f1, Y), pp(f1, NEXT)
    m3 = cat((z3, x3))
    acc = attn((m3, pp(m3, CORE)), acc)

    fx1, fy1, f2, acc = sync(fx1, fy1, f2, acc)
    fx2, fy2, zu = pp(f2, X), pp(f2, Y), pp(u_quarter, PREV)
    h_low, scaled_one, inverse_one = pcall(
        ln1_kernel, "ln1", [sds((T, D), BF), Far(sds((T, D), F32), sends=T // 128), sds((T, 1), F32)], (),
        [tokens_in, acc, row(b_out), row(gain_one), row(shift_one)], us=1e-5)
    acc, gp, act_low = ffn_own(h_low, w_up, w_down, row(b_up))
    ffn_saved = [(w_up, w_down, gp)]

    fx2, fy2, zu, acc = sync(fx2, fy2, zu, acc)
    fd1, fd2, zd = pp(fy1, X), pp(fx2, Y), pp(d_quarter, PREV)
    g1 = cat((f1, fx1, fy1))
    k1 = pp(g1, CORE)
    g2 = cat((f2, fx2, fy2))
    k2 = pp(g2, CORE)

    fd1, fd2, zd = sync(fd1, fd2, zd)
    gd = cat((fd1, fd2))
    kd = pp(gd, CORE)
    xu, yd = pp(zu, X), pp(zd, Y)
    gz = cat((zu, zd))
    kz = pp(gz, CORE)
    acc = ffn(infos[0], (g1, k1, gd, kd), acc)
    acc = ffn(infos[1], (g2, k2, gd, kd), tie(acc, kz), k=1)

    xu, yd, acc = sync(xu, yd, acc)
    gx = cat((xu, yd))
    acc = ffn(infos[2], (gz, kz, gx, pp(gx, CORE)), acc, pair=True)
    layer_out, two, two_low, vec_two = pcall(
        ln2_kernel, "ln2", [sds((R, D), F32), Far(sds((T, D), F32), sends=T // 128), sds((T, D), BF), sds((3, D), F32)], [t],
        [scaled_one, row(gain_one), row(shift_one), acc, row(b_down), row(gain_two), row(shift_two), grad_output], us=4)

    fast = n_dp == 8 and n_tp == 4
    n = D // 8

    def stage1(extra, keep, got):
        e = 8 if extra else 0
        W = keep.shape[1]
        sx, sy, rest = pcall(functools.partial(stage1_kernel, n, extra), "stage1",
                             [sds((n + e, W), F32), sds((n, W), F32), sds((2 * n + e, W), F32)], (), [keep, got], us=1)
        return pp(sx, X), pp(sy, Y), rest

    def stage2(extra, rest, gx, gy):
        e = 8 if extra else 0
        W = rest.shape[1]
        sx, sy, own = pcall(functools.partial(stage2_kernel, n, extra), "stage2",
                            [sds((n // 2, W), F32), sds((n // 2 + e, W), F32), sds((n + e, W), F32)], (), [rest, gx, gy], us=1)
        return pp(sx, X), pp(sy, Y), own

    def grads(kernel, W, e, ins, us):
        keep, give = pcall(kernel, "grads", [sds((D // 2 + e, W), F32)] * 2, [place], ins,
                           scratch=[pltpu.VMEM((D, W), F32)], us=us)
        return keep, pp(give, CORE)

    def plus_tp(v, got):
        return jnp.where(jnp.arange(8)[:, None] < 6, v + got, v)

    def bwd_other(k, acc, one_low):
        return attn_bwd_other(nh, t, bucket_len, one_low, *att_saved[k], q_row, k_col, infos[k - 1], q_own, acc)

    acc, up_low, grad_b_up = ffn_bwd(True, two_low, *ffn_saved[0])
    if fast:
        keep, got = grads(grads_ffn_kernel, 2 * H, 0, [two_low, act_low, h_low, up_low], 4)
        two_low = tie(two_low, keep)
    for k in range(1, n_tp):
        (acc,) = ffn_bwd(False, two_low, *ffn_saved[k], acc, far=k == 1)
    one_low, total, vec = pcall(
        ln1_back_kernel, "ln1_back", [sds((T, D), BF), sds((R, D), F32), sds((8, D), F32)], [t],
        [two, acc, scaled_one, inverse_one, row(gain_one), vec_two, grad_b_up], us=2)
    if fast:
        tv = pp(vec, swap(0, 1))
        gx, gy, rest = stage1(False, keep, tie(got, one_low))
        one_low = tie(one_low, rest)
    g_low, total, cols = attn_bwd_own(nh, t, first, bucket_len, one_low, *att_saved[0], q_row, k_col, total)
    if fast:
        vec = plus_tp(vec, tie(tv, g_low))
        tv = pp(vec, swap(0, 2))
        fx, fy, own_f = stage2(False, rest, tie(gx, g_low), gy)
        vec = plus_tp(vec, tie(tv, own_f))
        keep, got = grads(grads_attn_kernel, 4 * hw, 8, [tokens_in, g_low, one_low, attended, cols, vec], 3)
        one_low = tie(one_low, keep)
        acc = bwd_other(1, total, one_low)
        ax, ay, rest = stage1(True, keep, tie(got, acc))
        one_low = tie(one_low, rest)
        acc = bwd_other(2, acc, one_low)
        sx2, sy2, own_a = stage2(True, rest, tie(ax, acc), ay)
        ax, ay = sx2, sy2
        acc = bwd_other(3, acc, tie(one_low, own_a))
    else:
        acc = total
        for k in range(1, n_tp):
            acc = bwd_other(k, acc, one_low)
    grad_tokens = acc

    if fast:
        h = n // 2
        f = own_f + jnp.concatenate([fy, fx])
        a = own_a[:n] + jnp.concatenate([ay[:h], ax])
        vec = own_a[n:] + ay[h:]
    else:
        def scatter(x, y):
            return lax.psum_scatter(dg(x, y, TN), "dp", scatter_dimension=0, tiled=True)

        f = jnp.concatenate([scatter(two_low, act_low), scatter(h_low, up_low)], axis=1)
        a = jnp.concatenate([scatter(tokens_in, g_low), scatter(one_low, attended)], axis=1)
        vec = lax.psum(jnp.concatenate([lax.psum(vec[:6], "tensor"), vec[6:7], jnp.pad(jnp.concatenate([cols[:, :hw], cols[:, 2 * hw:]], 1), ((0, 0), (0, D - 2 * hw)))]), "dp")
    own_qkv = jnp.swapaxes(a[:, :3 * hw].reshape(-1, 3, hw), 0, 1)
    return (layer_out, grad_tokens, own_qkv, vec[7, :2 * hw].reshape(2, hw), a[:, 3 * hw:].T, vec[0], vec[1], vec[2], f[:, H:],
            vec[6, :H], f[:, :H].T, vec[3], vec[4], vec[5])


def solution(mesh):
    n_dp, n_tp = mesh.shape["dp"], mesh.shape["tensor"]
    in_specs = (
        P("dp", None), P(None, None, "tensor"), P(None, "tensor"), P("tensor", None), P(), P(), P(),
        P(None, "tensor"), P("tensor"), P("tensor", None), P(), P(), P(), P("dp"), P("dp"),
        P("tensor", None), P("dp", None),
    )
    out_specs = (
        P(("dp", "tensor"), None), P(("dp", "tensor"), None), P(None, "dp", "tensor"), P(None, "tensor"),
        P("tensor", "dp"), P(), P(), P(), P("dp", "tensor"), P("tensor"), P("tensor", "dp"), P(), P(), P(),
    )
    return jax.shard_map(functools.partial(body, n_dp, n_tp), mesh=mesh, in_specs=in_specs, out_specs=out_specs, check_vma=False)
```
